256 devices in a mesh: section: 8 (over z), tm: 32 (over x, y, core).
Axes of the slice: x: 4, y: 4, z: 8, core: 2. Of those that a mesh axis runs over, the one named last changes fastest.
Arguments:
- acts: bfloat16 [8, 2, 2048, 1024], P('section', None, 'tm'), may hold values from -600 to 600
- grad_top: bfloat16 [2, 2048, 1024], P(None, 'tm'), may hold values from -6 to 6
- w_in: bfloat16 [8, 1024, 3072], P('section'), may hold values from -0.1875 to 0.1875
- w_out: bfloat16 [8, 1024, 1024], P('section'), may hold values from -0.1875 to 0.1875
- offsets: int32 [32, 5], P('tm'), may hold values from 0 to 16, as said below
Outputs:
- d_acts: bfloat16 [8, 2, 2048, 1024], P('section', None, 'tm')
- d_w_in: float32 [8, 1024, 3072], P('section', 'tm')
- d_w_out: float32 [8, 1024, 1024], P('section', 'tm')
The draws below stay inside these ranges and needn't reach their ends.
Inputs may be any that keep to these rules, and one draw needn't show every extreme that they name: offsets[t, k] is 0 or 2**k, and 0 wherever t < 2**k; the last shard uses every level.
All inputs are finite; a program needn't handle non-finite values.
Results may differ from the reference program's by a relative error of at most 0.018.
The reference program's roundings to bfloat16 on the way count: a program that leaves them out, or rounds other values in their place, can miss the bound.
Values may be sent and summed in bfloat16 or wider, within the bound.
A program may use at most 128 MiB of HBM per device.

```python
import math
import jax
import jax.numpy as jnp
from jax import lax

D = 1024
HEAD_DIM = 64
TOK_DEV = 64
MB = 2
LAYERS = 8
SHARDS = 32
LEVELS = 5
SEQ = 2048


def draw_acts(key, part):
    shape = (LAYERS, MB, SEQ, D)
    first, second, third = jax.random.split(jax.random.fold_in(key, 11), 3)
    column_scale = jnp.exp(jax.random.uniform(second, (LAYERS, 1, 1, D), minval=0.0, maxval=math.log(10.0)))
    row_scale = jnp.exp(jax.random.uniform(third, (LAYERS, MB, SEQ, 1), minval=0.0, maxval=math.log(10.0)))
    values = jnp.clip(jax.random.normal(first, shape), -6.0, 6.0) * column_scale * row_scale
    return values.astype(jnp.bfloat16)


def draw_w_in(key, part):
    shape = (LAYERS, D, 3 * D)
    first = jax.random.fold_in(jax.random.fold_in(key, 23), 0)
    values = jnp.clip(jax.random.normal(first, shape), -6.0, 6.0) * D ** (-0.5)
    return values.astype(jnp.bfloat16)


def draw_offsets(key, part):
    chosen = jax.random.randint(jax.random.fold_in(key, 31), (SHARDS, LEVELS), 0, 4) < 3
    shard_row = jnp.arange(SHARDS, dtype=jnp.int32)[:, None]
    powers = (2 ** jnp.arange(LEVELS, dtype=jnp.int32))[None, :]
    chosen = chosen | (shard_row == SHARDS - 1)
    return jnp.where(chosen & (shard_row >= powers), powers, 0).astype(jnp.int32)


def levels(key, dims, cuts, smallest, top_value):
    def one(axis_at, parts):
        heights = jax.random.uniform(jax.random.fold_in(jax.random.fold_in(key, 6), axis_at), (parts,), jnp.float32, smallest / len(cuts), top_value / len(cuts))
        return jnp.repeat(jnp.exp(heights), dims[axis_at] // parts).reshape((-1,) + (1,) * (len(dims) - axis_at - 1))

    factor_of = one(*cuts[0])
    for cut in cuts[1:]:
        factor_of = factor_of * one(*cut)
    return factor_of


def gaussian(own_key, shape, width, reach, cuts=(), kind=jnp.bfloat16):
    result = jax.random.normal(own_key, shape, jnp.float32) * width
    if len(cuts) > 0:
        result = levels(own_key, shape, cuts, -0.22, 0.18) * result
    return jnp.clip(result, min=-reach, max=reach).astype(kind)


def setup_inputs(seed: int = 0) -> dict:
    arg_keys = jax.random.split(jax.random.key(seed), 6)
    return {
        "acts": draw_acts(jax.random.fold_in(arg_keys[5], 71), 0),
        "grad_top": gaussian(arg_keys[1], (MB, SEQ, D), 1.0, 6.0, ((1, 32),)),
        "w_in": draw_w_in(jax.random.fold_in(arg_keys[5], 71), 0),
        "w_out": gaussian(arg_keys[3], (LAYERS, D, D), D ** -0.5, 0.1875, ((0, 8),)),
        "offsets": draw_offsets(jax.random.fold_in(arg_keys[5], 71), 0),
    }


epsilon = 1e-06
negative_fill = -1e+30

def to_bf16(values):
    return lax.optimization_barrier(values.astype(jnp.bfloat16))

def normalize(inputs):
    values = inputs.astype(jnp.float32)
    inverse_rms = lax.rsqrt(lax.optimization_barrier(jnp.mean(values * values, axis=-1, keepdims=True)) + epsilon)
    return (values * inverse_rms, inverse_rms)

def shift_shards(stacked, offset):
    padding = jnp.zeros((abs(offset),) + stacked.shape[1:], stacked.dtype)
    if offset > 0:
        return jnp.concatenate([padding, stacked[:-offset]], 0)
    return jnp.concatenate([stacked[-offset:], padding], 0)

def key_bias(level_flags, shard_rows):
    position = jnp.arange(shard_rows)
    own_part = position[None, :] <= position[:, None]
    far_part = jnp.repeat(level_flags != 0, shard_rows)
    far_part = jnp.broadcast_to(far_part[None, :], (shard_rows, far_part.shape[0]))
    return jnp.concatenate([own_part, far_part], 1)

def softmax_keys(queries, key_heads, allowed):
    scores = jnp.einsum('ihd,jhd->hij', queries.astype(jnp.float32), key_heads.astype(jnp.float32)) * HEAD_DIM ** (-0.5)
    scores = jnp.where(allowed[None], scores, negative_fill)
    highest = lax.optimization_barrier(jnp.max(scores, axis=-1, keepdims=True))
    shifted_exp = jnp.where(allowed[None], jnp.exp(scores - highest), 0.0)
    return shifted_exp / lax.optimization_barrier(jnp.sum(shifted_exp, axis=-1, keepdims=True))

def attend_back(query_rows, key_rows, allowed, incoming, w_proj):
    shard_rows, model_width = query_rows.shape
    head_count = model_width // HEAD_DIM
    queries = query_rows.reshape(shard_rows, head_count, HEAD_DIM).astype(jnp.float32)
    key_heads = key_rows[:, :model_width].reshape(-1, head_count, HEAD_DIM).astype(jnp.float32)
    value_heads = key_rows[:, model_width:].reshape(-1, head_count, HEAD_DIM).astype(jnp.float32)
    probability = softmax_keys(queries, key_heads, allowed)
    rounded = to_bf16(probability).astype(jnp.float32)
    attended = jnp.einsum('hij,jhd->ihd', rounded, value_heads).reshape(shard_rows, model_width).astype(jnp.bfloat16)
    upstream = to_bf16(jnp.dot(incoming, w_proj.T, preferred_element_type=jnp.float32))
    up_heads = upstream.astype(jnp.float32).reshape(shard_rows, head_count, HEAD_DIM)
    att_heads = attended.astype(jnp.float32).reshape(shard_rows, head_count, HEAD_DIM)
    delta = jnp.einsum('ihd,ihd->hi', up_heads, att_heads)[..., None]
    prob_grad = jnp.einsum('ihd,jhd->hij', up_heads, value_heads)
    score_grad = to_bf16(probability * (prob_grad - delta)).astype(jnp.float32)
    scale_factor = HEAD_DIM ** (-0.5)
    query_grad = jnp.einsum('hij,jhd->ihd', score_grad, key_heads) * scale_factor
    key_grad = jnp.einsum('hij,ihd->jhd', score_grad, queries) * scale_factor
    value_grad = jnp.einsum('hij,ihd->jhd', rounded, up_heads)
    return (attended, query_grad.reshape(shard_rows, model_width), key_grad.reshape(-1, model_width), value_grad.reshape(-1, model_width))

def reference(acts, grad_top, w_in, w_out, offsets):
    model_width = acts.shape[-1]
    shard_rows = TOK_DEV
    shards = SHARDS
    grads_acts = [None] * LAYERS
    grads_in = [None] * LAYERS
    grads_out = [None] * LAYERS
    incoming = grad_top
    for layer in reversed(range(LAYERS)):
        w_qkv = w_in[layer]
        w_proj = w_out[layer]
        outgoing = []
        saved = []
        for micro in range(MB):
            normed, inverse_rms = normalize(acts[layer, micro])
            rounded_norm = normed.astype(jnp.bfloat16)
            qkv = jnp.dot(rounded_norm, w_qkv, preferred_element_type=jnp.float32).astype(jnp.bfloat16)
            shard_qkv = qkv.reshape(shards, shard_rows, 3 * model_width)
            queries = shard_qkv[..., :model_width]
            pairs = shard_qkv[..., model_width:]
            far_pairs = jnp.stack([shift_shards(pairs, 2 ** level) for level in range(LEVELS)], 1)
            gradient = incoming[micro].reshape(shards, shard_rows, model_width)

            def shard_pass(piece):
                query_rows, own_rows, far_rows, level_flags, grad_rows = piece
                key_rows = jnp.concatenate([own_rows, far_rows.reshape(-1, own_rows.shape[-1])], 0)
                return attend_back(query_rows, key_rows, key_bias(level_flags, shard_rows), grad_rows, w_proj)
            attended, query_grad, key_grad, value_grad = lax.map(shard_pass, (queries, pairs, far_pairs, offsets, gradient))
            owner_sum = jnp.concatenate([key_grad[:, :shard_rows], value_grad[:, :shard_rows]], -1)
            far_grad = jnp.concatenate([key_grad[:, shard_rows:], value_grad[:, shard_rows:]], -1)
            far_grad = far_grad.reshape(shards, LEVELS, shard_rows, 2 * model_width)
            for level in range(LEVELS):
                owner_sum = owner_sum + shift_shards(to_bf16(far_grad[:, level]).astype(jnp.float32), -2 ** level)
            qkv_grad = jnp.concatenate([query_grad, owner_sum], -1).astype(jnp.bfloat16).reshape(-1, 3 * model_width)
            norm_grad = jnp.dot(qkv_grad, w_qkv.T, preferred_element_type=jnp.float32)
            inner = lax.optimization_barrier(jnp.mean(norm_grad * normed, axis=-1, keepdims=True))
            grad_in = (incoming[micro].astype(jnp.float32) + inverse_rms * (norm_grad - normed * inner)).astype(jnp.bfloat16)
            outgoing.append(grad_in)
            saved.append((rounded_norm, qkv_grad, attended.reshape(-1, model_width), incoming[micro]))
        stacked = []
        for position in range(4):
            joined = jnp.stack([item[position] for item in saved], 0)
            joined = joined.reshape(MB, shards, shard_rows, joined.shape[-1])
            stacked.append(jnp.swapaxes(joined, 0, 1))

        def add_shard(carry, piece):
            normed_rows, qkv_rows, attended_rows, grad_rows = [item.reshape(-1, item.shape[-1]) for item in piece]
            first = jnp.dot(normed_rows.T, qkv_rows, preferred_element_type=jnp.float32)
            second = jnp.dot(attended_rows.T, grad_rows, preferred_element_type=jnp.float32)
            term = to_bf16(jnp.concatenate([first, second], 1)).astype(jnp.float32)
            return (carry + term, None)
        summed, _ = lax.scan(add_shard, jnp.zeros((model_width, 4 * model_width), jnp.float32), tuple(stacked))
        grads_in[layer] = summed[:, :3 * model_width]
        grads_out[layer] = summed[:, 3 * model_width:]
        incoming = jnp.stack(outgoing, 0)
        grads_acts[layer] = incoming
    return (jnp.stack(grads_acts, 0), jnp.stack(grads_in, 0), jnp.stack(grads_out, 0))
```

```python
import jax
import jax.numpy as jnp
from jax import lax
from jax.experimental import pallas as pl
from jax.experimental.pallas import tpu as pltpu
from jax.sharding import PartitionSpec as P

HEAD_DIM = 64
SCALE = HEAD_DIM ** (-0.5)
EPSILON = 1e-06
FILL = -1e30
MESH = pl.DeviceIdType.MESH

MB = 2
ROWS = 64
WIDTH = 1024
LEVELS = 5
BLOCKS = LEVELS + 1
KEYS = BLOCKS * ROWS
GROUP = 256
GROUPS = WIDTH // GROUP
CHUNK = 256
CHUNKS = WIDTH // CHUNK
PER = GROUP // HEAD_DIM

BF16 = jnp.bfloat16
F32 = jnp.float32


def dot(a, b):
    return lax.dot_general(a, b, (((1,), (0,)), ((), ())), preferred_element_type=F32)


def dot_nt(a, b):
    return lax.dot_general(a, b, (((1,), (1,)), ((), ())), preferred_element_type=F32)


def dot_tn(a, b):
    return lax.dot_general(a, b, (((0,), (0,)), ((), ())), preferred_element_type=F32)


def layer_kernel(
    sections,
    shards,
    acts_ref,
    gtop_ref,
    w_in_hbm,
    w_out_hbm,
    off_ref,
    dacts_ref,
    wg_ref,
    w_in,
    w_out,
    nall,
    normed,
    inv,
    qm,
    kv,
    p32,
    p16,
    bm,
    bias,
    inc,
    dq,
    part,
    att,
    ng,
    gsend,
    sbuf,
    rbuf,
    w_sem,
    fs,
    fr,
    bs,
    br,
    zs,
    zr,
):
    z = lax.axis_index("section")
    t = lax.axis_index("tm")
    steps = [2**level for level in range(LEVELS)]

    def up_shard(k):
        return lax.rem(t + steps[k], shards)

    def down_shard(k):
        return lax.rem(t + shards - steps[k], shards)

    copy_in = pltpu.make_async_copy(w_in_hbm, w_in, w_sem.at[0])
    copy_out = pltpu.make_async_copy(w_out_hbm, w_out, w_sem.at[1])
    copy_in.start()
    copy_out.start()

    barrier = pltpu.get_barrier_semaphore()
    for k in range(LEVELS):
        pl.semaphore_signal(barrier, inc=1, device_id=(z, up_shard(k)), device_id_type=MESH)
        if 2 * steps[k] != shards:
            pl.semaphore_signal(barrier, inc=1, device_id=(z, down_shard(k)), device_id_type=MESH)
    for step in (1, sections - 1):
        pl.semaphore_signal(
            barrier, inc=1, device_id=(lax.rem(z + step, sections), t), device_id_type=MESH
        )

    def fwd_copy(m, k):
        return pltpu.make_async_remote_copy(
            src_ref=nall.at[m, 0],
            dst_ref=nall.at[m, k + 1],
            send_sem=fs.at[m, k],
            recv_sem=fr.at[m, k],
            device_id=(z, up_shard(k)),
            device_id_type=MESH,
        )

    def bwd_copy(m, c, k):
        return pltpu.make_async_remote_copy(
            src_ref=sbuf.at[m, c, k],
            dst_ref=rbuf.at[m, c, k],
            send_sem=bs.at[m, c, k],
            recv_sem=br.at[m, c, k],
            device_id=(z, down_shard(k)),
            device_id_type=MESH,
        )

    def z_copy(m):
        return pltpu.make_async_remote_copy(
            src_ref=gsend.at[m],
            dst_ref=inc.at[m],
            send_sem=zs.at[m],
            recv_sem=zr.at[m],
            device_id=(lax.rem(z + sections - 1, sections), t),
            device_id_type=MESH,
        )

    for m in range(MB):
        x = acts_ref[m].astype(F32)
        inverse = lax.rsqrt(jnp.mean(x * x, axis=-1, keepdims=True) + EPSILON)
        value = x * inverse
        normed[m] = value
        inv[m] = jnp.broadcast_to(inverse, (ROWS, 128))
        nall[m, 0] = value.astype(BF16)
        for k in range(LEVELS):

            @pl.when(t < steps[k])
            def _():
                nall[m, k + 1] = jnp.zeros((ROWS, WIDTH), BF16)

    pl.semaphore_wait(barrier, 2 * LEVELS + 1)

    for m in range(MB):
        for k in reversed(range(LEVELS)):

            @pl.when(t + steps[k] < shards)
            def _():
                fwd_copy(m, k).start()

    row_head = lax.broadcasted_iota(jnp.int32, (GROUP, GROUP), 0) // HEAD_DIM
    lane_head = lax.broadcasted_iota(jnp.int32, (GROUP, GROUP), 1) // HEAD_DIM
    bm[...] = jnp.where(row_head == lane_head, 1.0, 0.0).astype(BF16)
    key_pos = lax.broadcasted_iota(jnp.int32, (ROWS, GROUP), 0)
    query_pos = lax.broadcasted_iota(jnp.int32, (ROWS, GROUP), 1) % ROWS
    bias[0:ROWS, :] = jnp.where(key_pos <= query_pos, 0.0, FILL)
    for k in range(LEVELS):
        fill = jnp.where(off_ref[0, k] != 0, 0.0, FILL)
        bias[(k + 1) * ROWS : (k + 2) * ROWS, :] = jnp.full((ROWS, GROUP), fill, F32)

    @pl.when(z == sections - 1)
    def _():
        inc[...] = gtop_ref[...]

    def spread(rows):
        return jnp.concatenate([rows] * PER, 0) * bm[...]

    def gather_heads(stacked):
        lanes = lax.broadcasted_iota(jnp.int32, (ROWS, GROUP), 1) // HEAD_DIM
        total = jnp.where(lanes == 0, stacked[0:ROWS], 0.0)
        for head in range(1, PER):
            total = jnp.where(lanes == head, stacked[head * ROWS : (head + 1) * ROWS], total)
        return total

    copy_in.wait()
    copy_out.wait()

    def own_query(c, carry):
        cols = pl.ds(pl.multiple_of(c * GROUP, GROUP), GROUP)
        both = jnp.concatenate([nall[0, 0], nall[1, 0]], 0)
        result = dot(both, w_in[:, cols]).astype(BF16)
        for m in range(MB):
            qm[m, c] = spread(result[m * ROWS : (m + 1) * ROWS])
        return carry

    lax.fori_loop(0, GROUPS, own_query, 0)

    def own_pair(c, carry):
        cols = pl.ds(pl.multiple_of(c * GROUP, GROUP), GROUP)
        source = pl.ds(pl.multiple_of(WIDTH + c * GROUP, GROUP), GROUP)
        both = jnp.concatenate([nall[0, 0], nall[1, 0]], 0)
        result = dot(both, w_in[:, source]).astype(BF16)
        for m in range(MB):
            kv[m, 0:ROWS, cols] = result[m * ROWS : (m + 1) * ROWS]
        return carry

    lax.fori_loop(0, 2 * GROUPS, own_pair, 0)

    def forward(m):
        for k in range(LEVELS):

            @pl.when(t >= steps[k])
            def _():
                fwd_copy(m, k).wait_recv()

        def far_pair(c, carry):
            cols = pl.ds(pl.multiple_of(c * GROUP, GROUP), GROUP)
            source = pl.ds(pl.multiple_of(WIDTH + c * GROUP, GROUP), GROUP)
            rows = nall[m, 1:BLOCKS].reshape(LEVELS * ROWS, WIDTH)
            kv[m, ROWS:KEYS, cols] = dot(rows, w_in[:, source]).astype(BF16)
            return carry

        lax.fori_loop(0, 2 * GROUPS, far_pair, 0)

        def probability(g, carry):
            cols = pl.ds(pl.multiple_of(g * GROUP, GROUP), GROUP)
            scores = dot_nt(kv[m, :, cols], qm[m, g]) * SCALE + bias[...]
            highest = jnp.max(scores, axis=0, keepdims=True)
            weights = jnp.exp(scores - highest)
            result = weights / jnp.sum(weights, axis=0, keepdims=True)
            p32[m, g] = result
            p16[m, g] = result.astype(BF16)
            return carry

        lax.fori_loop(0, GROUPS, probability, 0)

    def attend(m):
        def group(g, carry):
            cols = pl.ds(pl.multiple_of(g * GROUP, GROUP), GROUP)
            values = pl.ds(pl.multiple_of(WIDTH + g * GROUP, GROUP), GROUP)
            stacked = dot_tn(p16[m, g], kv[m, :, values])
            att[m * ROWS : (m + 1) * ROWS, cols] = gather_heads(stacked).astype(BF16)
            return carry

        lax.fori_loop(0, GROUPS, group, 0)

    def backward_send(m):
        @pl.when(z < sections - 1)
        def _():
            z_copy(m).wait_recv()

        def group(g, carry):
            cols = pl.ds(pl.multiple_of(g * GROUP, GROUP), GROUP)
            values = pl.ds(pl.multiple_of(WIDTH + g * GROUP, GROUP), GROUP)
            upstream = dot_nt(inc[m], w_out[cols, :]).astype(BF16)
            up_heads = spread(upstream)
            prob_grad = dot_nt(kv[m, :, values], up_heads)
            prob = p32[m, g]
            delta = jnp.sum(prob * prob_grad, axis=0, keepdims=True)
            score_grad = (prob * (prob_grad - delta)).astype(BF16)
            part[m, :, cols] = (dot(score_grad, qm[m, g]) * SCALE).astype(BF16)
            part[m, :, values] = dot(p16[m, g], up_heads).astype(BF16)
            stacked = dot_tn(score_grad, kv[m, :, cols])
            dq[m * ROWS : (m + 1) * ROWS, cols] = (gather_heads(stacked) * SCALE).astype(BF16)
            return carry

        lax.fori_loop(0, GROUPS, group, 0)

        def project(c, carry):
            cols = pl.ds(pl.multiple_of(c * CHUNK, CHUNK), CHUNK)
            result = dot_nt(part[m], w_in[cols, WIDTH : 3 * WIDTH])
            ng[m, :, cols] = result[0:ROWS]
            for k in reversed(range(LEVELS)):
                sbuf[m, c, k] = result[(k + 1) * ROWS : (k + 2) * ROWS].astype(BF16)

                @pl.when(t >= steps[k])
                def _():
                    bwd_copy(m, c, k).start()

            return carry

        lax.fori_loop(0, CHUNKS, project, 0)

        def own(c, carry):
            cols = pl.ds(pl.multiple_of(c * CHUNK, CHUNK), CHUNK)
            ng[m, :, cols] += dot_nt(dq[m * ROWS : (m + 1) * ROWS, :], w_in[cols, 0:WIDTH])
            return carry

        lax.fori_loop(0, CHUNKS, own, 0)

    def backward_finish(m):
        for c in range(CHUNKS):
            for k in range(LEVELS):

                @pl.when(t + steps[k] < shards)
                def _():
                    bwd_copy(m, c, k).wait_recv()
                    cols = slice(c * CHUNK, (c + 1) * CHUNK)
                    ng[m, :, cols] += rbuf[m, c, k].astype(F32)

        grad = ng[m]
        value = normed[m]
        inner = jnp.mean(grad * value, axis=-1, keepdims=True)
        result = (inc[m].astype(F32) + inv[m, :, 0:1] * (grad - value * inner)).astype(BF16)
        dacts_ref[m] = result
        gsend[m] = result

        @pl.when(z > 0)
        def _():
            z_copy(m).start()

    forward(0)
    backward_send(0)
    forward(1)
    attend(0)
    attend(1)
    backward_finish(0)
    backward_send(1)

    own_rows = jnp.concatenate([nall[0, 0], nall[1, 0]], 0)
    att_rows = att[...]
    inc_rows = inc[...].reshape(MB * ROWS, WIDTH)

    def weight(r, carry):
        rows = pl.ds(pl.multiple_of(r * CHUNK, CHUNK), CHUNK)
        far = nall[:, :, :, rows].reshape(MB * KEYS, CHUNK)
        own = jnp.concatenate([nall[0, 0, :, rows], nall[1, 0, :, rows]], 0)
        wg_ref[rows, 0:WIDTH] = dot_tn(own, dq[...]).astype(BF16)
        wg_ref[rows, WIDTH : 3 * WIDTH] = dot_tn(
            far, part[...].reshape(MB * KEYS, 2 * WIDTH)
        ).astype(BF16)
        wg_ref[rows, 3 * WIDTH : 4 * WIDTH] = dot_tn(
            att[:, rows], inc[...].reshape(MB * ROWS, WIDTH)
        ).astype(BF16)
        return carry

    lax.fori_loop(0, CHUNKS, weight, 0)
    backward_finish(1)

    for m in range(MB):
        for k in range(LEVELS):

            @pl.when(t + steps[k] < shards)
            def _():
                fwd_copy(m, k).wait_send()

            @pl.when(t >= steps[k])
            def _():
                for c in range(CHUNKS):
                    bwd_copy(m, c, k).wait_send()

        @pl.when(z > 0)
        def _():
            z_copy(m).wait_send()


def per_device(acts, grad_top, w_in, w_out, offsets):
    sections = lax.axis_size("section")
    shards = lax.axis_size("tm")
    import functools

    vmem = pl.BlockSpec(memory_space=pltpu.VMEM)
    d_acts, terms = pl.pallas_call(
        functools.partial(layer_kernel, sections, shards),
        out_shape=(
            jax.ShapeDtypeStruct((MB, ROWS, WIDTH), BF16),
            jax.ShapeDtypeStruct((WIDTH, 4 * WIDTH), BF16),
        ),
        in_specs=[
            vmem,
            vmem,
            pl.BlockSpec(memory_space=pl.ANY),
            pl.BlockSpec(memory_space=pl.ANY),
            pl.BlockSpec(memory_space=pltpu.SMEM),
        ],
        out_specs=(vmem, vmem),
        scratch_shapes=[
            pltpu.VMEM((WIDTH, 3 * WIDTH), BF16),
            pltpu.VMEM((WIDTH, WIDTH), BF16),
            pltpu.VMEM((MB, BLOCKS, ROWS, WIDTH), BF16),
            pltpu.VMEM((MB, ROWS, WIDTH), F32),
            pltpu.VMEM((MB, ROWS, 128), F32),
            pltpu.VMEM((MB, GROUPS, GROUP, GROUP), BF16),
            pltpu.VMEM((MB, KEYS, 2 * WIDTH), BF16),
            pltpu.VMEM((MB, GROUPS, KEYS, GROUP), F32),
            pltpu.VMEM((MB, GROUPS, KEYS, GROUP), BF16),
            pltpu.VMEM((GROUP, GROUP), BF16),
            pltpu.VMEM((KEYS, GROUP), F32),
            pltpu.VMEM((MB, ROWS, WIDTH), BF16),
            pltpu.VMEM((MB * ROWS, WIDTH), BF16),
            pltpu.VMEM((MB, KEYS, 2 * WIDTH), BF16),
            pltpu.VMEM((MB * ROWS, WIDTH), BF16),
            pltpu.VMEM((MB, ROWS, WIDTH), F32),
            pltpu.VMEM((MB, ROWS, WIDTH), BF16),
            pltpu.VMEM((MB, CHUNKS, LEVELS, ROWS, CHUNK), BF16),
            pltpu.VMEM((MB, CHUNKS, LEVELS, ROWS, CHUNK), BF16),
            pltpu.SemaphoreType.DMA((2,)),
            pltpu.SemaphoreType.DMA((MB, LEVELS)),
            pltpu.SemaphoreType.DMA((MB, LEVELS)),
            pltpu.SemaphoreType.DMA((MB, CHUNKS, LEVELS)),
            pltpu.SemaphoreType.DMA((MB, CHUNKS, LEVELS)),
            pltpu.SemaphoreType.DMA((MB,)),
            pltpu.SemaphoreType.DMA((MB,)),
        ],
        compiler_params=pltpu.CompilerParams(
            collective_id=0, has_side_effects=True, vmem_limit_bytes=60 * 1024 * 1024
        ),
        name="layer_kernel",
    )(acts[0], grad_top, w_in[0], w_out[0], offsets)
    summed = lax.psum_scatter(terms, "tm", scatter_dimension=0, tiled=True).astype(F32)
    return (d_acts[None], summed[None, :, : 3 * WIDTH], summed[None, :, 3 * WIDTH :])


def solution(mesh):
    placed = (
        P("section", None, "tm", None),
        P(None, "tm", None),
        P("section", None, None),
        P("section", None, None),
        P("tm", None),
    )
    return jax.shard_map(
        per_device,
        mesh=mesh,
        in_specs=placed,
        out_specs=(
            P("section", None, "tm", None),
            P("section", "tm", None),
            P("section", "tm", None),
        ),
        check_vma=False,
    )
```

```python
import functools

import jax
import jax.numpy as jnp
from jax import lax
from jax.experimental import pallas as pl
from jax.experimental.pallas import tpu as pltpu
from jax.sharding import PartitionSpec as P

HEAD_DIM = 64
SCALE = HEAD_DIM ** (-0.5)
EPSILON = 1e-06
FILL = -1e30
MESH = pl.DeviceIdType.MESH

MB = 2
ROWS = 64
WIDTH = 1024
LEVELS = 5
BLOCKS = LEVELS + 1
KEYS = BLOCKS * ROWS
GROUP = 256
GROUPS = WIDTH // GROUP
CHUNK = 256
CHUNKS = WIDTH // CHUNK
PER = GROUP // HEAD_DIM
SIDE = 4
SLICE = 32
PARTS = 8
COLS = 512
HALF = COLS // 2

BF16 = jnp.bfloat16
F32 = jnp.float32


def dot(a, b):
    return lax.dot_general(a, b, (((1,), (0,)), ((), ())), preferred_element_type=F32)


def dot_nt(a, b):
    return lax.dot_general(a, b, (((1,), (1,)), ((), ())), preferred_element_type=F32)


def dot_tn(a, b):
    return lax.dot_general(a, b, (((0,), (0,)), ((), ())), preferred_element_type=F32)


def layer_kernel(
    sections,
    shards,
    acts_ref,
    gtop_ref,
    w_in_hbm,
    w_out_hbm,
    off_ref,
    dacts_ref,
    dwin_ref,
    dwout_ref,
    w_in,
    w_out,
    nall,
    normed,
    inv,
    qm,
    kv,
    p32,
    p16,
    bm,
    bias,
    inc,
    dq,
    part,
    att,
    ng,
    gsend,
    sbuf,
    rbuf,
    w_sem,
    fs,
    fr,
    bs,
    br,
    zs,
    zr,
    n_t,
    own_t,
    att_t,
    psend,
    precv,
    total,
    send1,
    recv1,
    send2,
    recv2,
    column,
    send3,
    recv3,
    send4,
    recv4,
    ps,
    pr,
    s1,
    r1,
    s2,
    r2,
    s3,
    r3,
    s4,
    r4,
):
    z = lax.axis_index("section")
    t = lax.axis_index("tm")
    steps = [2**level for level in range(LEVELS)]
    place_x = t // 8
    place_y = lax.rem(t // 2, SIDE)
    core = lax.rem(t, 2)
    partner = t + 1 - 2 * core

    def along(axis, step):
        if axis == 0:
            return lax.rem(t + 8 * (step % SIDE), shards)
        return place_x * 8 + lax.rem(place_y + step % SIDE, SIDE) * 2 + core

    def up_shard(k):
        return lax.rem(t + steps[k], shards)

    def down_shard(k):
        return lax.rem(t + shards - steps[k], shards)

    copy_in = pltpu.make_async_copy(w_in_hbm, w_in, w_sem.at[0])
    copy_out = pltpu.make_async_copy(w_out_hbm, w_out, w_sem.at[1])
    copy_in.start()
    copy_out.start()

    barrier = pltpu.get_barrier_semaphore()
    for k in range(LEVELS):
        pl.semaphore_signal(barrier, inc=1, device_id=(z, up_shard(k)), device_id_type=MESH)
        if 2 * steps[k] != shards:
            pl.semaphore_signal(barrier, inc=1, device_id=(z, down_shard(k)), device_id_type=MESH)
    for peer in (along(1, 1), along(1, -1), partner):
        pl.semaphore_signal(barrier, inc=1, device_id=(z, peer), device_id_type=MESH)
    for step in (1, sections - 1):
        pl.semaphore_signal(
            barrier, inc=1, device_id=(lax.rem(z + step, sections), t), device_id_type=MESH
        )

    def fwd_copy(m, k):
        return pltpu.make_async_remote_copy(
            src_ref=nall.at[m, 0],
            dst_ref=nall.at[m, k + 1],
            send_sem=fs.at[m, k],
            recv_sem=fr.at[m, k],
            device_id=(z, up_shard(k)),
            device_id_type=MESH,
        )

    def bwd_copy(m, c, k):
        return pltpu.make_async_remote_copy(
            src_ref=sbuf.at[m, c, k],
            dst_ref=rbuf.at[m, c, k],
            send_sem=bs.at[m, c, k],
            recv_sem=br.at[m, c, k],
            device_id=(z, down_shard(k)),
            device_id_type=MESH,
        )

    def z_copy(m):
        return pltpu.make_async_remote_copy(
            src_ref=gsend.at[m],
            dst_ref=inc.at[m],
            send_sem=zs.at[m],
            recv_sem=zr.at[m],
            device_id=(lax.rem(z + sections - 1, sections), t),
            device_id_type=MESH,
        )

    for m in range(MB):
        x = acts_ref[m].astype(F32)
        inverse = lax.rsqrt(jnp.mean(x * x, axis=-1, keepdims=True) + EPSILON)
        value = x * inverse
        normed[m] = value
        inv[m] = jnp.broadcast_to(inverse, (ROWS, 128))
        nall[m, 0] = value.astype(BF16)
        for k in range(LEVELS):

            @pl.when(t < steps[k])
            def _():
                nall[m, k + 1] = jnp.zeros((ROWS, WIDTH), BF16)

    pl.semaphore_wait(barrier, 2 * LEVELS + 4)

    for m in range(MB):
        for k in reversed(range(LEVELS)):

            @pl.when(t + steps[k] < shards)
            def _():
                fwd_copy(m, k).start()

    row_head = lax.broadcasted_iota(jnp.int32, (GROUP, GROUP), 0) // HEAD_DIM
    lane_head = lax.broadcasted_iota(jnp.int32, (GROUP, GROUP), 1) // HEAD_DIM
    bm[...] = jnp.where(row_head == lane_head, 1.0, 0.0).astype(BF16)
    key_pos = lax.broadcasted_iota(jnp.int32, (ROWS, GROUP), 0)
    query_pos = lax.broadcasted_iota(jnp.int32, (ROWS, GROUP), 1) % ROWS
    bias[0:ROWS, :] = jnp.where(key_pos <= query_pos, 0.0, FILL)
    for k in range(LEVELS):
        fill = jnp.where(off_ref[0, k] != 0, 0.0, FILL)
        bias[(k + 1) * ROWS : (k + 2) * ROWS, :] = jnp.full((ROWS, GROUP), fill, F32)

    @pl.when(z == sections - 1)
    def _():
        inc[...] = gtop_ref[...]

    def spread(rows):
        return jnp.concatenate([rows] * PER, 0) * bm[...]

    def gather_heads(stacked):
        lanes = lax.broadcasted_iota(jnp.int32, (ROWS, GROUP), 1) // HEAD_DIM
        total = jnp.where(lanes == 0, stacked[0:ROWS], 0.0)
        for head in range(1, PER):
            total = jnp.where(lanes == head, stacked[head * ROWS : (head + 1) * ROWS], total)
        return total

    copy_in.wait()
    copy_out.wait()

    def own_query(c, carry):
        cols = pl.ds(pl.multiple_of(c * GROUP, GROUP), GROUP)
        both = jnp.concatenate([nall[0, 0], nall[1, 0]], 0)
        result = dot(both, w_in[:, cols]).astype(BF16)
        for m in range(MB):
            qm[m, c] = spread(result[m * ROWS : (m + 1) * ROWS])
        return carry

    lax.fori_loop(0, GROUPS, own_query, 0)

    def own_pair(c, carry):
        cols = pl.ds(pl.multiple_of(c * GROUP, GROUP), GROUP)
        source = pl.ds(pl.multiple_of(WIDTH + c * GROUP, GROUP), GROUP)
        both = jnp.concatenate([nall[0, 0], nall[1, 0]], 0)
        result = dot(both, w_in[:, source]).astype(BF16)
        for m in range(MB):
            kv[m, 0:ROWS, cols] = result[m * ROWS : (m + 1) * ROWS]
        return carry

    lax.fori_loop(0, 2 * GROUPS, own_pair, 0)

    def forward(m):
        for k in range(LEVELS):

            @pl.when(t >= steps[k])
            def _():
                fwd_copy(m, k).wait_recv()

        def far_pair(c, carry):
            cols = pl.ds(pl.multiple_of(c * GROUP, GROUP), GROUP)
            source = pl.ds(pl.multiple_of(WIDTH + c * GROUP, GROUP), GROUP)
            rows = nall[m, 1:BLOCKS].reshape(LEVELS * ROWS, WIDTH)
            kv[m, ROWS:KEYS, cols] = dot(rows, w_in[:, source]).astype(BF16)
            return carry

        lax.fori_loop(0, 2 * GROUPS, far_pair, 0)

        def probability(g, carry):
            cols = pl.ds(pl.multiple_of(g * GROUP, GROUP), GROUP)
            scores = dot_nt(kv[m, :, cols], qm[m, g]) * SCALE + bias[...]
            highest = jnp.max(scores, axis=0, keepdims=True)
            weights = jnp.exp(scores - highest)
            result = weights / jnp.sum(weights, axis=0, keepdims=True)
            p32[m, g] = result
            p16[m, g] = result.astype(BF16)
            return carry

        lax.fori_loop(0, GROUPS, probability, 0)

    def attend(m):
        def group(g, carry):
            cols = pl.ds(pl.multiple_of(g * GROUP, GROUP), GROUP)
            values = pl.ds(pl.multiple_of(WIDTH + g * GROUP, GROUP), GROUP)
            stacked = dot_tn(p16[m, g], kv[m, :, values])
            att[m * ROWS : (m + 1) * ROWS, cols] = gather_heads(stacked).astype(BF16)
            return carry

        lax.fori_loop(0, GROUPS, group, 0)

    def backward_send(m):
        @pl.when(z < sections - 1)
        def _():
            z_copy(m).wait_recv()

        def group(g, carry):
            cols = pl.ds(pl.multiple_of(g * GROUP, GROUP), GROUP)
            values = pl.ds(pl.multiple_of(WIDTH + g * GROUP, GROUP), GROUP)
            upstream = dot_nt(inc[m], w_out[cols, :]).astype(BF16)
            up_heads = spread(upstream)
            prob_grad = dot_nt(kv[m, :, values], up_heads)
            prob = p32[m, g]
            delta = jnp.sum(prob * prob_grad, axis=0, keepdims=True)
            score_grad = (prob * (prob_grad - delta)).astype(BF16)
            part[m, :, cols] = (dot(score_grad, qm[m, g]) * SCALE).astype(BF16)
            part[m, :, values] = dot(p16[m, g], up_heads).astype(BF16)
            stacked = dot_tn(score_grad, kv[m, :, cols])
            dq[m * ROWS : (m + 1) * ROWS, cols] = (gather_heads(stacked) * SCALE).astype(BF16)
            return carry

        lax.fori_loop(0, GROUPS, group, 0)

        def project(c, carry):
            cols = pl.ds(pl.multiple_of(c * CHUNK, CHUNK), CHUNK)
            result = dot_nt(part[m], w_in[cols, WIDTH : 3 * WIDTH])
            ng[m, :, cols] = result[0:ROWS]
            for k in reversed(range(LEVELS)):
                sbuf[m, c, k] = result[(k + 1) * ROWS : (k + 2) * ROWS].astype(BF16)

                @pl.when(t >= steps[k])
                def _():
                    bwd_copy(m, c, k).start()

            return carry

        lax.fori_loop(0, CHUNKS, project, 0)

        def own(c, carry):
            cols = pl.ds(pl.multiple_of(c * CHUNK, CHUNK), CHUNK)
            ng[m, :, cols] += dot_nt(dq[m * ROWS : (m + 1) * ROWS, :], w_in[cols, 0:WIDTH])
            return carry

        lax.fori_loop(0, CHUNKS, own, 0)

    def backward_finish(m):
        for c in range(CHUNKS):
            for k in range(LEVELS):

                @pl.when(t + steps[k] < shards)
                def _():
                    bwd_copy(m, c, k).wait_recv()
                    cols = slice(c * CHUNK, (c + 1) * CHUNK)
                    ng[m, :, cols] += rbuf[m, c, k].astype(F32)

        grad = ng[m]
        value = normed[m]
        inner = jnp.mean(grad * value, axis=-1, keepdims=True)
        result = (inc[m].astype(F32) + inv[m, :, 0:1] * (grad - value * inner)).astype(BF16)
        dacts_ref[m] = result
        gsend[m] = result

        @pl.when(z > 0)
        def _():
            z_copy(m).start()

    def remote(src, dst, send_sem, recv_sem, peer):
        return pltpu.make_async_remote_copy(
            src_ref=src,
            dst_ref=dst,
            send_sem=send_sem,
            recv_sem=recv_sem,
            device_id=(z, peer),
            device_id_type=MESH,
        )

    def pair_copy(i):
        return remote(psend.at[i], precv.at[i], ps.at[i], pr.at[i], partner)

    def ring_copy(stage, i, side):
        send, recv, ss, rs = ring_refs[stage]
        axis = (i + stage // 2) % 2
        return remote(
            send.at[i, side],
            recv.at[i, side],
            ss.at[i, side],
            rs.at[i, side],
            along(axis, 1 if side == 0 else -1),
        )

    ring_refs = (
        (send1, recv1, s1, r1),
        (send2, recv2, s2, r2),
        (send3, recv3, s3, r3),
        (send4, recv4, s4, r4),
    )

    def transpose_rows():
        def block(r, carry):
            rows = pl.ds(pl.multiple_of(r * CHUNK, CHUNK), CHUNK)
            owns = []
            for m in range(MB):
                tokens = nall[m, :, :, rows].reshape(KEYS, CHUNK)
                turned = tokens.T.reshape(SIDE, 2, SLICE, KEYS)
                for parity in range(2):
                    n_t[parity, r, :, :, m * KEYS : (m + 1) * KEYS] = turned[:, parity]
                owns.append(nall[m, 0, :, rows])
            turned = jnp.concatenate(owns, 0).T.reshape(SIDE, 2, SLICE, MB * ROWS)
            turned_att = att[:, rows].T.reshape(SIDE, 2, SLICE, MB * ROWS)
            for parity in range(2):
                own_t[parity, r] = turned[:, parity]
                att_t[parity, r] = turned_att[:, parity]
            return carry

        lax.fori_loop(0, SIDE, block, 0)

    def operands(i):
        if i < 2:
            return own_t, dq[:, i * COLS : (i + 1) * COLS], i * COLS
        if i < 4:
            low = (i - 2) * COLS
            return (
                att_t,
                inc[:, :, low : low + COLS].reshape(MB * ROWS, COLS),
                3 * WIDTH + low,
            )
        low = (i - 4) * COLS
        return n_t, part[:, :, low : low + COLS].reshape(MB * KEYS, COLS), WIDTH + low

    def weight_part(i):
        left, right, _ = operands(i)
        depth = right.shape[0]
        shape = (SIDE, SIDE, SLICE, COLS)
        away = left[1 - core].reshape(WIDTH // 2, depth)
        psend[i] = dot(away, right).astype(BF16).reshape(shape)
        pair_copy(i).start()
        here = left[core].reshape(WIDTH // 2, depth)
        total[i] = dot(here, right).reshape(shape)

    def pick(i, step):
        axis = i % 2
        where = lax.rem((place_x if axis == 0 else place_y) + step % SIDE, SIDE)
        return total[i, where] if axis == 0 else total[i, :, where]

    def pick_row(i, step):
        axis = (i + 1) % 2
        return column[i, lax.rem((place_x if axis == 0 else place_y) + step % SIDE, SIDE)]

    def ring_one(i):
        pair_copy(i).wait_recv()
        total[i] += precv[i].astype(F32)
        far = pick(i, 2).astype(BF16)
        send1[i, 0] = far[:, :, :HALF]
        send1[i, 1] = far[:, :, HALF:]
        for side in range(2):
            ring_copy(0, i, side).start()

    def ring_two(i):
        for side in range(2):
            ring_copy(0, i, side).wait_recv()
        right, left = pick(i, 1), pick(i, -1)
        send2[i, 0, :, :, :HALF] = (right[:, :, :HALF] + recv1[i, 0].astype(F32)).astype(BF16)
        send2[i, 0, :, :, HALF:] = right[:, :, HALF:].astype(BF16)
        ring_copy(1, i, 0).start()
        send2[i, 1, :, :, :HALF] = left[:, :, :HALF].astype(BF16)
        send2[i, 1, :, :, HALF:] = (left[:, :, HALF:] + recv1[i, 1].astype(F32)).astype(BF16)
        ring_copy(1, i, 1).start()

    def ring_three(i):
        for side in range(2):
            ring_copy(1, i, side).wait_recv()
        column[i] = pick(i, 0) + recv2[i, 0].astype(F32) + recv2[i, 1].astype(F32)
        far = pick_row(i, 2).astype(BF16)
        send3[i, 0] = far[:, :HALF]
        send3[i, 1] = far[:, HALF:]
        for side in range(2):
            ring_copy(2, i, side).start()

    def ring_four(i):
        for side in range(2):
            ring_copy(2, i, side).wait_recv()
        right, left = pick_row(i, 1), pick_row(i, -1)
        send4[i, 0, :, :HALF] = (right[:, :HALF] + recv3[i, 0].astype(F32)).astype(BF16)
        send4[i, 0, :, HALF:] = right[:, HALF:].astype(BF16)
        ring_copy(3, i, 0).start()
        send4[i, 1, :, :HALF] = left[:, :HALF].astype(BF16)
        send4[i, 1, :, HALF:] = (left[:, HALF:] + recv3[i, 1].astype(F32)).astype(BF16)
        ring_copy(3, i, 1).start()

    def ring_last(i):
        for side in range(2):
            ring_copy(3, i, side).wait_recv()
        result = pick_row(i, 0) + recv4[i, 0].astype(F32) + recv4[i, 1].astype(F32)
        low = operands(i)[2]
        if low < 3 * WIDTH:
            dwin_ref[:, low : low + COLS] = result
        else:
            dwout_ref[:, low - 3 * WIDTH : low - 3 * WIDTH + COLS] = result

    forward(0)
    backward_send(0)
    forward(1)
    attend(0)
    attend(1)
    backward_finish(0)
    transpose_rows()
    backward_send(1)

    @pl.when(z > 0)
    def _():
        backward_finish(1)

    for i in range(PARTS + 1):
        if i < PARTS:
            weight_part(i)
        if i >= 1:
            ring_one(i - 1)

    @pl.when(z == 0)
    def _():
        backward_finish(1)

    for i in range(PARTS + 3):
        if i < PARTS:
            ring_two(i)
        if 1 <= i <= PARTS:
            ring_three(i - 1)
        if 2 <= i <= PARTS + 1:
            ring_four(i - 2)
        if i >= 3:
            ring_last(i - 3)

    for i in range(PARTS):
        pair_copy(i).wait_send()
        for stage in range(4):
            for side in range(2):
                ring_copy(stage, i, side).wait_send()

    for m in range(MB):
        for k in range(LEVELS):

            @pl.when(t + steps[k] < shards)
            def _():
                fwd_copy(m, k).wait_send()

            @pl.when(t >= steps[k])
            def _():
                for c in range(CHUNKS):
                    bwd_copy(m, c, k).wait_send()

        @pl.when(z > 0)
        def _():
            z_copy(m).wait_send()


def per_device(acts, grad_top, w_in, w_out, offsets):
    sections = lax.axis_size("section")
    shards = lax.axis_size("tm")
    vmem = pl.BlockSpec(memory_space=pltpu.VMEM)
    d_acts, d_in, d_out = pl.pallas_call(
        functools.partial(layer_kernel, sections, shards),
        out_shape=(
            jax.ShapeDtypeStruct((MB, ROWS, WIDTH), BF16),
            jax.ShapeDtypeStruct((SLICE, 3 * WIDTH), F32),
            jax.ShapeDtypeStruct((SLICE, WIDTH), F32),
        ),
        in_specs=[
            vmem,
            vmem,
            pl.BlockSpec(memory_space=pl.ANY),
            pl.BlockSpec(memory_space=pl.ANY),
            pl.BlockSpec(memory_space=pltpu.SMEM),
        ],
        out_specs=(vmem, vmem, vmem),
        scratch_shapes=[
            pltpu.VMEM((WIDTH, 3 * WIDTH), BF16),
            pltpu.VMEM((WIDTH, WIDTH), BF16),
            pltpu.VMEM((MB, BLOCKS, ROWS, WIDTH), BF16),
            pltpu.VMEM((MB, ROWS, WIDTH), F32),
            pltpu.VMEM((MB, ROWS, 128), F32),
            pltpu.VMEM((MB, GROUPS, GROUP, GROUP), BF16),
            pltpu.VMEM((MB, KEYS, 2 * WIDTH), BF16),
            pltpu.VMEM((MB, GROUPS, KEYS, GROUP), F32),
            pltpu.VMEM((MB, GROUPS, KEYS, GROUP), BF16),
            pltpu.VMEM((GROUP, GROUP), BF16),
            pltpu.VMEM((KEYS, GROUP), F32),
            pltpu.VMEM((MB, ROWS, WIDTH), BF16),
            pltpu.VMEM((MB * ROWS, WIDTH), BF16),
            pltpu.VMEM((MB, KEYS, 2 * WIDTH), BF16),
            pltpu.VMEM((MB * ROWS, WIDTH), BF16),
            pltpu.VMEM((MB, ROWS, WIDTH), F32),
            pltpu.VMEM((MB, ROWS, WIDTH), BF16),
            pltpu.VMEM((MB, CHUNKS, LEVELS, ROWS, CHUNK), BF16),
            pltpu.VMEM((MB, CHUNKS, LEVELS, ROWS, CHUNK), BF16),
            pltpu.SemaphoreType.DMA((2,)),
            pltpu.SemaphoreType.DMA((MB, LEVELS)),
            pltpu.SemaphoreType.DMA((MB, LEVELS)),
            pltpu.SemaphoreType.DMA((MB, CHUNKS, LEVELS)),
            pltpu.SemaphoreType.DMA((MB, CHUNKS, LEVELS)),
            pltpu.SemaphoreType.DMA((MB,)),
            pltpu.SemaphoreType.DMA((MB,)),
            pltpu.VMEM((2, SIDE, SIDE, SLICE, MB * KEYS), BF16),
            pltpu.VMEM((2, SIDE, SIDE, SLICE, MB * ROWS), BF16),
            pltpu.VMEM((2, SIDE, SIDE, SLICE, MB * ROWS), BF16),
            pltpu.VMEM((PARTS, SIDE, SIDE, SLICE, COLS), BF16),
            pltpu.VMEM((PARTS, SIDE, SIDE, SLICE, COLS), BF16),
            pltpu.VMEM((PARTS, SIDE, SIDE, SLICE, COLS), F32),
            pltpu.VMEM((PARTS, 2, SIDE, SLICE, HALF), BF16),
            pltpu.VMEM((PARTS, 2, SIDE, SLICE, HALF), BF16),
            pltpu.VMEM((PARTS, 2, SIDE, SLICE, COLS), BF16),
            pltpu.VMEM((PARTS, 2, SIDE, SLICE, COLS), BF16),
            pltpu.VMEM((PARTS, SIDE, SLICE, COLS), F32),
            pltpu.VMEM((PARTS, 2, SLICE, HALF), BF16),
            pltpu.VMEM((PARTS, 2, SLICE, HALF), BF16),
            pltpu.VMEM((PARTS, 2, SLICE, COLS), BF16),
            pltpu.VMEM((PARTS, 2, SLICE, COLS), BF16),
            pltpu.SemaphoreType.DMA((PARTS,)),
            pltpu.SemaphoreType.DMA((PARTS,)),
        ]
        + [pltpu.SemaphoreType.DMA((PARTS, 2))] * 8,
        compiler_params=pltpu.CompilerParams(
            collective_id=0, has_side_effects=True, vmem_limit_bytes=63 * 1024 * 1024
        ),
        name="layer_kernel",
    )(acts[0], grad_top, w_in[0], w_out[0], offsets)
    return (d_acts[None], d_in[None], d_out[None])


def solution(mesh):
    placed = (
        P("section", None, "tm", None),
        P(None, "tm", None),
        P("section", None, None),
        P("section", None, None),
        P("tm", None),
    )
    return jax.shard_map(
        per_device,
        mesh=mesh,
        in_specs=placed,
        out_specs=(
            P("section", None, "tm", None),
            P("section", "tm", None),
            P("section", "tm", None),
        ),
        check_vma=False,
    )
```

```python
import functools

import jax
import jax.numpy as jnp
from jax import lax
from jax.experimental import pallas as pl
from jax.experimental.pallas import tpu as pltpu
from jax.sharding import PartitionSpec as P

HEAD_DIM = 64
SCALE = HEAD_DIM ** (-0.5)
EPSILON = 1e-06
FILL = -1e30
MESH = pl.DeviceIdType.MESH

MB = 2
ROWS = 64
WIDTH = 1024
LEVELS = 5
BLOCKS = LEVELS + 1
KEYS = BLOCKS * ROWS
GROUP = 256
GROUPS = WIDTH // GROUP
CHUNK = 256
CHUNKS = WIDTH // CHUNK
PER = GROUP // HEAD_DIM
SIDE = 4
SLICE = 32
PARTS = 8
COLS = 512
HALF = COLS // 2

BF16 = jnp.bfloat16
F32 = jnp.float32


def dot(a, b):
    return lax.dot_general(a, b, (((1,), (0,)), ((), ())), preferred_element_type=F32)


def dot_nt(a, b):
    return lax.dot_general(a, b, (((1,), (1,)), ((), ())), preferred_element_type=F32)


def dot_tn(a, b):
    return lax.dot_general(a, b, (((0,), (0,)), ((), ())), preferred_element_type=F32)


def layer_kernel(
    sections,
    shards,
    acts_ref,
    gtop_ref,
    w_in_hbm,
    w_out_hbm,
    off_ref,
    dacts_ref,
    dwin_ref,
    dwout_ref,
    w_in,
    w_out,
    nall,
    normed,
    inv,
    qm,
    kv,
    p32,
    p16,
    bm,
    bias,
    inc,
    dq,
    part,
    att,
    ng,
    gsend,
    sbuf,
    rbuf,
    w_sem,
    fs,
    fr,
    bs,
    br,
    zs,
    zr,
    n_t,
    own_t,
    att_t,
    psend,
    precv,
    total,
    send1,
    recv1,
    send2,
    recv2,
    column,
    send3,
    recv3,
    send4,
    recv4,
    ps,
    pr,
    s1,
    r1,
    s2,
    r2,
    s3,
    r3,
    s4,
    r4,
    sg,
    up32,
    up16,
):
    z = lax.axis_index("section")
    t = lax.axis_index("tm")
    steps = [2**level for level in range(LEVELS)]
    place_x = t // 8
    place_y = lax.rem(t // 2, SIDE)
    core = lax.rem(t, 2)
    partner = t + 1 - 2 * core

    def along(axis, step):
        if axis == 0:
            return lax.rem(t + 8 * (step % SIDE), shards)
        return place_x * 8 + lax.rem(place_y + step % SIDE, SIDE) * 2 + core

    def up_shard(k):
        return lax.rem(t + steps[k], shards)

    def down_shard(k):
        return lax.rem(t + shards - steps[k], shards)

    copy_in = pltpu.make_async_copy(w_in_hbm, w_in, w_sem.at[0])
    copy_out = pltpu.make_async_copy(w_out_hbm, w_out, w_sem.at[1])
    copy_in.start()
    copy_out.start()

    barrier = pltpu.get_barrier_semaphore()
    for k in range(LEVELS):
        pl.semaphore_signal(barrier, inc=1, device_id=(z, up_shard(k)), device_id_type=MESH)
        if 2 * steps[k] != shards:
            pl.semaphore_signal(barrier, inc=1, device_id=(z, down_shard(k)), device_id_type=MESH)
    for peer in (along(1, 1), along(1, -1), partner):
        pl.semaphore_signal(barrier, inc=1, device_id=(z, peer), device_id_type=MESH)
    for step in (1, sections - 1):
        pl.semaphore_signal(
            barrier, inc=1, device_id=(lax.rem(z + step, sections), t), device_id_type=MESH
        )

    def fwd_copy(m, k):
        return pltpu.make_async_remote_copy(
            src_ref=nall.at[m, 0],
            dst_ref=nall.at[m, k + 1],
            send_sem=fs.at[m, k],
            recv_sem=fr.at[m, k],
            device_id=(z, up_shard(k)),
            device_id_type=MESH,
        )

    def bwd_copy(m, c, k):
        return pltpu.make_async_remote_copy(
            src_ref=sbuf.at[m, c, k],
            dst_ref=rbuf.at[m, c, k],
            send_sem=bs.at[m, c, k],
            recv_sem=br.at[m, c, k],
            device_id=(z, down_shard(k)),
            device_id_type=MESH,
        )

    def z_copy(m, h):
        cols = pl.ds(h * COLS, COLS)
        return pltpu.make_async_remote_copy(
            src_ref=gsend.at[m, :, cols],
            dst_ref=inc.at[m, :, cols],
            send_sem=zs.at[m, h],
            recv_sem=zr.at[m, h],
            device_id=(lax.rem(z + sections - 1, sections), t),
            device_id_type=MESH,
        )

    for m in range(MB):
        x = acts_ref[m].astype(F32)
        inverse = lax.rsqrt(jnp.mean(x * x, axis=-1, keepdims=True) + EPSILON)
        value = x * inverse
        normed[m] = value
        inv[m] = jnp.broadcast_to(inverse, (ROWS, 128))
        nall[m, 0] = value.astype(BF16)
        if m == 0:
            pl.semaphore_wait(barrier, 2 * LEVELS + 4)
        for k in reversed(range(LEVELS)):

            @pl.when(t + steps[k] < shards)
            def _():
                fwd_copy(m, k).start()

        for k in range(LEVELS):

            @pl.when(t < steps[k])
            def _():
                nall[m, k + 1] = jnp.zeros((ROWS, WIDTH), BF16)

    row_head = lax.broadcasted_iota(jnp.int32, (GROUP, GROUP), 0) // HEAD_DIM
    lane_head = lax.broadcasted_iota(jnp.int32, (GROUP, GROUP), 1) // HEAD_DIM
    bm[...] = jnp.where(row_head == lane_head, 1.0, 0.0).astype(BF16)
    key_pos = lax.broadcasted_iota(jnp.int32, (ROWS, GROUP), 0)
    query_pos = lax.broadcasted_iota(jnp.int32, (ROWS, GROUP), 1) % ROWS
    bias[0:ROWS, :] = jnp.where(key_pos <= query_pos, 0.0, FILL)
    for k in range(LEVELS):
        fill = jnp.where(off_ref[0, k] != 0, 0.0, FILL)
        bias[(k + 1) * ROWS : (k + 2) * ROWS, :] = jnp.full((ROWS, GROUP), fill, F32)

    @pl.when(z == sections - 1)
    def _():
        inc[...] = gtop_ref[...]

    def spread(rows):
        return jnp.concatenate([rows] * PER, 0) * bm[...]

    def gather_heads(stacked):
        lanes = lax.broadcasted_iota(jnp.int32, (ROWS, GROUP), 1) // HEAD_DIM
        total = jnp.where(lanes == 0, stacked[0:ROWS], 0.0)
        for head in range(1, PER):
            total = jnp.where(lanes == head, stacked[head * ROWS : (head + 1) * ROWS], total)
        return total

    copy_in.wait()
    copy_out.wait()

    def own_query(c, carry):
        cols = pl.ds(pl.multiple_of(c * GROUP, GROUP), GROUP)
        both = jnp.concatenate([nall[0, 0], nall[1, 0]], 0)
        result = dot(both, w_in[:, cols]).astype(BF16)
        for m in range(MB):
            qm[m, c] = spread(result[m * ROWS : (m + 1) * ROWS])
        return carry

    lax.fori_loop(0, GROUPS, own_query, 0)

    def own_pair(c, carry):
        cols = pl.ds(pl.multiple_of(c * GROUP, GROUP), GROUP)
        source = pl.ds(pl.multiple_of(WIDTH + c * GROUP, GROUP), GROUP)
        both = jnp.concatenate([nall[0, 0], nall[1, 0]], 0)
        result = dot(both, w_in[:, source]).astype(BF16)
        for m in range(MB):
            kv[m, 0:ROWS, cols] = result[m * ROWS : (m + 1) * ROWS]
        return carry

    lax.fori_loop(0, 2 * GROUPS, own_pair, 0)

    def forward(m):
        for k in range(LEVELS):

            @pl.when(t >= steps[k])
            def _():
                fwd_copy(m, k).wait_recv()

        def far_pair(c, carry):
            cols = pl.ds(pl.multiple_of(c * GROUP, GROUP), GROUP)
            source = pl.ds(pl.multiple_of(WIDTH + c * GROUP, GROUP), GROUP)
            rows = nall[m, 1:BLOCKS].reshape(LEVELS * ROWS, WIDTH)
            kv[m, ROWS:KEYS, cols] = dot(rows, w_in[:, source]).astype(BF16)
            return carry

        lax.fori_loop(0, 2 * GROUPS, far_pair, 0, unroll=2)

        def probability(g, carry):
            cols = pl.ds(pl.multiple_of(g * GROUP, GROUP), GROUP)
            scores = dot_nt(kv[m, :, cols], qm[m, g]) * SCALE + bias[...]
            highest = jnp.max(scores, axis=0, keepdims=True)
            weights = jnp.exp(scores - highest)
            result = weights / jnp.sum(weights, axis=0, keepdims=True)
            p32[m, g] = result
            p16[m, g] = result.astype(BF16)
            return carry

        lax.fori_loop(0, GROUPS, probability, 0, unroll=True)

    def attend(m):
        def group(g, carry):
            cols = pl.ds(pl.multiple_of(g * GROUP, GROUP), GROUP)
            values = pl.ds(pl.multiple_of(WIDTH + g * GROUP, GROUP), GROUP)
            stacked = dot_tn(p16[m, g], kv[m, :, values])
            att[m * ROWS : (m + 1) * ROWS, cols] = gather_heads(stacked).astype(BF16)
            return carry

        lax.fori_loop(0, GROUPS, group, 0)

    def wait_incoming(m, h):
        z_copy(m, h).wait_recv()

    def stage_upstream(m):
        waits = (z < sections - 1) if m == 0 else (z < sections - 1) & (z > 0)

        @pl.when(waits)
        def _():
            wait_incoming(m, 0)

        def first(g, carry):
            cols = pl.ds(pl.multiple_of(g * GROUP, GROUP), GROUP)
            up32[:, cols] = dot_nt(inc[m, :, 0:COLS], w_out[cols, 0:COLS])
            return carry

        lax.fori_loop(0, GROUPS, first, 0, unroll=True)

        @pl.when(waits)
        def _():
            wait_incoming(m, 1)

        def second(g, carry):
            cols = pl.ds(pl.multiple_of(g * GROUP, GROUP), GROUP)
            rest = dot_nt(inc[m, :, COLS : 2 * COLS], w_out[cols, COLS : 2 * COLS])
            up16[:, cols] = (up32[:, cols] + rest).astype(BF16)
            return carry

        lax.fori_loop(0, GROUPS, second, 0, unroll=True)

    def stage_parts(m):
        def group(g, carry):
            cols = pl.ds(pl.multiple_of(g * GROUP, GROUP), GROUP)
            values = pl.ds(pl.multiple_of(WIDTH + g * GROUP, GROUP), GROUP)
            up_heads = spread(up16[:, cols])
            prob_grad = dot_nt(kv[m, :, values], up_heads)
            part[m, :, values] = dot(p16[m, g], up_heads).astype(BF16)
            prob = p32[m, g]
            delta = jnp.sum(prob * prob_grad, axis=0, keepdims=True)
            score_grad = (prob * (prob_grad - delta)).astype(BF16)
            sg[g] = score_grad
            part[m, :, cols] = (dot(score_grad, qm[m, g]) * SCALE).astype(BF16)
            return carry

        lax.fori_loop(0, GROUPS, group, 0, unroll=True)

    def stage_project(m):
        def project(c, carry):
            cols = pl.ds(pl.multiple_of(c * CHUNK, CHUNK), CHUNK)
            result = dot_nt(part[m, ROWS:KEYS, :], w_in[cols, WIDTH : 3 * WIDTH])
            for k in reversed(range(LEVELS)):
                sbuf[m, c, k] = result[k * ROWS : (k + 1) * ROWS].astype(BF16)

                @pl.when(t >= steps[k])
                def _():
                    bwd_copy(m, c, k).start()

            return carry

        lax.fori_loop(0, CHUNKS, project, 0)

    def stage_query(m):
        def group(g, carry):
            cols = pl.ds(pl.multiple_of(g * GROUP, GROUP), GROUP)
            stacked = dot_tn(sg[g], kv[m, :, cols])
            dq[m * ROWS : (m + 1) * ROWS, cols] = (gather_heads(stacked) * SCALE).astype(BF16)
            return carry

        lax.fori_loop(0, GROUPS, group, 0, unroll=True)

    def stage_own(m):
        def own(c, carry):
            cols = pl.ds(pl.multiple_of(c * CHUNK, CHUNK), CHUNK)
            ng[m, :, cols] = dot_nt(
                dq[m * ROWS : (m + 1) * ROWS, :], w_in[cols, 0:WIDTH]
            ) + dot_nt(part[m, 0:ROWS, :], w_in[cols, WIDTH : 3 * WIDTH])
            return carry

        lax.fori_loop(0, CHUNKS, own, 0)

    def backward_finish(m):
        for c in range(CHUNKS):
            for k in range(LEVELS):

                @pl.when(t + steps[k] < shards)
                def _():
                    bwd_copy(m, c, k).wait_recv()
                    cols = slice(c * CHUNK, (c + 1) * CHUNK)
                    ng[m, :, cols] += rbuf[m, c, k].astype(F32)

        grad = ng[m]
        value = normed[m]
        inner = jnp.mean(grad * value, axis=-1, keepdims=True)
        for h in range(2):
            cols = slice(h * COLS, (h + 1) * COLS)
            change = inv[m, :, 0:1] * (grad[:, cols] - value[:, cols] * inner)
            result = (inc[m, :, cols].astype(F32) + change).astype(BF16)
            gsend[m, :, cols] = result

            @pl.when(z > 0)
            def _():
                z_copy(m, h).start()

            dacts_ref[m, :, cols] = result

    def remote(src, dst, send_sem, recv_sem, peer):
        return pltpu.make_async_remote_copy(
            src_ref=src,
            dst_ref=dst,
            send_sem=send_sem,
            recv_sem=recv_sem,
            device_id=(z, peer),
            device_id_type=MESH,
        )

    def pair_copy(i):
        return remote(psend.at[i], precv.at[i], ps.at[i], pr.at[i], partner)

    def ring_copy(stage, i, side):
        send, recv, ss, rs = ring_refs[stage]
        axis = (i + stage // 2) % 2
        return remote(
            send.at[i, side],
            recv.at[i, side],
            ss.at[i, side],
            rs.at[i, side],
            along(axis, 1 if side == 0 else -1),
        )

    ring_refs = (
        (send1, recv1, s1, r1),
        (send2, recv2, s2, r2),
        (send3, recv3, s3, r3),
        (send4, recv4, s4, r4),
    )

    def transpose_rows():
        def block(r, carry):
            rows = pl.ds(pl.multiple_of(r * CHUNK, CHUNK), CHUNK)
            owns = []
            for m in range(MB):
                tokens = nall[m, :, :, rows].reshape(KEYS, CHUNK)
                turned = tokens.T.reshape(SIDE, 2, SLICE, KEYS)
                for parity in range(2):
                    n_t[parity, r, :, :, m * KEYS : (m + 1) * KEYS] = turned[:, parity]
                owns.append(nall[m, 0, :, rows])
            turned = jnp.concatenate(owns, 0).T.reshape(SIDE, 2, SLICE, MB * ROWS)
            turned_att = att[:, rows].T.reshape(SIDE, 2, SLICE, MB * ROWS)
            for parity in range(2):
                own_t[parity, r] = turned[:, parity]
                att_t[parity, r] = turned_att[:, parity]
            return carry

        lax.fori_loop(0, SIDE, block, 0)

    def operands(i):
        if i < 2:
            low = i * COLS
            right = inc[:, :, low : low + COLS].reshape(MB * ROWS, COLS)
            return att_t, right, 3 * WIDTH + low
        if i < 6:
            low = (i - 2) * COLS
            right = part[:, :, low : low + COLS].reshape(MB * KEYS, COLS)
            return n_t, right, WIDTH + low
        low = (i - 6) * COLS
        return own_t, dq[:, low : low + COLS], low

    def weight_part(i):
        left, right, _ = operands(i)
        depth = right.shape[0]
        shape = (SIDE, SIDE, SLICE, COLS)
        away = left[1 - core].reshape(WIDTH // 2, depth)
        psend[i] = dot(away, right).astype(BF16).reshape(shape)
        pair_copy(i).start()
        here = left[core].reshape(WIDTH // 2, depth)
        total[i] = dot(here, right).reshape(shape)

    def pick(i, step):
        axis = i % 2
        where = lax.rem((place_x if axis == 0 else place_y) + step % SIDE, SIDE)
        return total[i, where] if axis == 0 else total[i, :, where]

    def pick_row(i, step):
        axis = (i + 1) % 2
        return column[i, lax.rem((place_x if axis == 0 else place_y) + step % SIDE, SIDE)]

    def ring_one(i):
        pair_copy(i).wait_recv()
        total[i] += precv[i].astype(F32)
        far = pick(i, 2).astype(BF16)
        send1[i, 0] = far[:, :, :HALF]
        send1[i, 1] = far[:, :, HALF:]
        for side in range(2):
            ring_copy(0, i, side).start()

    def ring_two(i):
        for side in range(2):
            ring_copy(0, i, side).wait_recv()
        right, left = pick(i, 1), pick(i, -1)
        send2[i, 0, :, :, :HALF] = (right[:, :, :HALF] + recv1[i, 0].astype(F32)).astype(BF16)
        send2[i, 0, :, :, HALF:] = right[:, :, HALF:].astype(BF16)
        ring_copy(1, i, 0).start()
        send2[i, 1, :, :, :HALF] = left[:, :, :HALF].astype(BF16)
        send2[i, 1, :, :, HALF:] = (left[:, :, HALF:] + recv1[i, 1].astype(F32)).astype(BF16)
        ring_copy(1, i, 1).start()

    def ring_three(i):
        for side in range(2):
            ring_copy(1, i, side).wait_recv()
        column[i] = pick(i, 0) + recv2[i, 0].astype(F32) + recv2[i, 1].astype(F32)
        far = pick_row(i, 2).astype(BF16)
        send3[i, 0] = far[:, :HALF]
        send3[i, 1] = far[:, HALF:]
        for side in range(2):
            ring_copy(2, i, side).start()

    def ring_four(i):
        for side in range(2):
            ring_copy(2, i, side).wait_recv()
        right, left = pick_row(i, 1), pick_row(i, -1)
        send4[i, 0, :, :HALF] = (right[:, :HALF] + recv3[i, 0].astype(F32)).astype(BF16)
        send4[i, 0, :, HALF:] = right[:, HALF:].astype(BF16)
        ring_copy(3, i, 0).start()
        send4[i, 1, :, :HALF] = left[:, :HALF].astype(BF16)
        send4[i, 1, :, HALF:] = (left[:, HALF:] + recv3[i, 1].astype(F32)).astype(BF16)
        ring_copy(3, i, 1).start()

    def ring_last(i):
        for side in range(2):
            ring_copy(3, i, side).wait_recv()
        result = pick_row(i, 0) + recv4[i, 0].astype(F32) + recv4[i, 1].astype(F32)
        low = (3 * WIDTH if i < 2 else WIDTH - 2 * COLS if i < 6 else -6 * COLS) + i * COLS
        if low < 3 * WIDTH:
            dwin_ref[:, low : low + COLS] = result
        else:
            dwout_ref[:, low - 3 * WIDTH : low - 3 * WIDTH + COLS] = result

    def rest_forward():
        attend(0)
        attend(1)
        transpose_rows()

    last = z == sections - 1
    forward(0)

    @pl.when(z < sections - 1)
    def _():
        forward(1)
        rest_forward()

    stage_upstream(0)
    stage_parts(0)
    stage_project(0)

    @pl.when(last)
    def _():
        forward(1)

    stage_query(0)
    stage_own(0)
    backward_finish(0)

    @pl.when(z == 0)
    def _():
        wait_incoming(1, 0)
        wait_incoming(1, 1)
        weight_part(0)
        weight_part(1)

    stage_upstream(1)
    stage_parts(1)

    @pl.when(z > 0)
    def _():
        stage_project(1)

    stage_query(1)

    @pl.when(z > 0)
    def _():
        stage_own(1)
        backward_finish(1)

        @pl.when(last)
        def _():
            rest_forward()

        weight_part(0)
        weight_part(1)

    ring_one(0)
    for i in range(2, PARTS):
        weight_part(i)
        ring_one(i - 1)
    ring_one(PARTS - 1)

    @pl.when(z == 0)
    def _():
        stage_project(1)
        stage_own(1)

    for i in range(PARTS + 3):
        if i < PARTS:
            ring_two(i)
        if 1 <= i <= PARTS:
            ring_three(i - 1)
        if 2 <= i <= PARTS + 1:
            ring_four(i - 2)
        if i >= 3:
            ring_last(i - 3)
        if i == PARTS - 1:

            @pl.when(z == 0)
            def _():
                backward_finish(1)

    for i in range(PARTS):
        pair_copy(i).wait_send()
        for stage in range(4):
            for side in range(2):
                ring_copy(stage, i, side).wait_send()

    for m in range(MB):
        for k in range(LEVELS):

            @pl.when(t + steps[k] < shards)
            def _():
                fwd_copy(m, k).wait_send()

            @pl.when(t >= steps[k])
            def _():
                for c in range(CHUNKS):
                    bwd_copy(m, c, k).wait_send()

        @pl.when(z > 0)
        def _():
            for h in range(2):
                z_copy(m, h).wait_send()


def result_kernel(a, b, c, a_out, b_out, c_out, a_buf, b_buf, c_buf, sem_in, sem_out):
    sources, buffers, targets = (a, b, c), (a_buf, b_buf, c_buf), (a_out, b_out, c_out)
    fetch = [pltpu.make_async_copy(sources[i], buffers[i], sem_in.at[i]) for i in range(3)]
    store = [pltpu.make_async_copy(buffers[i], targets[i], sem_out.at[i]) for i in range(3)]
    for copy in fetch:
        copy.start()
    for i in range(3):
        fetch[i].wait()
        store[i].start()
    for copy in store:
        copy.wait()


def per_device(acts, grad_top, w_in, w_out, offsets):
    sections = lax.axis_size("section")
    shards = lax.axis_size("tm")
    vmem = pl.BlockSpec(memory_space=pltpu.VMEM)
    d_acts, d_in, d_out = pl.pallas_call(
        functools.partial(layer_kernel, sections, shards),
        out_shape=(
            jax.ShapeDtypeStruct((MB, ROWS, WIDTH), BF16),
            jax.ShapeDtypeStruct((SLICE, 3 * WIDTH), F32),
            jax.ShapeDtypeStruct((SLICE, WIDTH), F32),
        ),
        in_specs=[
            vmem,
            vmem,
            pl.BlockSpec(memory_space=pl.ANY),
            pl.BlockSpec(memory_space=pl.ANY),
            pl.BlockSpec(memory_space=pltpu.SMEM),
        ],
        out_specs=(vmem, vmem, vmem),
        scratch_shapes=[
            pltpu.VMEM((WIDTH, 3 * WIDTH), BF16),
            pltpu.VMEM((WIDTH, WIDTH), BF16),
            pltpu.VMEM((MB, BLOCKS, ROWS, WIDTH), BF16),
            pltpu.VMEM((MB, ROWS, WIDTH), F32),
            pltpu.VMEM((MB, ROWS, 128), F32),
            pltpu.VMEM((MB, GROUPS, GROUP, GROUP), BF16),
            pltpu.VMEM((MB, KEYS, 2 * WIDTH), BF16),
            pltpu.VMEM((MB, GROUPS, KEYS, GROUP), F32),
            pltpu.VMEM((MB, GROUPS, KEYS, GROUP), BF16),
            pltpu.VMEM((GROUP, GROUP), BF16),
            pltpu.VMEM((KEYS, GROUP), F32),
            pltpu.VMEM((MB, ROWS, WIDTH), BF16),
            pltpu.VMEM((MB * ROWS, WIDTH), BF16),
            pltpu.VMEM((MB, KEYS, 2 * WIDTH), BF16),
            pltpu.VMEM((MB * ROWS, WIDTH), BF16),
            pltpu.VMEM((MB, ROWS, WIDTH), F32),
            pltpu.VMEM((MB, ROWS, WIDTH), BF16),
            pltpu.VMEM((MB, CHUNKS, LEVELS, ROWS, CHUNK), BF16),
            pltpu.VMEM((MB, CHUNKS, LEVELS, ROWS, CHUNK), BF16),
            pltpu.SemaphoreType.DMA((2,)),
            pltpu.SemaphoreType.DMA((MB, LEVELS)),
            pltpu.SemaphoreType.DMA((MB, LEVELS)),
            pltpu.SemaphoreType.DMA((MB, CHUNKS, LEVELS)),
            pltpu.SemaphoreType.DMA((MB, CHUNKS, LEVELS)),
            pltpu.SemaphoreType.DMA((MB, 2)),
            pltpu.SemaphoreType.DMA((MB, 2)),
            pltpu.VMEM((2, SIDE, SIDE, SLICE, MB * KEYS), BF16),
            pltpu.VMEM((2, SIDE, SIDE, SLICE, MB * ROWS), BF16),
            pltpu.VMEM((2, SIDE, SIDE, SLICE, MB * ROWS), BF16),
            pltpu.VMEM((PARTS, SIDE, SIDE, SLICE, COLS), BF16),
            pltpu.VMEM((PARTS, SIDE, SIDE, SLICE, COLS), BF16),
            pltpu.VMEM((PARTS, SIDE, SIDE, SLICE, COLS), F32),
            pltpu.VMEM((PARTS, 2, SIDE, SLICE, HALF), BF16),
            pltpu.VMEM((PARTS, 2, SIDE, SLICE, HALF), BF16),
            pltpu.VMEM((PARTS, 2, SIDE, SLICE, COLS), BF16),
            pltpu.VMEM((PARTS, 2, SIDE, SLICE, COLS), BF16),
            pltpu.VMEM((PARTS, SIDE, SLICE, COLS), F32),
            pltpu.VMEM((PARTS, 2, SLICE, HALF), BF16),
            pltpu.VMEM((PARTS, 2, SLICE, HALF), BF16),
            pltpu.VMEM((PARTS, 2, SLICE, COLS), BF16),
            pltpu.VMEM((PARTS, 2, SLICE, COLS), BF16),
            pltpu.SemaphoreType.DMA((PARTS,)),
            pltpu.SemaphoreType.DMA((PARTS,)),
        ]
        + [pltpu.SemaphoreType.DMA((PARTS, 2))] * 8
        + [
            pltpu.VMEM((GROUPS, KEYS, GROUP), BF16),
            pltpu.VMEM((ROWS, WIDTH), F32),
            pltpu.VMEM((ROWS, WIDTH), BF16),
        ],
        compiler_params=pltpu.CompilerParams(
            collective_id=0, has_side_effects=True, vmem_limit_bytes=63 * 1024 * 1024
        ),
        name="layer_kernel",
    )(acts[0], grad_top, w_in[0], w_out[0], offsets)
    results = (d_acts, d_in, d_out)
    anywhere = pl.BlockSpec(memory_space=pl.ANY)
    d_acts, d_in, d_out = pl.pallas_call(
        result_kernel,
        out_shape=tuple(jax.ShapeDtypeStruct(r.shape, r.dtype) for r in results),
        in_specs=[anywhere] * 3,
        out_specs=(anywhere,) * 3,
        scratch_shapes=[pltpu.VMEM(r.shape, r.dtype) for r in results]
        + [pltpu.SemaphoreType.DMA((3,)), pltpu.SemaphoreType.DMA((3,))],
        name="result_kernel",
    )(*results)
    return (d_acts[None], d_in[None], d_out[None])


def solution(mesh):
    placed = (
        P("section", None, "tm", None),
        P(None, "tm", None),
        P("section", None, None),
        P("section", None, None),
        P("tm", None),
    )
    return jax.shard_map(
        per_device,
        mesh=mesh,
        in_specs=placed,
        out_specs=(
            P("section", None, "tm", None),
            P("section", "tm", None),
            P("section", "tm", None),
        ),
        check_vma=False,
    )
```

```python
import functools

import jax
import jax.numpy as jnp
from jax import lax
from jax.experimental import pallas as pl
from jax.experimental.pallas import tpu as pltpu
from jax.sharding import PartitionSpec as P

HEAD_DIM = 64
SCALE = HEAD_DIM ** (-0.5)
EPSILON = 1e-06
FILL = -1e30
MESH = pl.DeviceIdType.MESH

MB = 2
ROWS = 64
WIDTH = 1024
LEVELS = 5
BLOCKS = LEVELS + 1
KEYS = BLOCKS * ROWS
GROUP = 256
GROUPS = WIDTH // GROUP
CHUNK = 256
CHUNKS = WIDTH // CHUNK
PER = GROUP // HEAD_DIM
SIDE = 4
ROW = 8
CROSS = 3
SLICE = 32
PARTS = 8
COLS = 512
HALF = COLS // 2

BF16 = jnp.bfloat16
F32 = jnp.float32


def dot(a, b):
    return lax.dot_general(a, b, (((1,), (0,)), ((), ())), preferred_element_type=F32)


def dot_nt(a, b):
    return lax.dot_general(a, b, (((1,), (1,)), ((), ())), preferred_element_type=F32)


def dot_tn(a, b):
    return lax.dot_general(a, b, (((0,), (0,)), ((), ())), preferred_element_type=F32)


def layer_kernel(
    sections,
    shards,
    acts_ref,
    gtop_ref,
    w_in_hbm,
    w_out_hbm,
    off_ref,
    dacts_ref,
    dwin_ref,
    dwout_ref,
    w_in,
    w_out,
    nall,
    normed,
    inv,
    qm,
    kv,
    p32,
    p16,
    bm,
    bias,
    inc,
    dq,
    part,
    att,
    ng,
    gsend,
    sbuf,
    rbuf,
    w_sem,
    fs,
    fr,
    bs,
    br,
    zs,
    zr,
    n_t,
    own_t,
    att_t,
    psend,
    precv,
    total,
    send1,
    recv1,
    send2,
    recv2,
    column,
    send3,
    recv3,
    send4,
    recv4,
    ps,
    pr,
    s1,
    r1,
    s2,
    r2,
    s3,
    r3,
    s4,
    r4,
    sg,
    up32,
    up16,
    qbuf,
    direct,
    qs,
    qr,
    fq,
    direct1,
    pbuf,
    bp,
    bq,
    fp,
):
    z = lax.axis_index("section")
    t = lax.axis_index("tm")
    steps = [2**level for level in range(LEVELS)]
    place_x = t // 8
    place_y = lax.rem(t // 2, SIDE)
    core = lax.rem(t, 2)
    partner = t + 1 - 2 * core
    column_of = lax.rem(t, ROW)

    def sends_direct_down(k):
        if k == 0:
            return core == 1
        ok = t >= steps[k]
        return ok & (column_of >= steps[k]) if k < CROSS else ok

    def gets_direct_down(k):
        if k == 0:
            return core == 0
        ok = t + steps[k] < shards
        return ok & (column_of + steps[k] < ROW) if k < CROSS else ok

    def sends_direct_up(k):
        return gets_direct_down(k)

    def sends_cross(k):
        return (t >= ROW) & (column_of < steps[k])

    def relays(k):
        return (t >= ROW) & (column_of + steps[k] >= ROW)

    joins = (core == 1) & (t >= 3)
    gives = (core == 0) & (t >= 2)
    relay = (t >= ROW) & (column_of >= ROW // 2)

    def cross_target(k):
        return lax.rem(t + ROW - steps[k], shards)

    def cross_back(k):
        return lax.rem(t + shards - ROW + steps[k], shards)

    def along(axis, step):
        if axis == 0:
            return lax.rem(t + 8 * (step % SIDE), shards)
        return place_x * 8 + lax.rem(place_y + step % SIDE, SIDE) * 2 + core

    def up_shard(k):
        return lax.rem(t + steps[k], shards)

    def down_shard(k):
        return lax.rem(t + shards - steps[k], shards)

    copy_in = pltpu.make_async_copy(w_in_hbm, w_in, w_sem.at[0])
    copy_out = pltpu.make_async_copy(w_out_hbm, w_out, w_sem.at[1])
    copy_in.start()
    copy_out.start()

    barrier = pltpu.get_barrier_semaphore()
    for k in range(LEVELS):
        pl.semaphore_signal(barrier, inc=1, device_id=(z, up_shard(k)), device_id_type=MESH)
        if 2 * steps[k] != shards:
            pl.semaphore_signal(barrier, inc=1, device_id=(z, down_shard(k)), device_id_type=MESH)
    peers = (along(1, 1), along(1, -1), partner)
    peers += (cross_target(1), cross_back(1))
    for peer in peers:
        pl.semaphore_signal(barrier, inc=1, device_id=(z, peer), device_id_type=MESH)
    for step in (1, sections - 1):
        pl.semaphore_signal(
            barrier, inc=1, device_id=(lax.rem(z + step, sections), t), device_id_type=MESH
        )

    def fwd_copy(m, k):
        return pltpu.make_async_remote_copy(
            src_ref=nall.at[m, 0],
            dst_ref=nall.at[m, k + 1],
            send_sem=fs.at[m, k],
            recv_sem=fr.at[m, k],
            device_id=(z, up_shard(k)),
            device_id_type=MESH,
        )

    def bwd_copy(m, c, k):
        return pltpu.make_async_remote_copy(
            src_ref=sbuf.at[m, c, k],
            dst_ref=rbuf.at[m, c, k],
            send_sem=bs.at[m, c, k],
            recv_sem=br.at[m, c, k],
            device_id=(z, down_shard(k)),
            device_id_type=MESH,
        )

    def cross_copy(m, c, k):
        return pltpu.make_async_remote_copy(
            src_ref=sbuf.at[m, c, k],
            dst_ref=qbuf.at[m, c, k],
            send_sem=qs.at[m, c, k],
            recv_sem=qr.at[m, c, k],
            device_id=(z, cross_target(k)),
            device_id_type=MESH,
        )

    def fwd_cross(m, k):
        return pltpu.make_async_remote_copy(
            src_ref=nall.at[m, CROSS + 1],
            dst_ref=nall.at[m, k + 1],
            send_sem=fq.at[m, k],
            recv_sem=fr.at[m, k],
            device_id=(z, cross_back(k)),
            device_id_type=MESH,
        )

    def join_copy(m, c):
        return pltpu.make_async_remote_copy(
            src_ref=sbuf.at[m, c, 0],
            dst_ref=pbuf.at[m, c],
            send_sem=bp.at[m, c],
            recv_sem=bq.at[m, c],
            device_id=(z, partner),
            device_id_type=MESH,
        )

    def fwd_pair(m):
        return pltpu.make_async_remote_copy(
            src_ref=nall.at[m, 2],
            dst_ref=nall.at[m, 1],
            send_sem=fp.at[m],
            recv_sem=fr.at[m, 0],
            device_id=(z, partner),
            device_id_type=MESH,
        )

    def z_copy(m, h):
        cols = pl.ds(h * COLS, COLS)
        return pltpu.make_async_remote_copy(
            src_ref=gsend.at[m, :, cols],
            dst_ref=inc.at[m, :, cols],
            send_sem=zs.at[m, h],
            recv_sem=zr.at[m, h],
            device_id=(lax.rem(z + sections - 1, sections), t),
            device_id_type=MESH,
        )

    def forward_send(m, levels):
        for k in levels:

            @pl.when(sends_direct_up(k))
            def _():
                fwd_copy(m, k).start()

    for m in range(MB):
        x = acts_ref[m].astype(F32)
        inverse = lax.rsqrt(jnp.mean(x * x, axis=-1, keepdims=True) + EPSILON)
        value = x * inverse
        normed[m] = value
        inv[m] = jnp.broadcast_to(inverse, (ROWS, 128))
        nall[m, 0] = value.astype(BF16)
        if m == 0:
            pl.semaphore_wait(barrier, 2 * LEVELS + 6)
        if m == 0:
            forward_send(0, (3, 4, 2, 1, 0))
        else:
            forward_send(1, (3,))

        for k in range(LEVELS):

            @pl.when(t < steps[k])
            def _():
                nall[m, k + 1] = jnp.zeros((ROWS, WIDTH), BF16)

    row_head = lax.broadcasted_iota(jnp.int32, (GROUP, GROUP), 0) // HEAD_DIM
    lane_head = lax.broadcasted_iota(jnp.int32, (GROUP, GROUP), 1) // HEAD_DIM
    bm[...] = jnp.where(row_head == lane_head, 1.0, 0.0).astype(BF16)
    key_pos = lax.broadcasted_iota(jnp.int32, (ROWS, GROUP), 0)
    query_pos = lax.broadcasted_iota(jnp.int32, (ROWS, GROUP), 1) % ROWS
    bias[0:ROWS, :] = jnp.where(key_pos <= query_pos, 0.0, FILL)
    for k in range(LEVELS):
        fill = jnp.where(off_ref[0, k] != 0, 0.0, FILL)
        bias[(k + 1) * ROWS : (k + 2) * ROWS, :] = jnp.full((ROWS, GROUP), fill, F32)

    @pl.when(z == sections - 1)
    def _():
        inc[...] = gtop_ref[...]

    def spread(rows):
        return jnp.concatenate([rows] * PER, 0) * bm[...]

    def gather_heads(stacked):
        lanes = lax.broadcasted_iota(jnp.int32, (ROWS, GROUP), 1) // HEAD_DIM
        total = jnp.where(lanes == 0, stacked[0:ROWS], 0.0)
        for head in range(1, PER):
            total = jnp.where(lanes == head, stacked[head * ROWS : (head + 1) * ROWS], total)
        return total

    copy_in.wait()
    copy_out.wait()

    def own_query(c, carry):
        cols = pl.ds(pl.multiple_of(c * GROUP, GROUP), GROUP)
        both = jnp.concatenate([nall[0, 0], nall[1, 0]], 0)
        result = dot(both, w_in[:, cols]).astype(BF16)
        for m in range(MB):
            qm[m, c] = spread(result[m * ROWS : (m + 1) * ROWS])
        return carry

    def own_pair(c, carry):
        cols = pl.ds(pl.multiple_of(c * GROUP, GROUP), GROUP)
        source = pl.ds(pl.multiple_of(WIDTH + c * GROUP, GROUP), GROUP)
        both = jnp.concatenate([nall[0, 0], nall[1, 0]], 0)
        result = dot(both, w_in[:, source]).astype(BF16)
        for m in range(MB):
            kv[m, 0:ROWS, cols] = result[m * ROWS : (m + 1) * ROWS]
        return carry

    def own_projections():
        lax.fori_loop(0, GROUPS, own_query, 0, unroll=2)
        lax.fori_loop(0, 2 * GROUPS, own_pair, 0, unroll=2)

    def forward_relay(m):
        @pl.when(t >= steps[CROSS])
        def _():
            fwd_copy(m, CROSS).wait_recv()

        for k in reversed(range(1, CROSS)):

            @pl.when(relays(k))
            def _():
                fwd_cross(m, k).start()

    def forward_join(m):
        @pl.when(t >= steps[1])
        def _():
            fwd_copy(m, 1).wait_recv()

        @pl.when(joins)
        def _():
            fwd_pair(m).start()

    def forward(m):
        for k in (0, 2, 4):

            @pl.when(t >= steps[k])
            def _():
                fwd_copy(m, k).wait_recv()

        def far_pair(c, carry):
            cols = pl.ds(pl.multiple_of(c * GROUP, GROUP), GROUP)
            source = pl.ds(pl.multiple_of(WIDTH + c * GROUP, GROUP), GROUP)
            rows = nall[m, 1:BLOCKS].reshape(LEVELS * ROWS, WIDTH)
            kv[m, ROWS:KEYS, cols] = dot(rows, w_in[:, source]).astype(BF16)
            return carry

        lax.fori_loop(0, 2 * GROUPS, far_pair, 0, unroll=2)

        def probability(g, carry):
            cols = pl.ds(pl.multiple_of(g * GROUP, GROUP), GROUP)
            scores = dot_nt(kv[m, :, cols], qm[m, g]) * SCALE + bias[...]
            highest = jnp.max(scores, axis=0, keepdims=True)
            weights = jnp.exp(scores - highest)
            result = weights / jnp.sum(weights, axis=0, keepdims=True)
            p32[m, g] = result
            p16[m, g] = result.astype(BF16)
            return carry

        lax.fori_loop(0, GROUPS, probability, 0, unroll=True)

    def attend(m):
        def group(g, carry):
            cols = pl.ds(pl.multiple_of(g * GROUP, GROUP), GROUP)
            values = pl.ds(pl.multiple_of(WIDTH + g * GROUP, GROUP), GROUP)
            stacked = dot_tn(p16[m, g], kv[m, :, values])
            att[m * ROWS : (m + 1) * ROWS, cols] = gather_heads(stacked).astype(BF16)
            return carry

        lax.fori_loop(0, GROUPS, group, 0)

    def wait_incoming(m, h):
        z_copy(m, h).wait_recv()

    def stage_upstream(m):
        waits = (z < sections - 1) if m == 0 else (z < sections - 1) & (z > 0)

        @pl.when(waits)
        def _():
            wait_incoming(m, 0)

        def first(g, carry):
            cols = pl.ds(pl.multiple_of(g * GROUP, GROUP), GROUP)
            up32[:, cols] = dot_nt(inc[m, :, 0:COLS], w_out[cols, 0:COLS])
            return carry

        lax.fori_loop(0, GROUPS, first, 0, unroll=True)

        @pl.when(waits)
        def _():
            wait_incoming(m, 1)

        def second(g, carry):
            cols = pl.ds(pl.multiple_of(g * GROUP, GROUP), GROUP)
            rest = dot_nt(inc[m, :, COLS : 2 * COLS], w_out[cols, COLS : 2 * COLS])
            up16[:, cols] = (up32[:, cols] + rest).astype(BF16)
            return carry

        lax.fori_loop(0, GROUPS, second, 0, unroll=True)

    def stage_parts(m):
        def group(g, carry):
            cols = pl.ds(pl.multiple_of(g * GROUP, GROUP), GROUP)
            values = pl.ds(pl.multiple_of(WIDTH + g * GROUP, GROUP), GROUP)
            up_heads = spread(up16[:, cols])
            prob_grad = dot_nt(kv[m, :, values], up_heads)
            part[m, :, values] = dot(p16[m, g], up_heads).astype(BF16)
            prob = p32[m, g]
            delta = jnp.sum(prob * prob_grad, axis=0, keepdims=True)
            score_grad = (prob * (prob_grad - delta)).astype(BF16)
            sg[g] = score_grad
            part[m, :, cols] = (dot(score_grad, qm[m, g]) * SCALE).astype(BF16)
            return carry

        lax.fori_loop(0, GROUPS, group, 0, unroll=True)

    def stage_project(m):
        def project(c, carry):
            cols = pl.ds(pl.multiple_of(c * CHUNK, CHUNK), CHUNK)
            result = dot_nt(part[m, ROWS:KEYS, :], w_in[cols, WIDTH : 3 * WIDTH])
            for k in (2, 0, 1, 4, 3):
                term = result[k * ROWS : (k + 1) * ROWS]
                sbuf[m, c, k] = term.astype(BF16)
                send = sends_direct_down(k)
                if k == 0:

                    @pl.when(gives)
                    def _():
                        join_copy(m, c).start()

                if k == 1:
                    direct1[c] = term
                    send = send & jnp.logical_not(joins)

                    @pl.when(sends_cross(k) & jnp.logical_not(joins))
                    def _():
                        cross_copy(m, c, k).start()

                if k == 2:

                    @pl.when(sends_cross(k))
                    def _():
                        cross_copy(m, c, k).start()

                if k == CROSS:
                    direct[c] = term
                    send = send & jnp.logical_not(relay)

                @pl.when(send)
                def _():
                    bwd_copy(m, c, k).start()

            @pl.when(joins & (c > 0))
            def _():
                join_send(m, c - 1)

            return carry

        def join_send(m, c):
            join_copy(m, c).wait_recv()
            sbuf[m, c, 1] = (direct1[c] + pbuf[m, c].astype(F32)).astype(BF16)

            @pl.when(sends_direct_down(1))
            def _():
                bwd_copy(m, c, 1).start()

            @pl.when(sends_cross(1))
            def _():
                cross_copy(m, c, 1).start()

        lax.fori_loop(0, CHUNKS, project, 0)

        @pl.when(joins)
        def _():
            join_send(m, CHUNKS - 1)

    def stage_relay(m):
        @pl.when(relay)
        def _():
            for c in range(CHUNKS):
                for k in reversed(range(1, CROSS)):

                    @pl.when(relays(k))
                    def _():
                        cross_copy(m, c, k).wait_recv()
                        direct[c] += qbuf[m, c, k].astype(F32)

                sbuf[m, c, CROSS] = direct[c].astype(BF16)
                bwd_copy(m, c, CROSS).start()

    def stage_query(m):
        def group(g, carry):
            cols = pl.ds(pl.multiple_of(g * GROUP, GROUP), GROUP)
            stacked = dot_tn(sg[g], kv[m, :, cols])
            dq[m * ROWS : (m + 1) * ROWS, cols] = (gather_heads(stacked) * SCALE).astype(BF16)
            return carry

        lax.fori_loop(0, GROUPS, group, 0, unroll=True)

    def stage_own(m):
        def own(c, carry):
            cols = pl.ds(pl.multiple_of(c * CHUNK, CHUNK), CHUNK)
            ng[m, :, cols] = dot_nt(
                dq[m * ROWS : (m + 1) * ROWS, :], w_in[cols, 0:WIDTH]
            ) + dot_nt(part[m, 0:ROWS, :], w_in[cols, WIDTH : 3 * WIDTH])
            return carry

        lax.fori_loop(0, CHUNKS, own, 0)

    def backward_finish(m):
        for c in range(CHUNKS):
            for k in range(LEVELS):

                @pl.when(gets_direct_down(k))
                def _():
                    bwd_copy(m, c, k).wait_recv()
                    cols = slice(c * CHUNK, (c + 1) * CHUNK)
                    ng[m, :, cols] += rbuf[m, c, k].astype(F32)

        grad = ng[m]
        value = normed[m]
        inner = jnp.mean(grad * value, axis=-1, keepdims=True)
        for h in range(2):
            cols = slice(h * COLS, (h + 1) * COLS)
            change = inv[m, :, 0:1] * (grad[:, cols] - value[:, cols] * inner)
            result = (inc[m, :, cols].astype(F32) + change).astype(BF16)
            gsend[m, :, cols] = result

            @pl.when(z > 0)
            def _():
                z_copy(m, h).start()

            dacts_ref[m, :, cols] = result

    def remote(src, dst, send_sem, recv_sem, peer):
        return pltpu.make_async_remote_copy(
            src_ref=src,
            dst_ref=dst,
            send_sem=send_sem,
            recv_sem=recv_sem,
            device_id=(z, peer),
            device_id_type=MESH,
        )

    def pair_copy(i):
        return remote(psend.at[i], precv.at[i], ps.at[i], pr.at[i], partner)

    def ring_copy(stage, i, side):
        send, recv, ss, rs = ring_refs[stage]
        axis = (i + stage // 2) % 2
        return remote(
            send.at[i, side],
            recv.at[i, side],
            ss.at[i, side],
            rs.at[i, side],
            along(axis, 1 if side == 0 else -1),
        )

    ring_refs = (
        (send1, recv1, s1, r1),
        (send2, recv2, s2, r2),
        (send3, recv3, s3, r3),
        (send4, recv4, s4, r4),
    )

    def transpose_rows():
        def block(r, carry):
            rows = pl.ds(pl.multiple_of(r * CHUNK, CHUNK), CHUNK)
            owns = []
            for m in range(MB):
                tokens = nall[m, :, :, rows].reshape(KEYS, CHUNK)
                turned = tokens.T.reshape(SIDE, 2, SLICE, KEYS)
                for parity in range(2):
                    n_t[parity, r, :, :, m * KEYS : (m + 1) * KEYS] = turned[:, parity]
                owns.append(nall[m, 0, :, rows])
            turned = jnp.concatenate(owns, 0).T.reshape(SIDE, 2, SLICE, MB * ROWS)
            turned_att = att[:, rows].T.reshape(SIDE, 2, SLICE, MB * ROWS)
            for parity in range(2):
                own_t[parity, r] = turned[:, parity]
                att_t[parity, r] = turned_att[:, parity]
            return carry

        lax.fori_loop(0, SIDE, block, 0)

    def operands(i):
        if i < 2:
            low = i * COLS
            right = inc[:, :, low : low + COLS].reshape(MB * ROWS, COLS)
            return att_t, right, 3 * WIDTH + low
        if i < 6:
            low = (i - 2) * COLS
            right = part[:, :, low : low + COLS].reshape(MB * KEYS, COLS)
            return n_t, right, WIDTH + low
        low = (i - 6) * COLS
        return own_t, dq[:, low : low + COLS], low

    def weight_part(i):
        left, right, _ = operands(i)
        depth = right.shape[0]
        shape = (SIDE, SIDE, SLICE, COLS)
        away = left[1 - core].reshape(WIDTH // 2, depth)
        psend[i] = dot(away, right).astype(BF16).reshape(shape)
        pair_copy(i).start()
        here = left[core].reshape(WIDTH // 2, depth)
        total[i] = dot(here, right).reshape(shape)

    def pick(i, step):
        axis = i % 2
        where = lax.rem((place_x if axis == 0 else place_y) + step % SIDE, SIDE)
        return total[i, where] if axis == 0 else total[i, :, where]

    def pick_row(i, step):
        axis = (i + 1) % 2
        return column[i, lax.rem((place_x if axis == 0 else place_y) + step % SIDE, SIDE)]

    def ring_one(i):
        pair_copy(i).wait_recv()
        total[i] += precv[i].astype(F32)
        far = pick(i, 2).astype(BF16)
        send1[i, 0] = far[:, :, :HALF]
        send1[i, 1] = far[:, :, HALF:]
        for side in range(2):
            ring_copy(0, i, side).start()

    def ring_two(i):
        for side in range(2):
            ring_copy(0, i, side).wait_recv()
        right, left = pick(i, 1), pick(i, -1)
        send2[i, 0, :, :, :HALF] = (right[:, :, :HALF] + recv1[i, 0].astype(F32)).astype(BF16)
        send2[i, 0, :, :, HALF:] = right[:, :, HALF:].astype(BF16)
        ring_copy(1, i, 0).start()
        send2[i, 1, :, :, :HALF] = left[:, :, :HALF].astype(BF16)
        send2[i, 1, :, :, HALF:] = (left[:, :, HALF:] + recv1[i, 1].astype(F32)).astype(BF16)
        ring_copy(1, i, 1).start()

    def ring_three(i):
        for side in range(2):
            ring_copy(1, i, side).wait_recv()
        column[i] = pick(i, 0) + recv2[i, 0].astype(F32) + recv2[i, 1].astype(F32)
        far = pick_row(i, 2).astype(BF16)
        send3[i, 0] = far[:, :HALF]
        send3[i, 1] = far[:, HALF:]
        for side in range(2):
            ring_copy(2, i, side).start()

    def ring_four(i):
        for side in range(2):
            ring_copy(2, i, side).wait_recv()
        right, left = pick_row(i, 1), pick_row(i, -1)
        send4[i, 0, :, :HALF] = (right[:, :HALF] + recv3[i, 0].astype(F32)).astype(BF16)
        send4[i, 0, :, HALF:] = right[:, HALF:].astype(BF16)
        ring_copy(3, i, 0).start()
        send4[i, 1, :, :HALF] = left[:, :HALF].astype(BF16)
        send4[i, 1, :, HALF:] = (left[:, HALF:] + recv3[i, 1].astype(F32)).astype(BF16)
        ring_copy(3, i, 1).start()

    def ring_last(i):
        for side in range(2):
            ring_copy(3, i, side).wait_recv()
        result = pick_row(i, 0) + recv4[i, 0].astype(F32) + recv4[i, 1].astype(F32)
        low = (3 * WIDTH if i < 2 else WIDTH - 2 * COLS if i < 6 else -6 * COLS) + i * COLS
        if low < 3 * WIDTH:
            dwin_ref[:, low : low + COLS] = result
        else:
            dwout_ref[:, low - 3 * WIDTH : low - 3 * WIDTH + COLS] = result

    def rest_forward():
        attend(0)
        attend(1)
        transpose_rows()

    last = z == sections - 1
    forward_relay(0)
    forward_send(1, (4, 2, 1, 0))
    own_projections()
    forward_join(0)
    forward_relay(1)
    forward(0)
    forward_join(1)

    @pl.when(z < sections - 1)
    def _():
        forward(1)
        rest_forward()

    stage_upstream(0)
    stage_parts(0)
    stage_project(0)

    @pl.when(last)
    def _():
        forward(1)

    stage_query(0)
    stage_relay(0)
    stage_own(0)
    backward_finish(0)

    @pl.when(z == 0)
    def _():
        wait_incoming(1, 0)
        wait_incoming(1, 1)
        weight_part(0)
        weight_part(1)

    stage_upstream(1)

    @pl.when(z == 0)
    def _():
        ring_one(0)
        ring_one(1)

    stage_parts(1)

    @pl.when(z > 0)
    def _():
        stage_project(1)

    stage_query(1)

    @pl.when(z > 0)
    def _():
        stage_relay(1)
        stage_own(1)
        backward_finish(1)

        @pl.when(last)
        def _():
            rest_forward()

        weight_part(0)
        weight_part(1)
        ring_one(0)
        ring_one(1)

    for i in range(2, PARTS):
        weight_part(i)
        if i > 2:
            ring_one(i - 1)
    ring_one(PARTS - 1)

    @pl.when(z == 0)
    def _():
        stage_project(1)
        stage_own(1)
        stage_relay(1)

    for i in range(PARTS + 3):
        if i < PARTS:
            ring_two(i)
        if 1 <= i <= PARTS:
            ring_three(i - 1)
        if 2 <= i <= PARTS + 1:
            ring_four(i - 2)
        if i >= 3:
            ring_last(i - 3)
        if i == PARTS - 1:

            @pl.when(z == 0)
            def _():
                backward_finish(1)

    for i in range(PARTS):
        pair_copy(i).wait_send()
        for stage in range(4):
            for side in range(2):
                ring_copy(stage, i, side).wait_send()

    for m in range(MB):
        for k in range(LEVELS):

            @pl.when(sends_direct_up(k))
            def _():
                fwd_copy(m, k).wait_send()

            @pl.when(sends_direct_down(k))
            def _():
                for c in range(CHUNKS):
                    bwd_copy(m, c, k).wait_send()

            if 0 < k < CROSS:

                @pl.when(relays(k))
                def _():
                    fwd_cross(m, k).wait_send()

                @pl.when(sends_cross(k))
                def _():
                    for c in range(CHUNKS):
                        cross_copy(m, c, k).wait_send()

        @pl.when(joins)
        def _():
            fwd_pair(m).wait_send()

        @pl.when(gives)
        def _():
            for c in range(CHUNKS):
                join_copy(m, c).wait_send()

        @pl.when(z > 0)
        def _():
            for h in range(2):
                z_copy(m, h).wait_send()


def result_kernel(a, b, c, a_out, b_out, c_out, a_buf, b_buf, c_buf, sem_in, sem_out):
    sources, buffers, targets = (a, b, c), (a_buf, b_buf, c_buf), (a_out, b_out, c_out)
    fetch = [pltpu.make_async_copy(sources[i], buffers[i], sem_in.at[i]) for i in range(3)]
    store = [pltpu.make_async_copy(buffers[i], targets[i], sem_out.at[i]) for i in range(3)]
    for copy in fetch:
        copy.start()
    for i in range(3):
        fetch[i].wait()
        store[i].start()
    for copy in store:
        copy.wait()


def per_device(acts, grad_top, w_in, w_out, offsets):
    sections = lax.axis_size("section")
    shards = lax.axis_size("tm")
    vmem = pl.BlockSpec(memory_space=pltpu.VMEM)
    d_acts, d_in, d_out = pl.pallas_call(
        functools.partial(layer_kernel, sections, shards),
        out_shape=(
            jax.ShapeDtypeStruct((MB, ROWS, WIDTH), BF16),
            jax.ShapeDtypeStruct((SLICE, 3 * WIDTH), F32),
            jax.ShapeDtypeStruct((SLICE, WIDTH), F32),
        ),
        in_specs=[
            vmem,
            vmem,
            pl.BlockSpec(memory_space=pl.ANY),
            pl.BlockSpec(memory_space=pl.ANY),
            pl.BlockSpec(memory_space=pltpu.SMEM),
        ],
        out_specs=(vmem, vmem, vmem),
        scratch_shapes=[
            pltpu.VMEM((WIDTH, 3 * WIDTH), BF16),
            pltpu.VMEM((WIDTH, WIDTH), BF16),
            pltpu.VMEM((MB, BLOCKS, ROWS, WIDTH), BF16),
            pltpu.VMEM((MB, ROWS, WIDTH), F32),
            pltpu.VMEM((MB, ROWS, 128), F32),
            pltpu.VMEM((MB, GROUPS, GROUP, GROUP), BF16),
            pltpu.VMEM((MB, KEYS, 2 * WIDTH), BF16),
            pltpu.VMEM((MB, GROUPS, KEYS, GROUP), F32),
            pltpu.VMEM((MB, GROUPS, KEYS, GROUP), BF16),
            pltpu.VMEM((GROUP, GROUP), BF16),
            pltpu.VMEM((KEYS, GROUP), F32),
            pltpu.VMEM((MB, ROWS, WIDTH), BF16),
            pltpu.VMEM((MB * ROWS, WIDTH), BF16),
            pltpu.VMEM((MB, KEYS, 2 * WIDTH), BF16),
            pltpu.VMEM((MB * ROWS, WIDTH), BF16),
            pltpu.VMEM((MB, ROWS, WIDTH), F32),
            pltpu.VMEM((MB, ROWS, WIDTH), BF16),
            pltpu.VMEM((MB, CHUNKS, LEVELS, ROWS, CHUNK), BF16),
            pltpu.VMEM((MB, CHUNKS, LEVELS, ROWS, CHUNK), BF16),
            pltpu.SemaphoreType.DMA((2,)),
            pltpu.SemaphoreType.DMA((MB, LEVELS)),
            pltpu.SemaphoreType.DMA((MB, LEVELS)),
            pltpu.SemaphoreType.DMA((MB, CHUNKS, LEVELS)),
            pltpu.SemaphoreType.DMA((MB, CHUNKS, LEVELS)),
            pltpu.SemaphoreType.DMA((MB, 2)),
            pltpu.SemaphoreType.DMA((MB, 2)),
            pltpu.VMEM((2, SIDE, SIDE, SLICE, MB * KEYS), BF16),
            pltpu.VMEM((2, SIDE, SIDE, SLICE, MB * ROWS), BF16),
            pltpu.VMEM((2, SIDE, SIDE, SLICE, MB * ROWS), BF16),
            pltpu.VMEM((PARTS, SIDE, SIDE, SLICE, COLS), BF16),
            pltpu.VMEM((PARTS, SIDE, SIDE, SLICE, COLS), BF16),
            pltpu.VMEM((PARTS, SIDE, SIDE, SLICE, COLS), F32),
            pltpu.VMEM((PARTS, 2, SIDE, SLICE, HALF), BF16),
            pltpu.VMEM((PARTS, 2, SIDE, SLICE, HALF), BF16),
            pltpu.VMEM((PARTS, 2, SIDE, SLICE, COLS), BF16),
            pltpu.VMEM((PARTS, 2, SIDE, SLICE, COLS), BF16),
            pltpu.VMEM((PARTS, SIDE, SLICE, COLS), F32),
            pltpu.VMEM((PARTS, 2, SLICE, HALF), BF16),
            pltpu.VMEM((PARTS, 2, SLICE, HALF), BF16),
            pltpu.VMEM((PARTS, 2, SLICE, COLS), BF16),
            pltpu.VMEM((PARTS, 2, SLICE, COLS), BF16),
            pltpu.SemaphoreType.DMA((PARTS,)),
            pltpu.SemaphoreType.DMA((PARTS,)),
        ]
        + [pltpu.SemaphoreType.DMA((PARTS, 2))] * 8
        + [
            pltpu.VMEM((GROUPS, KEYS, GROUP), BF16),
            pltpu.VMEM((ROWS, WIDTH), F32),
            pltpu.VMEM((ROWS, WIDTH), BF16),
            pltpu.VMEM((MB, CHUNKS, CROSS, ROWS, CHUNK), BF16),
            pltpu.VMEM((CHUNKS, ROWS, CHUNK), F32),
            pltpu.SemaphoreType.DMA((MB, CHUNKS, CROSS)),
            pltpu.SemaphoreType.DMA((MB, CHUNKS, CROSS)),
            pltpu.SemaphoreType.DMA((MB, CROSS)),
            pltpu.VMEM((CHUNKS, ROWS, CHUNK), F32),
            pltpu.VMEM((MB, CHUNKS, ROWS, CHUNK), BF16),
            pltpu.SemaphoreType.DMA((MB, CHUNKS)),
            pltpu.SemaphoreType.DMA((MB, CHUNKS)),
            pltpu.SemaphoreType.DMA((MB,)),
        ],
        compiler_params=pltpu.CompilerParams(
            collective_id=0, has_side_effects=True, vmem_limit_bytes=63 * 1024 * 1024
        ),
        name="layer_kernel",
    )(acts[0], grad_top, w_in[0], w_out[0], offsets)
    results = (d_acts, d_in, d_out)
    anywhere = pl.BlockSpec(memory_space=pl.ANY)
    d_acts, d_in, d_out = pl.pallas_call(
        result_kernel,
        out_shape=tuple(jax.ShapeDtypeStruct(r.shape, r.dtype) for r in results),
        in_specs=[anywhere] * 3,
        out_specs=(anywhere,) * 3,
        scratch_shapes=[pltpu.VMEM(r.shape, r.dtype) for r in results]
        + [pltpu.SemaphoreType.DMA((3,)), pltpu.SemaphoreType.DMA((3,))],
        name="result_kernel",
    )(*results)
    return (d_acts[None], d_in[None], d_out[None])


def solution(mesh):
    placed = (
        P("section", None, "tm", None),
        P(None, "tm", None),
        P("section", None, None),
        P("section", None, None),
        P("tm", None),
    )
    return jax.shard_map(
        per_device,
        mesh=mesh,
        in_specs=placed,
        out_specs=(
            P("section", None, "tm", None),
            P("section", "tm", None),
            P("section", "tm", None),
        ),
        check_vma=False,
    )
```

```python
import functools

import jax
import jax.numpy as jnp
from jax import lax
from jax.experimental import pallas as pl
from jax.experimental.pallas import tpu as pltpu
from jax.sharding import PartitionSpec as P

HEAD_DIM = 64
SCALE = HEAD_DIM ** (-0.5)
EPSILON = 1e-06
FILL = -1e30
MESH = pl.DeviceIdType.MESH

MB = 2
ROWS = 64
WIDTH = 1024
LEVELS = 5
BLOCKS = LEVELS + 1
KEYS = BLOCKS * ROWS
GROUP = 256
GROUPS = WIDTH // GROUP
CHUNK = 256
CHUNKS = WIDTH // CHUNK
PER = GROUP // HEAD_DIM
SIDE = 4
ROW = 8
CROSS = 3
SLICE = 32
PARTS = 8
COLS = 512
HALF = COLS // 2

BF16 = jnp.bfloat16
F32 = jnp.float32


def dot(a, b):
    return lax.dot_general(a, b, (((1,), (0,)), ((), ())), preferred_element_type=F32)


def dot_nt(a, b):
    return lax.dot_general(a, b, (((1,), (1,)), ((), ())), preferred_element_type=F32)


def dot_tn(a, b):
    return lax.dot_general(a, b, (((0,), (0,)), ((), ())), preferred_element_type=F32)


def layer_kernel(
    sections,
    shards,
    acts_ref,
    gtop_ref,
    w_in_hbm,
    w_out_hbm,
    off_ref,
    dacts_ref,
    dwin_ref,
    dwout_ref,
    w_in,
    w_out,
    nall,
    normed,
    inv,
    qm,
    kv,
    p32,
    p16,
    bm,
    bias,
    inc,
    dq,
    part,
    att,
    ng,
    gsend,
    sbuf,
    rbuf,
    w_sem,
    fs,
    fr,
    bs,
    br,
    zs,
    zr,
    n_t,
    own_t,
    att_t,
    psend,
    precv,
    total,
    send1,
    recv1,
    send2,
    recv2,
    column,
    send3,
    recv3,
    send4,
    recv4,
    ps,
    pr,
    s1,
    r1,
    s2,
    r2,
    s3,
    r3,
    s4,
    r4,
    sg,
    up32,
    up16,
    qbuf,
    direct,
    qs,
    qr,
    fq,
    direct1,
    pbuf,
    bp,
    bq,
    fp,
):
    z = lax.axis_index("section")
    t = lax.axis_index("tm")
    steps = [2**level for level in range(LEVELS)]
    place_x = t // 8
    place_y = lax.rem(t // 2, SIDE)
    core = lax.rem(t, 2)
    partner = t + 1 - 2 * core
    column_of = lax.rem(t, ROW)

    def sends_direct_down(k):
        if k == 0:
            return core == 1
        ok = t >= steps[k]
        return ok & (column_of >= steps[k]) if k < CROSS else ok

    def gets_direct_down(k):
        if k == 0:
            return core == 0
        ok = t + steps[k] < shards
        return ok & (column_of + steps[k] < ROW) if k < CROSS else ok

    def sends_direct_up(k):
        return gets_direct_down(k)

    def sends_cross(k):
        return (t >= ROW) & (column_of < steps[k])

    def relays(k):
        return (t >= ROW) & (column_of + steps[k] >= ROW)

    joins = (core == 1) & (t >= 3)
    gives = (core == 0) & (t >= 2)
    relay = (t >= ROW) & (column_of >= ROW // 2)

    def cross_target(k):
        return lax.rem(t + ROW - steps[k], shards)

    def cross_back(k):
        return lax.rem(t + shards - ROW + steps[k], shards)

    def along(axis, step):
        if axis == 0:
            return lax.rem(t + 8 * (step % SIDE), shards)
        return place_x * 8 + lax.rem(place_y + step % SIDE, SIDE) * 2 + core

    def up_shard(k):
        return lax.rem(t + steps[k], shards)

    def down_shard(k):
        return lax.rem(t + shards - steps[k], shards)

    copy_in = pltpu.make_async_copy(w_in_hbm, w_in, w_sem.at[0])
    copy_out = pltpu.make_async_copy(w_out_hbm, w_out, w_sem.at[1])
    copy_in.start()
    copy_out.start()

    barrier = pltpu.get_barrier_semaphore()
    for k in range(LEVELS):
        pl.semaphore_signal(barrier, inc=1, device_id=(z, up_shard(k)), device_id_type=MESH)
        if 2 * steps[k] != shards:
            pl.semaphore_signal(barrier, inc=1, device_id=(z, down_shard(k)), device_id_type=MESH)
    peers = (along(1, 1), along(1, -1), partner)
    peers += (cross_target(1), cross_back(1))
    for peer in peers:
        pl.semaphore_signal(barrier, inc=1, device_id=(z, peer), device_id_type=MESH)
    for step in (1, sections - 1):
        pl.semaphore_signal(
            barrier, inc=1, device_id=(lax.rem(z + step, sections), t), device_id_type=MESH
        )

    def fwd_copy(m, k):
        return pltpu.make_async_remote_copy(
            src_ref=nall.at[m, 0],
            dst_ref=nall.at[m, k + 1],
            send_sem=fs.at[m, k],
            recv_sem=fr.at[m, k],
            device_id=(z, up_shard(k)),
            device_id_type=MESH,
        )

    def bwd_copy(m, c, k):
        return pltpu.make_async_remote_copy(
            src_ref=sbuf.at[m, c, k],
            dst_ref=rbuf.at[m, c, k],
            send_sem=bs.at[m, c, k],
            recv_sem=br.at[m, c, k],
            device_id=(z, down_shard(k)),
            device_id_type=MESH,
        )

    def cross_copy(m, c, k):
        return pltpu.make_async_remote_copy(
            src_ref=sbuf.at[m, c, k],
            dst_ref=qbuf.at[m, c, k],
            send_sem=qs.at[m, c, k],
            recv_sem=qr.at[m, c, k],
            device_id=(z, cross_target(k)),
            device_id_type=MESH,
        )

    def fwd_cross(m, k):
        return pltpu.make_async_remote_copy(
            src_ref=nall.at[m, CROSS + 1],
            dst_ref=nall.at[m, k + 1],
            send_sem=fq.at[m, k],
            recv_sem=fr.at[m, k],
            device_id=(z, cross_back(k)),
            device_id_type=MESH,
        )

    def join_copy(m, c):
        return pltpu.make_async_remote_copy(
            src_ref=sbuf.at[m, c, 0],
            dst_ref=pbuf.at[m, c],
            send_sem=bp.at[m, c],
            recv_sem=bq.at[m, c],
            device_id=(z, partner),
            device_id_type=MESH,
        )

    def fwd_pair(m):
        return pltpu.make_async_remote_copy(
            src_ref=nall.at[m, 2],
            dst_ref=nall.at[m, 1],
            send_sem=fp.at[m],
            recv_sem=fr.at[m, 0],
            device_id=(z, partner),
            device_id_type=MESH,
        )

    def z_copy(m, h):
        cols = pl.ds(h * COLS, COLS)
        return pltpu.make_async_remote_copy(
            src_ref=gsend.at[m, :, cols],
            dst_ref=inc.at[m, :, cols],
            send_sem=zs.at[m, h],
            recv_sem=zr.at[m, h],
            device_id=(lax.rem(z + sections - 1, sections), t),
            device_id_type=MESH,
        )

    def forward_send(m, levels):
        for k in levels:

            @pl.when(sends_direct_up(k))
            def _():
                fwd_copy(m, k).start()

    for m in range(MB):
        x = acts_ref[m].astype(F32)
        inverse = lax.rsqrt(jnp.mean(x * x, axis=-1, keepdims=True) + EPSILON)
        value = x * inverse
        normed[m] = value
        inv[m] = jnp.broadcast_to(inverse, (ROWS, 128))
        nall[m, 0] = value.astype(BF16)
        if m == 0:
            pl.semaphore_wait(barrier, 2 * LEVELS + 6)
        if m == 0:
            forward_send(0, (3, 4, 2, 1, 0))
        else:
            forward_send(1, (3,))

        for k in range(LEVELS):

            @pl.when(t < steps[k])
            def _():
                nall[m, k + 1] = jnp.zeros((ROWS, WIDTH), BF16)

    row_head = lax.broadcasted_iota(jnp.int32, (GROUP, GROUP), 0) // HEAD_DIM
    lane_head = lax.broadcasted_iota(jnp.int32, (GROUP, GROUP), 1) // HEAD_DIM
    bm[...] = jnp.where(row_head == lane_head, 1.0, 0.0).astype(BF16)
    key_pos = lax.broadcasted_iota(jnp.int32, (ROWS, GROUP), 0)
    query_pos = lax.broadcasted_iota(jnp.int32, (ROWS, GROUP), 1) % ROWS
    bias[0:ROWS, :] = jnp.where(key_pos <= query_pos, 0.0, FILL)
    for k in range(LEVELS):
        fill = jnp.where(off_ref[0, k] != 0, 0.0, FILL)
        bias[(k + 1) * ROWS : (k + 2) * ROWS, :] = jnp.full((ROWS, GROUP), fill, F32)

    @pl.when(z == sections - 1)
    def _():
        inc[...] = gtop_ref[...]

    def spread(rows):
        return jnp.concatenate([rows] * PER, 0) * bm[...]

    def gather_heads(stacked):
        lanes = lax.broadcasted_iota(jnp.int32, (ROWS, GROUP), 1) // HEAD_DIM
        total = jnp.where(lanes == 0, stacked[0:ROWS], 0.0)
        for head in range(1, PER):
            total = jnp.where(lanes == head, stacked[head * ROWS : (head + 1) * ROWS], total)
        return total

    def own_query(c, carry):
        cols = pl.ds(pl.multiple_of(c * GROUP, GROUP), GROUP)
        both = jnp.concatenate([nall[0, 0], nall[1, 0]], 0)
        result = dot(both, w_in[:, cols]).astype(BF16)
        for m in range(MB):
            qm[m, c] = spread(result[m * ROWS : (m + 1) * ROWS])
        return carry

    def own_pair(c, carry):
        cols = pl.ds(pl.multiple_of(c * GROUP, GROUP), GROUP)
        source = pl.ds(pl.multiple_of(WIDTH + c * GROUP, GROUP), GROUP)
        both = jnp.concatenate([nall[0, 0], nall[1, 0]], 0)
        result = dot(both, w_in[:, source]).astype(BF16)
        for m in range(MB):
            kv[m, 0:ROWS, cols] = result[m * ROWS : (m + 1) * ROWS]
        return carry

    def own_projections():
        lax.fori_loop(0, GROUPS, own_query, 0, unroll=2)
        lax.fori_loop(0, 2 * GROUPS, own_pair, 0, unroll=2)

    def forward_relay(m):
        @pl.when(t >= steps[CROSS])
        def _():
            fwd_copy(m, CROSS).wait_recv()

        for k in reversed(range(1, CROSS)):

            @pl.when(relays(k))
            def _():
                fwd_cross(m, k).start()

    def forward_join(m):
        @pl.when(t >= steps[1])
        def _():
            fwd_copy(m, 1).wait_recv()

        @pl.when(joins)
        def _():
            fwd_pair(m).start()

    def forward_keys(m):
        for k in (0, 2, 4):

            @pl.when(t >= steps[k])
            def _():
                fwd_copy(m, k).wait_recv()

        def far_pair(c, carry):
            cols = pl.ds(pl.multiple_of(c * GROUP, GROUP), GROUP)
            source = pl.ds(pl.multiple_of(WIDTH + c * GROUP, GROUP), GROUP)
            rows = nall[m, 1:BLOCKS].reshape(LEVELS * ROWS, WIDTH)
            kv[m, ROWS:KEYS, cols] = dot(rows, w_in[:, source]).astype(BF16)
            return carry

        lax.fori_loop(0, 2 * GROUPS, far_pair, 0, unroll=2)

    def forward_weights(m):
        def probability(g, carry):
            cols = pl.ds(pl.multiple_of(g * GROUP, GROUP), GROUP)
            scores = dot_nt(kv[m, :, cols], qm[m, g]) * SCALE + bias[...]
            highest = jnp.max(scores, axis=0, keepdims=True)
            weights = jnp.exp(scores - highest)
            result = weights / jnp.sum(weights, axis=0, keepdims=True)
            p32[m, g] = result
            p16[m, g] = result.astype(BF16)
            return carry

        lax.fori_loop(0, GROUPS, probability, 0, unroll=True)

    def attend(m):
        def group(g, carry):
            cols = pl.ds(pl.multiple_of(g * GROUP, GROUP), GROUP)
            values = pl.ds(pl.multiple_of(WIDTH + g * GROUP, GROUP), GROUP)
            stacked = dot_tn(p16[m, g], kv[m, :, values])
            att[m * ROWS : (m + 1) * ROWS, cols] = gather_heads(stacked).astype(BF16)
            return carry

        lax.fori_loop(0, GROUPS, group, 0)

    def wait_incoming(m, h):
        z_copy(m, h).wait_recv()

    def stage_upstream(m):
        waits = (z < sections - 1) if m == 0 else (z < sections - 1) & (z > 0)

        @pl.when(waits)
        def _():
            wait_incoming(m, 0)

        def first(g, carry):
            cols = pl.ds(pl.multiple_of(g * GROUP, GROUP), GROUP)
            up32[:, cols] = dot_nt(inc[m, :, 0:COLS], w_out[cols, 0:COLS])
            return carry

        lax.fori_loop(0, GROUPS, first, 0, unroll=True)

        @pl.when(waits)
        def _():
            wait_incoming(m, 1)

        def second(g, carry):
            cols = pl.ds(pl.multiple_of(g * GROUP, GROUP), GROUP)
            rest = dot_nt(inc[m, :, COLS : 2 * COLS], w_out[cols, COLS : 2 * COLS])
            up16[:, cols] = (up32[:, cols] + rest).astype(BF16)
            return carry

        lax.fori_loop(0, GROUPS, second, 0, unroll=True)

    def stage_parts(m):
        def group(g, carry):
            cols = pl.ds(pl.multiple_of(g * GROUP, GROUP), GROUP)
            values = pl.ds(pl.multiple_of(WIDTH + g * GROUP, GROUP), GROUP)
            up_heads = spread(up16[:, cols])
            prob_grad = dot_nt(kv[m, :, values], up_heads)
            part[m, :, values] = dot(p16[m, g], up_heads).astype(BF16)
            prob = p32[m, g]
            delta = jnp.sum(prob * prob_grad, axis=0, keepdims=True)
            score_grad = (prob * (prob_grad - delta)).astype(BF16)
            sg[g] = score_grad
            part[m, :, cols] = (dot(score_grad, qm[m, g]) * SCALE).astype(BF16)
            return carry

        lax.fori_loop(0, GROUPS, group, 0, unroll=True)

    def stage_project(m):
        def project(c, carry):
            cols = pl.ds(pl.multiple_of(c * CHUNK, CHUNK), CHUNK)
            result = dot_nt(part[m, ROWS:KEYS, :], w_in[cols, WIDTH : 3 * WIDTH])
            for k in (2, 0, 1, 4, 3):
                term = result[k * ROWS : (k + 1) * ROWS]
                sbuf[m, c, k] = term.astype(BF16)
                send = sends_direct_down(k)
                if k == 0:

                    @pl.when(gives)
                    def _():
                        join_copy(m, c).start()

                if k == 1:
                    direct1[c] = term
                    send = send & jnp.logical_not(joins)

                    @pl.when(sends_cross(k) & jnp.logical_not(joins))
                    def _():
                        cross_copy(m, c, k).start()

                if k == 2:

                    @pl.when(sends_cross(k))
                    def _():
                        cross_copy(m, c, k).start()

                if k == CROSS:
                    direct[c] = term
                    send = send & jnp.logical_not(relay)

                @pl.when(send)
                def _():
                    bwd_copy(m, c, k).start()

            @pl.when(joins & (c > 0))
            def _():
                join_send(m, c - 1)

            return carry

        def join_send(m, c):
            join_copy(m, c).wait_recv()
            sbuf[m, c, 1] = (direct1[c] + pbuf[m, c].astype(F32)).astype(BF16)

            @pl.when(sends_direct_down(1))
            def _():
                bwd_copy(m, c, 1).start()

            @pl.when(sends_cross(1))
            def _():
                cross_copy(m, c, 1).start()

        lax.fori_loop(0, CHUNKS, project, 0)

        @pl.when(joins)
        def _():
            join_send(m, CHUNKS - 1)

    def stage_relay(m):
        @pl.when(relay)
        def _():
            for c in range(CHUNKS):
                for k in reversed(range(1, CROSS)):

                    @pl.when(relays(k))
                    def _():
                        cross_copy(m, c, k).wait_recv()
                        direct[c] += qbuf[m, c, k].astype(F32)

                sbuf[m, c, CROSS] = direct[c].astype(BF16)
                bwd_copy(m, c, CROSS).start()

    def stage_query(m):
        def group(g, carry):
            cols = pl.ds(pl.multiple_of(g * GROUP, GROUP), GROUP)
            stacked = dot_tn(sg[g], kv[m, :, cols])
            dq[m * ROWS : (m + 1) * ROWS, cols] = (gather_heads(stacked) * SCALE).astype(BF16)
            return carry

        lax.fori_loop(0, GROUPS, group, 0, unroll=True)

    def stage_own(m):
        def own(c, carry):
            cols = pl.ds(pl.multiple_of(c * CHUNK, CHUNK), CHUNK)
            ng[m, :, cols] = dot_nt(
                dq[m * ROWS : (m + 1) * ROWS, :], w_in[cols, 0:WIDTH]
            ) + dot_nt(part[m, 0:ROWS, :], w_in[cols, WIDTH : 3 * WIDTH])
            return carry

        lax.fori_loop(0, CHUNKS, own, 0)

    def backward_finish(m):
        for c in range(CHUNKS):
            for k in range(LEVELS):

                @pl.when(gets_direct_down(k))
                def _():
                    bwd_copy(m, c, k).wait_recv()
                    cols = slice(c * CHUNK, (c + 1) * CHUNK)
                    ng[m, :, cols] += rbuf[m, c, k].astype(F32)

        grad = ng[m]
        value = normed[m]
        inner = jnp.mean(grad * value, axis=-1, keepdims=True)
        for h in range(2):
            cols = slice(h * COLS, (h + 1) * COLS)
            change = inv[m, :, 0:1] * (grad[:, cols] - value[:, cols] * inner)
            result = (inc[m, :, cols].astype(F32) + change).astype(BF16)
            gsend[m, :, cols] = result

            @pl.when(z > 0)
            def _():
                z_copy(m, h).start()

            dacts_ref[m, :, cols] = result

    def remote(src, dst, send_sem, recv_sem, peer):
        return pltpu.make_async_remote_copy(
            src_ref=src,
            dst_ref=dst,
            send_sem=send_sem,
            recv_sem=recv_sem,
            device_id=(z, peer),
            device_id_type=MESH,
        )

    def pair_copy(i):
        return remote(psend.at[i], precv.at[i], ps.at[i], pr.at[i], partner)

    def ring_copy(stage, i, side):
        send, recv, ss, rs = ring_refs[stage]
        axis = (i + stage // 2) % 2
        return remote(
            send.at[i, side],
            recv.at[i, side],
            ss.at[i, side],
            rs.at[i, side],
            along(axis, 1 if side == 0 else -1),
        )

    ring_refs = (
        (send1, recv1, s1, r1),
        (send2, recv2, s2, r2),
        (send3, recv3, s3, r3),
        (send4, recv4, s4, r4),
    )

    def transpose_rows():
        def block(r, carry):
            rows = pl.ds(pl.multiple_of(r * CHUNK, CHUNK), CHUNK)
            owns = []
            for m in range(MB):
                tokens = nall[m, :, :, rows].reshape(KEYS, CHUNK)
                turned = tokens.T.reshape(SIDE, 2, SLICE, KEYS)
                for parity in range(2):
                    n_t[parity, r, :, :, m * KEYS : (m + 1) * KEYS] = turned[:, parity]
                owns.append(nall[m, 0, :, rows])
            turned = jnp.concatenate(owns, 0).T.reshape(SIDE, 2, SLICE, MB * ROWS)
            turned_att = att[:, rows].T.reshape(SIDE, 2, SLICE, MB * ROWS)
            for parity in range(2):
                own_t[parity, r] = turned[:, parity]
                att_t[parity, r] = turned_att[:, parity]
            return carry

        lax.fori_loop(0, SIDE, block, 0)

    def operands(i):
        if i < 2:
            low = i * COLS
            right = inc[:, :, low : low + COLS].reshape(MB * ROWS, COLS)
            return att_t, right, 3 * WIDTH + low
        if i < 4:
            low = (i - 2) * COLS
            return own_t, dq[:, low : low + COLS], low
        low = (i - 4) * COLS
        right = part[:, :, low : low + COLS].reshape(MB * KEYS, COLS)
        return n_t, right, WIDTH + low

    def weight_part(i):
        left, right, _ = operands(i)
        depth = right.shape[0]
        shape = (SIDE, SIDE, SLICE, COLS)
        away = left[1 - core].reshape(WIDTH // 2, depth)
        psend[i] = dot(away, right).astype(BF16).reshape(shape)
        pair_copy(i).start()
        here = left[core].reshape(WIDTH // 2, depth)
        total[i] = dot(here, right).reshape(shape)

    def pick(i, step):
        axis = i % 2
        where = lax.rem((place_x if axis == 0 else place_y) + step % SIDE, SIDE)
        return total[i, where] if axis == 0 else total[i, :, where]

    def pick_row(i, step):
        axis = (i + 1) % 2
        return column[i, lax.rem((place_x if axis == 0 else place_y) + step % SIDE, SIDE)]

    def ring_one(i):
        pair_copy(i).wait_recv()
        total[i] += precv[i].astype(F32)
        far = pick(i, 2).astype(BF16)
        send1[i, 0] = far[:, :, :HALF]
        send1[i, 1] = far[:, :, HALF:]
        for side in range(2):
            ring_copy(0, i, side).start()

    def ring_two(i):
        for side in range(2):
            ring_copy(0, i, side).wait_recv()
        right, left = pick(i, 1), pick(i, -1)
        send2[i, 0, :, :, :HALF] = (right[:, :, :HALF] + recv1[i, 0].astype(F32)).astype(BF16)
        send2[i, 0, :, :, HALF:] = right[:, :, HALF:].astype(BF16)
        ring_copy(1, i, 0).start()
        send2[i, 1, :, :, :HALF] = left[:, :, :HALF].astype(BF16)
        send2[i, 1, :, :, HALF:] = (left[:, :, HALF:] + recv1[i, 1].astype(F32)).astype(BF16)
        ring_copy(1, i, 1).start()

    def ring_three(i):
        for side in range(2):
            ring_copy(1, i, side).wait_recv()
        column[i] = pick(i, 0) + recv2[i, 0].astype(F32) + recv2[i, 1].astype(F32)
        far = pick_row(i, 2).astype(BF16)
        send3[i, 0] = far[:, :HALF]
        send3[i, 1] = far[:, HALF:]
        for side in range(2):
            ring_copy(2, i, side).start()

    def ring_four(i):
        for side in range(2):
            ring_copy(2, i, side).wait_recv()
        right, left = pick_row(i, 1), pick_row(i, -1)
        send4[i, 0, :, :HALF] = (right[:, :HALF] + recv3[i, 0].astype(F32)).astype(BF16)
        send4[i, 0, :, HALF:] = right[:, HALF:].astype(BF16)
        ring_copy(3, i, 0).start()
        send4[i, 1, :, :HALF] = left[:, :HALF].astype(BF16)
        send4[i, 1, :, HALF:] = (left[:, HALF:] + recv3[i, 1].astype(F32)).astype(BF16)
        ring_copy(3, i, 1).start()

    def ring_last(i):
        for side in range(2):
            ring_copy(3, i, side).wait_recv()
        result = pick_row(i, 0) + recv4[i, 0].astype(F32) + recv4[i, 1].astype(F32)
        low = (3 * WIDTH if i < 2 else -2 * COLS if i < 4 else WIDTH - 4 * COLS) + i * COLS
        if low < 3 * WIDTH:
            dwin_ref[:, low : low + COLS] = result
        else:
            dwout_ref[:, low - 3 * WIDTH : low - 3 * WIDTH + COLS] = result

    def rest_forward():
        attend(0)
        attend(1)
        transpose_rows()

    last = z == sections - 1
    forward_relay(0)
    forward_send(1, (4, 2, 1, 0))
    copy_in.wait()
    own_projections()
    forward_join(0)
    forward_relay(1)
    forward_keys(0)
    forward_weights(0)
    forward_join(1)
    copy_out.wait()

    @pl.when(z < sections - 1)
    def _():
        forward_keys(1)
        forward_weights(1)
        rest_forward()

    stage_upstream(0)
    stage_parts(0)
    stage_project(0)

    @pl.when(last)
    def _():
        forward_keys(1)

    stage_query(0)
    stage_relay(0)

    @pl.when(last)
    def _():
        forward_weights(1)

    stage_own(0)
    backward_finish(0)

    @pl.when(z == 0)
    def _():
        wait_incoming(1, 0)
        wait_incoming(1, 1)
        weight_part(0)
        weight_part(1)

    stage_upstream(1)

    @pl.when(z == 0)
    def _():
        ring_one(0)
        ring_one(1)

    stage_parts(1)

    @pl.when(z > 0)
    def _():
        stage_project(1)

    stage_query(1)

    @pl.when(z > 0)
    def _():
        stage_relay(1)
        stage_own(1)
        backward_finish(1)

        @pl.when(last)
        def _():
            rest_forward()

        weight_part(0)
        weight_part(1)
        ring_one(0)
        ring_one(1)

    for i in range(2, PARTS):
        weight_part(i)
        if i > 2:
            ring_one(i - 1)
            ring_two(i - 3)
    ring_one(PARTS - 1)
    ring_two(PARTS - 3)

    @pl.when(z == 0)
    def _():
        stage_project(1)
        stage_own(1)

    ring_three(0)
    ring_two(PARTS - 2)
    ring_three(1)
    ring_two(PARTS - 1)

    @pl.when(z == 0)
    def _():
        stage_relay(1)

    for i in range(2, PARTS + 3):
        if i < PARTS:
            ring_three(i)
        if i < PARTS + 2:
            ring_four(i - 2)
        if 4 <= i:
            ring_last(i - 4)
        if i == PARTS - 1:

            @pl.when(z == 0)
            def _():
                backward_finish(1)

    ring_last(PARTS - 1)

    for i in range(PARTS):
        pair_copy(i).wait_send()
        for stage in range(4):
            for side in range(2):
                ring_copy(stage, i, side).wait_send()

    for m in range(MB):
        for k in range(LEVELS):

            @pl.when(sends_direct_up(k))
            def _():
                fwd_copy(m, k).wait_send()

            @pl.when(sends_direct_down(k))
            def _():
                for c in range(CHUNKS):
                    bwd_copy(m, c, k).wait_send()

            if 0 < k < CROSS:

                @pl.when(relays(k))
                def _():
                    fwd_cross(m, k).wait_send()

                @pl.when(sends_cross(k))
                def _():
                    for c in range(CHUNKS):
                        cross_copy(m, c, k).wait_send()

        @pl.when(joins)
        def _():
            fwd_pair(m).wait_send()

        @pl.when(gives)
        def _():
            for c in range(CHUNKS):
                join_copy(m, c).wait_send()

        @pl.when(z > 0)
        def _():
            for h in range(2):
                z_copy(m, h).wait_send()


def result_kernel(a, b, c, a_out, b_out, c_out, a_buf, b_buf, c_buf, sem_in, sem_out):
    sources, buffers, targets = (a, b, c), (a_buf, b_buf, c_buf), (a_out, b_out, c_out)
    fetch = [pltpu.make_async_copy(sources[i], buffers[i], sem_in.at[i]) for i in range(3)]
    store = [pltpu.make_async_copy(buffers[i], targets[i], sem_out.at[i]) for i in range(3)]
    for copy in fetch:
        copy.start()
    for i in range(3):
        fetch[i].wait()
        store[i].start()
    for copy in store:
        copy.wait()


def per_device(acts, grad_top, w_in, w_out, offsets):
    sections = lax.axis_size("section")
    shards = lax.axis_size("tm")
    vmem = pl.BlockSpec(memory_space=pltpu.VMEM)
    d_acts, d_in, d_out = pl.pallas_call(
        functools.partial(layer_kernel, sections, shards),
        out_shape=(
            jax.ShapeDtypeStruct((MB, ROWS, WIDTH), BF16),
            jax.ShapeDtypeStruct((SLICE, 3 * WIDTH), F32),
            jax.ShapeDtypeStruct((SLICE, WIDTH), F32),
        ),
        in_specs=[
            vmem,
            vmem,
            pl.BlockSpec(memory_space=pl.ANY),
            pl.BlockSpec(memory_space=pl.ANY),
            pl.BlockSpec(memory_space=pltpu.SMEM),
        ],
        out_specs=(vmem, vmem, vmem),
        scratch_shapes=[
            pltpu.VMEM((WIDTH, 3 * WIDTH), BF16),
            pltpu.VMEM((WIDTH, WIDTH), BF16),
            pltpu.VMEM((MB, BLOCKS, ROWS, WIDTH), BF16),
            pltpu.VMEM((MB, ROWS, WIDTH), F32),
            pltpu.VMEM((MB, ROWS, 128), F32),
            pltpu.VMEM((MB, GROUPS, GROUP, GROUP), BF16),
            pltpu.VMEM((MB, KEYS, 2 * WIDTH), BF16),
            pltpu.VMEM((MB, GROUPS, KEYS, GROUP), F32),
            pltpu.VMEM((MB, GROUPS, KEYS, GROUP), BF16),
            pltpu.VMEM((GROUP, GROUP), BF16),
            pltpu.VMEM((KEYS, GROUP), F32),
            pltpu.VMEM((MB, ROWS, WIDTH), BF16),
            pltpu.VMEM((MB * ROWS, WIDTH), BF16),
            pltpu.VMEM((MB, KEYS, 2 * WIDTH), BF16),
            pltpu.VMEM((MB * ROWS, WIDTH), BF16),
            pltpu.VMEM((MB, ROWS, WIDTH), F32),
            pltpu.VMEM((MB, ROWS, WIDTH), BF16),
            pltpu.VMEM((MB, CHUNKS, LEVELS, ROWS, CHUNK), BF16),
            pltpu.VMEM((MB, CHUNKS, LEVELS, ROWS, CHUNK), BF16),
            pltpu.SemaphoreType.DMA((2,)),
            pltpu.SemaphoreType.DMA((MB, LEVELS)),
            pltpu.SemaphoreType.DMA((MB, LEVELS)),
            pltpu.SemaphoreType.DMA((MB, CHUNKS, LEVELS)),
            pltpu.SemaphoreType.DMA((MB, CHUNKS, LEVELS)),
            pltpu.SemaphoreType.DMA((MB, 2)),
            pltpu.SemaphoreType.DMA((MB, 2)),
            pltpu.VMEM((2, SIDE, SIDE, SLICE, MB * KEYS), BF16),
            pltpu.VMEM((2, SIDE, SIDE, SLICE, MB * ROWS), BF16),
            pltpu.VMEM((2, SIDE, SIDE, SLICE, MB * ROWS), BF16),
            pltpu.VMEM((PARTS, SIDE, SIDE, SLICE, COLS), BF16),
            pltpu.VMEM((PARTS, SIDE, SIDE, SLICE, COLS), BF16),
            pltpu.VMEM((PARTS, SIDE, SIDE, SLICE, COLS), F32),
            pltpu.VMEM((PARTS, 2, SIDE, SLICE, HALF), BF16),
            pltpu.VMEM((PARTS, 2, SIDE, SLICE, HALF), BF16),
            pltpu.VMEM((PARTS, 2, SIDE, SLICE, COLS), BF16),
            pltpu.VMEM((PARTS, 2, SIDE, SLICE, COLS), BF16),
            pltpu.VMEM((PARTS, SIDE, SLICE, COLS), F32),
            pltpu.VMEM((PARTS, 2, SLICE, HALF), BF16),
            pltpu.VMEM((PARTS, 2, SLICE, HALF), BF16),
            pltpu.VMEM((PARTS, 2, SLICE, COLS), BF16),
            pltpu.VMEM((PARTS, 2, SLICE, COLS), BF16),
            pltpu.SemaphoreType.DMA((PARTS,)),
            pltpu.SemaphoreType.DMA((PARTS,)),
        ]
        + [pltpu.SemaphoreType.DMA((PARTS, 2))] * 8
        + [
            pltpu.VMEM((GROUPS, KEYS, GROUP), BF16),
            pltpu.VMEM((ROWS, WIDTH), F32),
            pltpu.VMEM((ROWS, WIDTH), BF16),
            pltpu.VMEM((MB, CHUNKS, CROSS, ROWS, CHUNK), BF16),
            pltpu.VMEM((CHUNKS, ROWS, CHUNK), F32),
            pltpu.SemaphoreType.DMA((MB, CHUNKS, CROSS)),
            pltpu.SemaphoreType.DMA((MB, CHUNKS, CROSS)),
            pltpu.SemaphoreType.DMA((MB, CROSS)),
            pltpu.VMEM((CHUNKS, ROWS, CHUNK), F32),
            pltpu.VMEM((MB, CHUNKS, ROWS, CHUNK), BF16),
            pltpu.SemaphoreType.DMA((MB, CHUNKS)),
            pltpu.SemaphoreType.DMA((MB, CHUNKS)),
            pltpu.SemaphoreType.DMA((MB,)),
        ],
        compiler_params=pltpu.CompilerParams(
            collective_id=0, has_side_effects=True, vmem_limit_bytes=63 * 1024 * 1024
        ),
        name="layer_kernel",
    )(acts[0], grad_top, w_in[0], w_out[0], offsets)
    results = (d_acts, d_in, d_out)
    anywhere = pl.BlockSpec(memory_space=pl.ANY)
    d_acts, d_in, d_out = pl.pallas_call(
        result_kernel,
        out_shape=tuple(jax.ShapeDtypeStruct(r.shape, r.dtype) for r in results),
        in_specs=[anywhere] * 3,
        out_specs=(anywhere,) * 3,
        scratch_shapes=[pltpu.VMEM(r.shape, r.dtype) for r in results]
        + [pltpu.SemaphoreType.DMA((3,)), pltpu.SemaphoreType.DMA((3,))],
        name="result_kernel",
    )(*results)
    return (d_acts[None], d_in[None], d_out[None])


def solution(mesh):
    placed = (
        P("section", None, "tm", None),
        P(None, "tm", None),
        P("section", None, None),
        P("section", None, None),
        P("tm", None),
    )
    return jax.shard_map(
        per_device,
        mesh=mesh,
        in_specs=placed,
        out_specs=(
            P("section", None, "tm", None),
            P("section", "tm", None),
            P("section", "tm", None),
        ),
        check_vma=False,
    )
```

```python
import functools

import jax
import jax.numpy as jnp
from jax import lax
from jax.experimental import pallas as pl
from jax.experimental.pallas import tpu as pltpu
from jax.sharding import PartitionSpec as P

HEAD_DIM = 64
SCALE = HEAD_DIM ** (-0.5)
EPSILON = 1e-06
FILL = -1e30
MESH = pl.DeviceIdType.MESH

MB = 2
ROWS = 64
WIDTH = 1024
LEVELS = 5
BLOCKS = LEVELS + 1
KEYS = BLOCKS * ROWS
GROUP = 256
GROUPS = WIDTH // GROUP
CHUNK = 256
CHUNKS = WIDTH // CHUNK
PER = GROUP // HEAD_DIM
SIDE = 4
ROW = 8
CROSS = 3
SLICE = 32
PARTS = 8
COLS = 512
HALF = COLS // 2

BF16 = jnp.bfloat16
F32 = jnp.float32


def dot(a, b):
    return lax.dot_general(a, b, (((1,), (0,)), ((), ())), preferred_element_type=F32)


def dot_nt(a, b):
    return lax.dot_general(a, b, (((1,), (1,)), ((), ())), preferred_element_type=F32)


def dot_tn(a, b):
    return lax.dot_general(a, b, (((0,), (0,)), ((), ())), preferred_element_type=F32)


def layer_kernel(
    sections,
    shards,
    acts_ref,
    gtop_ref,
    w_in_hbm,
    w_out_hbm,
    off_ref,
    dacts_ref,
    dwin_ref,
    dwout_ref,
    w_in,
    w_out,
    nall,
    normed,
    inv,
    qm,
    kv,
    p32,
    p16,
    bm,
    bias,
    inc,
    dq,
    part,
    att,
    ng,
    gsend,
    sbuf,
    rbuf,
    w_sem,
    fs,
    fr,
    bs,
    br,
    zs,
    zr,
    n_t,
    own_t,
    att_t,
    psend,
    precv,
    total,
    send1,
    recv1,
    send2,
    recv2,
    column,
    send3,
    recv3,
    send4,
    recv4,
    ps,
    pr,
    s1,
    r1,
    s2,
    r2,
    s3,
    r3,
    s4,
    r4,
    sg,
    up32,
    up16,
    qbuf,
    direct,
    qs,
    qr,
    fq,
    direct1,
    pbuf,
    bp,
    bq,
    fp,
):
    z = lax.axis_index("section")
    t = lax.axis_index("tm")
    steps = [2**level for level in range(LEVELS)]
    place_x = t // 8
    place_y = lax.rem(t // 2, SIDE)
    core = lax.rem(t, 2)
    partner = t + 1 - 2 * core
    column_of = lax.rem(t, ROW)

    def sends_direct_down(k):
        if k == 0:
            return core == 1
        ok = t >= steps[k]
        return ok & (column_of >= steps[k]) if k < CROSS else ok

    def gets_direct_down(k):
        if k == 0:
            return core == 0
        ok = t + steps[k] < shards
        return ok & (column_of + steps[k] < ROW) if k < CROSS else ok

    def sends_direct_up(k):
        return gets_direct_down(k)

    def sends_cross(k):
        return (t >= ROW) & (column_of < steps[k])

    def relays(k):
        return (t >= ROW) & (column_of + steps[k] >= ROW)

    joins = (core == 1) & (t >= 3)
    gives = (core == 0) & (t >= 2)
    relay = (t >= ROW) & (column_of >= ROW // 2)

    def cross_target(k):
        return lax.rem(t + ROW - steps[k], shards)

    def cross_back(k):
        return lax.rem(t + shards - ROW + steps[k], shards)

    def along(axis, step):
        if axis == 0:
            return lax.rem(t + 8 * (step % SIDE), shards)
        return place_x * 8 + lax.rem(place_y + step % SIDE, SIDE) * 2 + core

    def up_shard(k):
        return lax.rem(t + steps[k], shards)

    def down_shard(k):
        return lax.rem(t + shards - steps[k], shards)

    copy_in = pltpu.make_async_copy(w_in_hbm, w_in, w_sem.at[0])
    copy_out = pltpu.make_async_copy(w_out_hbm, w_out, w_sem.at[1])
    copy_in.start()
    copy_out.start()

    barrier = pltpu.get_barrier_semaphore()
    for k in range(LEVELS):
        pl.semaphore_signal(barrier, inc=1, device_id=(z, up_shard(k)), device_id_type=MESH)
        if 2 * steps[k] != shards:
            pl.semaphore_signal(barrier, inc=1, device_id=(z, down_shard(k)), device_id_type=MESH)
    peers = (along(1, 1), along(1, -1), partner)
    peers += (cross_target(1), cross_back(1))
    for peer in peers:
        pl.semaphore_signal(barrier, inc=1, device_id=(z, peer), device_id_type=MESH)
    for step in (1, sections - 1):
        pl.semaphore_signal(
            barrier, inc=1, device_id=(lax.rem(z + step, sections), t), device_id_type=MESH
        )

    def fwd_copy(m, k):
        return pltpu.make_async_remote_copy(
            src_ref=nall.at[m, 0],
            dst_ref=nall.at[m, k + 1],
            send_sem=fs.at[m, k],
            recv_sem=fr.at[m, k],
            device_id=(z, up_shard(k)),
            device_id_type=MESH,
        )

    def bwd_copy(m, c, k):
        return pltpu.make_async_remote_copy(
            src_ref=sbuf.at[m, c, k],
            dst_ref=rbuf.at[m, c, k],
            send_sem=bs.at[m, c, k],
            recv_sem=br.at[m, c, k],
            device_id=(z, down_shard(k)),
            device_id_type=MESH,
        )

    def cross_copy(m, c, k):
        return pltpu.make_async_remote_copy(
            src_ref=sbuf.at[m, c, k],
            dst_ref=qbuf.at[m, c, k],
            send_sem=qs.at[m, c, k],
            recv_sem=qr.at[m, c, k],
            device_id=(z, cross_target(k)),
            device_id_type=MESH,
        )

    def fwd_cross(m, k):
        return pltpu.make_async_remote_copy(
            src_ref=nall.at[m, CROSS + 1],
            dst_ref=nall.at[m, k + 1],
            send_sem=fq.at[m, k],
            recv_sem=fr.at[m, k],
            device_id=(z, cross_back(k)),
            device_id_type=MESH,
        )

    def join_copy(m, c):
        return pltpu.make_async_remote_copy(
            src_ref=sbuf.at[m, c, 0],
            dst_ref=pbuf.at[m, c],
            send_sem=bp.at[m, c],
            recv_sem=bq.at[m, c],
            device_id=(z, partner),
            device_id_type=MESH,
        )

    def fwd_pair(m):
        return pltpu.make_async_remote_copy(
            src_ref=nall.at[m, 2],
            dst_ref=nall.at[m, 1],
            send_sem=fp.at[m],
            recv_sem=fr.at[m, 0],
            device_id=(z, partner),
            device_id_type=MESH,
        )

    def z_copy(m, h):
        cols = pl.ds(h * COLS, COLS)
        return pltpu.make_async_remote_copy(
            src_ref=gsend.at[m, :, cols],
            dst_ref=inc.at[m, :, cols],
            send_sem=zs.at[m, h],
            recv_sem=zr.at[m, h],
            device_id=(lax.rem(z + sections - 1, sections), t),
            device_id_type=MESH,
        )

    def forward_send(m, levels):
        for k in levels:

            @pl.when(sends_direct_up(k))
            def _():
                fwd_copy(m, k).start()

    for m in range(MB):
        x = acts_ref[m].astype(F32)
        inverse = lax.rsqrt(jnp.mean(x * x, axis=-1, keepdims=True) + EPSILON)
        value = x * inverse
        normed[m] = value
        inv[m] = jnp.broadcast_to(inverse, (ROWS, 128))
        nall[m, 0] = value.astype(BF16)
        if m == 0:
            pl.semaphore_wait(barrier, 2 * LEVELS + 6)
        if m == 0:
            forward_send(0, (3, 4, 2, 1, 0))
        else:
            forward_send(1, (3,))

        for k in range(LEVELS):

            @pl.when(t < steps[k])
            def _():
                nall[m, k + 1] = jnp.zeros((ROWS, WIDTH), BF16)

    row_head = lax.broadcasted_iota(jnp.int32, (GROUP, GROUP), 0) // HEAD_DIM
    lane_head = lax.broadcasted_iota(jnp.int32, (GROUP, GROUP), 1) // HEAD_DIM
    bm[...] = jnp.where(row_head == lane_head, 1.0, 0.0).astype(BF16)
    key_pos = lax.broadcasted_iota(jnp.int32, (ROWS, GROUP), 0)
    query_pos = lax.broadcasted_iota(jnp.int32, (ROWS, GROUP), 1) % ROWS
    bias[0:ROWS, :] = jnp.where(key_pos <= query_pos, 0.0, FILL)
    for k in range(LEVELS):
        fill = jnp.where(off_ref[0, k] != 0, 0.0, FILL)
        bias[(k + 1) * ROWS : (k + 2) * ROWS, :] = jnp.full((ROWS, GROUP), fill, F32)

    @pl.when(z == sections - 1)
    def _():
        inc[...] = gtop_ref[...]

    for k in range(LEVELS):

        @pl.when(jnp.logical_not(gets_direct_down(k)))
        def _():
            rbuf[:, :, k] = jnp.zeros((MB, CHUNKS, ROWS, CHUNK), BF16)

    def spread(rows):
        return jnp.concatenate([rows] * PER, 0) * bm[...]

    def gather_heads(stacked):
        lanes = lax.broadcasted_iota(jnp.int32, (ROWS, GROUP), 1) // HEAD_DIM
        total = jnp.where(lanes == 0, stacked[0:ROWS], 0.0)
        for head in range(1, PER):
            total = jnp.where(lanes == head, stacked[head * ROWS : (head + 1) * ROWS], total)
        return total

    def own_query(c, carry):
        cols = pl.ds(pl.multiple_of(c * GROUP, GROUP), GROUP)
        both = jnp.concatenate([nall[0, 0], nall[1, 0]], 0)
        result = dot(both, w_in[:, cols]).astype(BF16)
        for m in range(MB):
            qm[m, c] = spread(result[m * ROWS : (m + 1) * ROWS])
        return carry

    def own_pair(c, carry):
        cols = pl.ds(pl.multiple_of(c * GROUP, GROUP), GROUP)
        source = pl.ds(pl.multiple_of(WIDTH + c * GROUP, GROUP), GROUP)
        both = jnp.concatenate([nall[0, 0], nall[1, 0]], 0)
        result = dot(both, w_in[:, source]).astype(BF16)
        for m in range(MB):
            kv[m, 0:ROWS, cols] = result[m * ROWS : (m + 1) * ROWS]
        return carry

    def own_projections():
        lax.fori_loop(0, GROUPS, own_query, 0, unroll=2)
        lax.fori_loop(0, 2 * GROUPS, own_pair, 0, unroll=2)

    def forward_relay(m):
        @pl.when(t >= steps[CROSS])
        def _():
            fwd_copy(m, CROSS).wait_recv()

        for k in reversed(range(1, CROSS)):

            @pl.when(relays(k))
            def _():
                fwd_cross(m, k).start()

    def forward_join(m):
        @pl.when(t >= steps[1])
        def _():
            fwd_copy(m, 1).wait_recv()

        @pl.when(joins)
        def _():
            fwd_pair(m).start()

    def forward_keys(m):
        for k in (0, 2, 4):

            @pl.when(t >= steps[k])
            def _():
                fwd_copy(m, k).wait_recv()

        def far_pair(c, carry):
            cols = pl.ds(pl.multiple_of(c * GROUP, GROUP), GROUP)
            source = pl.ds(pl.multiple_of(WIDTH + c * GROUP, GROUP), GROUP)
            rows = nall[m, 1:BLOCKS].reshape(LEVELS * ROWS, WIDTH)
            kv[m, ROWS:KEYS, cols] = dot(rows, w_in[:, source]).astype(BF16)
            return carry

        lax.fori_loop(0, 2 * GROUPS, far_pair, 0, unroll=2)

    def forward_weights(m):
        def probability(g, carry):
            cols = pl.ds(pl.multiple_of(g * GROUP, GROUP), GROUP)
            scores = dot_nt(kv[m, :, cols], qm[m, g]) * SCALE + bias[...]
            highest = jnp.max(scores, axis=0, keepdims=True)
            weights = jnp.exp(scores - highest)
            result = weights / jnp.sum(weights, axis=0, keepdims=True)
            p32[m, g] = result
            p16[m, g] = result.astype(BF16)
            return carry

        lax.fori_loop(0, GROUPS, probability, 0, unroll=True)

    def attend(m):
        def group(g, carry):
            cols = pl.ds(pl.multiple_of(g * GROUP, GROUP), GROUP)
            values = pl.ds(pl.multiple_of(WIDTH + g * GROUP, GROUP), GROUP)
            stacked = dot_tn(p16[m, g], kv[m, :, values])
            att[m * ROWS : (m + 1) * ROWS, cols] = gather_heads(stacked).astype(BF16)
            return carry

        lax.fori_loop(0, GROUPS, group, 0)

    def wait_incoming(m, h):
        z_copy(m, h).wait_recv()

    def stage_upstream(m):
        waits = (z < sections - 1) if m == 0 else (z < sections - 1) & (z > 0)

        @pl.when(waits)
        def _():
            wait_incoming(m, 0)

        def first(g, carry):
            cols = pl.ds(pl.multiple_of(g * GROUP, GROUP), GROUP)
            up32[:, cols] = dot_nt(inc[m, :, 0:COLS], w_out[cols, 0:COLS])
            return carry

        lax.fori_loop(0, GROUPS, first, 0, unroll=True)

        @pl.when(waits)
        def _():
            wait_incoming(m, 1)

        def second(g, carry):
            cols = pl.ds(pl.multiple_of(g * GROUP, GROUP), GROUP)
            rest = dot_nt(inc[m, :, COLS : 2 * COLS], w_out[cols, COLS : 2 * COLS])
            up16[:, cols] = (up32[:, cols] + rest).astype(BF16)
            return carry

        lax.fori_loop(0, GROUPS, second, 0, unroll=True)

    def stage_parts(m):
        def group(g, carry):
            cols = pl.ds(pl.multiple_of(g * GROUP, GROUP), GROUP)
            values = pl.ds(pl.multiple_of(WIDTH + g * GROUP, GROUP), GROUP)
            up_heads = spread(up16[:, cols])
            prob_grad = dot_nt(kv[m, :, values], up_heads)
            part[m, :, values] = dot(p16[m, g], up_heads).astype(BF16)
            prob = p32[m, g]
            delta = jnp.sum(prob * prob_grad, axis=0, keepdims=True)
            score_grad = (prob * (prob_grad - delta)).astype(BF16)
            sg[g] = score_grad
            part[m, :, cols] = (dot(score_grad, qm[m, g]) * SCALE).astype(BF16)
            return carry

        lax.fori_loop(0, GROUPS, group, 0, unroll=True)

    def stage_project(m):
        def near(c, carry):
            cols = pl.ds(pl.multiple_of(c * CHUNK, CHUNK), CHUNK)
            rows = part[m, ROWS : (CROSS + 1) * ROWS, :]
            result = dot_nt(rows, w_in[cols, WIDTH : 3 * WIDTH])
            for k in (2, 0, 1):
                term = result[k * ROWS : (k + 1) * ROWS]
                sbuf[m, c, k] = term.astype(BF16)
                send = sends_direct_down(k)
                if k == 0:

                    @pl.when(gives)
                    def _():
                        join_copy(m, c).start()

                if k == 1:
                    direct1[c] = term
                    send = send & jnp.logical_not(joins)

                    @pl.when(sends_cross(k) & jnp.logical_not(joins))
                    def _():
                        cross_copy(m, c, k).start()

                if k == 2:

                    @pl.when(sends_cross(k))
                    def _():
                        cross_copy(m, c, k).start()

                @pl.when(send)
                def _():
                    bwd_copy(m, c, k).start()

            return carry

        def join_send(c):
            join_copy(m, c).wait_recv()
            sbuf[m, c, 1] = (direct1[c] + pbuf[m, c].astype(F32)).astype(BF16)

            @pl.when(sends_direct_down(1))
            def _():
                bwd_copy(m, c, 1).start()

            @pl.when(sends_cross(1))
            def _():
                cross_copy(m, c, 1).start()

        def far(c, carry):
            @pl.when(joins & (c == 0))
            def _():
                join_send(0)
                join_send(1)

            @pl.when(joins & (c == 2))
            def _():
                join_send(2)

            cols = pl.ds(pl.multiple_of(c * CHUNK, CHUNK), CHUNK)
            rows = jnp.concatenate([part[m, 0:ROWS, :], part[m, (CROSS + 1) * ROWS : KEYS, :]], 0)
            result = dot_nt(rows, w_in[cols, WIDTH : 3 * WIDTH])
            ng[m, :, cols] = result[0:ROWS]
            for k in (4, 3):
                term = result[(k - 2) * ROWS : (k - 1) * ROWS]
                sbuf[m, c, k] = term.astype(BF16)
                send = sends_direct_down(k)
                if k == CROSS:
                    direct[c] = term
                    send = send & jnp.logical_not(relay)

                @pl.when(send)
                def _():
                    bwd_copy(m, c, k).start()

            return carry

        lax.fori_loop(0, CHUNKS, near, 0)
        lax.fori_loop(0, CHUNKS, far, 0)

        @pl.when(joins)
        def _():
            join_send(3)

    def stage_relay(m):
        @pl.when(relay)
        def _():
            for c in range(CHUNKS):
                for k in reversed(range(1, CROSS)):

                    @pl.when(relays(k))
                    def _():
                        cross_copy(m, c, k).wait_recv()
                        direct[c] += qbuf[m, c, k].astype(F32)

                sbuf[m, c, CROSS] = direct[c].astype(BF16)
                bwd_copy(m, c, CROSS).start()

    def stage_query(m):
        def group(g, carry):
            cols = pl.ds(pl.multiple_of(g * GROUP, GROUP), GROUP)
            stacked = dot_tn(sg[g], kv[m, :, cols])
            dq[m * ROWS : (m + 1) * ROWS, cols] = (gather_heads(stacked) * SCALE).astype(BF16)
            return carry

        lax.fori_loop(0, GROUPS, group, 0, unroll=True)

    def stage_own(m):
        def own(c, carry):
            cols = pl.ds(pl.multiple_of(c * CHUNK, CHUNK), CHUNK)
            ng[m, :, cols] += dot_nt(dq[m * ROWS : (m + 1) * ROWS, :], w_in[cols, 0:WIDTH])
            return carry

        lax.fori_loop(0, CHUNKS, own, 0)

    def backward_finish(m):
        early = (0, 1, 2, 4)
        for c in range(CHUNKS):
            cols = slice(c * CHUNK, (c + 1) * CHUNK)
            for k in early:

                @pl.when(gets_direct_down(k))
                def _():
                    bwd_copy(m, c, k).wait_recv()

            ng[m, :, cols] += sum(rbuf[m, c, k].astype(F32) for k in early)

        for c in range(CHUNKS):

            @pl.when(gets_direct_down(CROSS))
            def _():
                bwd_copy(m, c, CROSS).wait_recv()

        pieces = []
        for c in range(CHUNKS):
            cols = slice(c * CHUNK, (c + 1) * CHUNK)
            pieces.append(ng[m, :, cols] + rbuf[m, c, CROSS].astype(F32))
        grad = jnp.concatenate(pieces, 1)
        value = normed[m]
        inner = jnp.mean(grad * value, axis=-1, keepdims=True)
        for h in range(2):
            cols = slice(h * COLS, (h + 1) * COLS)
            change = inv[m, :, 0:1] * (grad[:, cols] - value[:, cols] * inner)
            result = (inc[m, :, cols].astype(F32) + change).astype(BF16)
            gsend[m, :, cols] = result

            @pl.when(z > 0)
            def _():
                z_copy(m, h).start()

            dacts_ref[m, :, cols] = result

    def remote(src, dst, send_sem, recv_sem, peer):
        return pltpu.make_async_remote_copy(
            src_ref=src,
            dst_ref=dst,
            send_sem=send_sem,
            recv_sem=recv_sem,
            device_id=(z, peer),
            device_id_type=MESH,
        )

    def pair_copy(i):
        return remote(psend.at[i], precv.at[i], ps.at[i], pr.at[i], partner)

    def ring_copy(stage, i, side):
        send, recv, ss, rs = ring_refs[stage]
        axis = (i + stage // 2) % 2
        return remote(
            send.at[i, side],
            recv.at[i, side],
            ss.at[i, side],
            rs.at[i, side],
            along(axis, 1 if side == 0 else -1),
        )

    ring_refs = (
        (send1, recv1, s1, r1),
        (send2, recv2, s2, r2),
        (send3, recv3, s3, r3),
        (send4, recv4, s4, r4),
    )

    def transpose_rows():
        def block(r, carry):
            rows = pl.ds(pl.multiple_of(r * CHUNK, CHUNK), CHUNK)
            owns = []
            for m in range(MB):
                tokens = nall[m, :, :, rows].reshape(KEYS, CHUNK)
                turned = tokens.T.reshape(SIDE, 2, SLICE, KEYS)
                for parity in range(2):
                    n_t[parity, r, :, :, m * KEYS : (m + 1) * KEYS] = turned[:, parity]
                owns.append(nall[m, 0, :, rows])
            turned = jnp.concatenate(owns, 0).T.reshape(SIDE, 2, SLICE, MB * ROWS)
            turned_att = att[:, rows].T.reshape(SIDE, 2, SLICE, MB * ROWS)
            for parity in range(2):
                own_t[parity, r] = turned[:, parity]
                att_t[parity, r] = turned_att[:, parity]
            return carry

        lax.fori_loop(0, SIDE, block, 0)

    def operands(i):
        if i < 2:
            low = i * COLS
            right = inc[:, :, low : low + COLS].reshape(MB * ROWS, COLS)
            return att_t, right, 3 * WIDTH + low
        if i < 4:
            low = (i - 2) * COLS
            return own_t, dq[:, low : low + COLS], low
        low = (i - 4) * COLS
        right = part[:, :, low : low + COLS].reshape(MB * KEYS, COLS)
        return n_t, right, WIDTH + low

    def weight_part(i):
        left, right, _ = operands(i)
        depth = right.shape[0]
        shape = (SIDE, SIDE, SLICE, COLS)
        away = left[1 - core].reshape(WIDTH // 2, depth)
        psend[i] = dot(away, right).astype(BF16).reshape(shape)
        pair_copy(i).start()
        here = left[core].reshape(WIDTH // 2, depth)
        total[i] = dot(here, right).reshape(shape)

    def pick(i, step):
        axis = i % 2
        where = lax.rem((place_x if axis == 0 else place_y) + step % SIDE, SIDE)
        return total[i, where] if axis == 0 else total[i, :, where]

    def pick_row(i, step):
        axis = (i + 1) % 2
        return column[i, lax.rem((place_x if axis == 0 else place_y) + step % SIDE, SIDE)]

    def ring_one(i):
        pair_copy(i).wait_recv()
        total[i] += precv[i].astype(F32)
        far = pick(i, 2).astype(BF16)
        send1[i, 0] = far[:, :, :HALF]
        send1[i, 1] = far[:, :, HALF:]
        for side in range(2):
            ring_copy(0, i, side).start()

    def ring_two(i):
        for side in range(2):
            ring_copy(0, i, side).wait_recv()
        right, left = pick(i, 1), pick(i, -1)
        send2[i, 0, :, :, :HALF] = (right[:, :, :HALF] + recv1[i, 0].astype(F32)).astype(BF16)
        send2[i, 0, :, :, HALF:] = right[:, :, HALF:].astype(BF16)
        ring_copy(1, i, 0).start()
        send2[i, 1, :, :, :HALF] = left[:, :, :HALF].astype(BF16)
        send2[i, 1, :, :, HALF:] = (left[:, :, HALF:] + recv1[i, 1].astype(F32)).astype(BF16)
        ring_copy(1, i, 1).start()

    def ring_three(i):
        for side in range(2):
            ring_copy(1, i, side).wait_recv()
        column[i] = pick(i, 0) + recv2[i, 0].astype(F32) + recv2[i, 1].astype(F32)
        far = pick_row(i, 2).astype(BF16)
        send3[i, 0] = far[:, :HALF]
        send3[i, 1] = far[:, HALF:]
        for side in range(2):
            ring_copy(2, i, side).start()

    def ring_four(i):
        for side in range(2):
            ring_copy(2, i, side).wait_recv()
        right, left = pick_row(i, 1), pick_row(i, -1)
        send4[i, 0, :, :HALF] = (right[:, :HALF] + recv3[i, 0].astype(F32)).astype(BF16)
        send4[i, 0, :, HALF:] = right[:, HALF:].astype(BF16)
        ring_copy(3, i, 0).start()
        send4[i, 1, :, :HALF] = left[:, :HALF].astype(BF16)
        send4[i, 1, :, HALF:] = (left[:, HALF:] + recv3[i, 1].astype(F32)).astype(BF16)
        ring_copy(3, i, 1).start()

    def ring_last(i):
        for side in range(2):
            ring_copy(3, i, side).wait_recv()
        result = pick_row(i, 0) + recv4[i, 0].astype(F32) + recv4[i, 1].astype(F32)
        low = (3 * WIDTH if i < 2 else -2 * COLS if i < 4 else WIDTH - 4 * COLS) + i * COLS
        if low < 3 * WIDTH:
            dwin_ref[:, low : low + COLS] = result
        else:
            dwout_ref[:, low - 3 * WIDTH : low - 3 * WIDTH + COLS] = result

    def rest_forward():
        attend(0)
        attend(1)
        transpose_rows()

    last = z == sections - 1
    forward_relay(0)
    forward_send(1, (4, 2, 1, 0))
    copy_in.wait()
    own_projections()
    forward_join(0)
    forward_relay(1)
    forward_keys(0)
    forward_weights(0)
    forward_join(1)
    copy_out.wait()

    @pl.when(z < sections - 1)
    def _():
        forward_keys(1)
        forward_weights(1)
        rest_forward()

    stage_upstream(0)
    stage_parts(0)
    stage_project(0)

    @pl.when(last)
    def _():
        forward_keys(1)

    stage_query(0)
    stage_relay(0)

    @pl.when(last)
    def _():
        forward_weights(1)

    stage_own(0)
    backward_finish(0)

    @pl.when(z == 0)
    def _():
        wait_incoming(1, 0)
        wait_incoming(1, 1)
        weight_part(0)
        weight_part(1)

    stage_upstream(1)

    @pl.when(z == 0)
    def _():
        ring_one(0)
        ring_one(1)

    stage_parts(1)

    @pl.when(z > 0)
    def _():
        stage_project(1)

    stage_query(1)

    @pl.when(z > 0)
    def _():
        stage_relay(1)
        stage_own(1)
        backward_finish(1)

        @pl.when(last)
        def _():
            rest_forward()

        weight_part(0)
        weight_part(1)
        ring_one(0)
        ring_one(1)

    for i in range(2, PARTS):
        weight_part(i)
        if i > 2:
            ring_one(i - 1)
            ring_two(i - 3)
    ring_one(PARTS - 1)
    ring_two(PARTS - 3)

    @pl.when(z == 0)
    def _():
        stage_project(1)
        stage_own(1)

    ring_three(0)
    ring_two(PARTS - 2)
    ring_three(1)
    ring_two(PARTS - 1)

    @pl.when(z == 0)
    def _():
        stage_relay(1)

    for i in range(2, PARTS + 3):
        if i < PARTS:
            ring_three(i)
        if i < PARTS + 2:
            ring_four(i - 2)
        if 4 <= i:
            ring_last(i - 4)
        if i == PARTS - 1:

            @pl.when(z == 0)
            def _():
                backward_finish(1)

    ring_last(PARTS - 1)

    for i in range(PARTS):
        pair_copy(i).wait_send()
        for stage in range(4):
            for side in range(2):
                ring_copy(stage, i, side).wait_send()

    for m in range(MB):
        for k in range(LEVELS):

            @pl.when(sends_direct_up(k))
            def _():
                fwd_copy(m, k).wait_send()

            @pl.when(sends_direct_down(k))
            def _():
                for c in range(CHUNKS):
                    bwd_copy(m, c, k).wait_send()

            if 0 < k < CROSS:

                @pl.when(relays(k))
                def _():
                    fwd_cross(m, k).wait_send()

                @pl.when(sends_cross(k))
                def _():
                    for c in range(CHUNKS):
                        cross_copy(m, c, k).wait_send()

        @pl.when(joins)
        def _():
            fwd_pair(m).wait_send()

        @pl.when(gives)
        def _():
            for c in range(CHUNKS):
                join_copy(m, c).wait_send()

        @pl.when(z > 0)
        def _():
            for h in range(2):
                z_copy(m, h).wait_send()


def result_kernel(a, b, c, a_out, b_out, c_out, a_buf, b_buf, c_buf, sem_in, sem_out):
    sources, buffers, targets = (a, b, c), (a_buf, b_buf, c_buf), (a_out, b_out, c_out)
    fetch = [pltpu.make_async_copy(sources[i], buffers[i], sem_in.at[i]) for i in range(3)]
    store = [pltpu.make_async_copy(buffers[i], targets[i], sem_out.at[i]) for i in range(3)]
    for copy in fetch:
        copy.start()
    for i in range(3):
        fetch[i].wait()
        store[i].start()
    for copy in store:
        copy.wait()


def per_device(acts, grad_top, w_in, w_out, offsets):
    sections = lax.axis_size("section")
    shards = lax.axis_size("tm")
    vmem = pl.BlockSpec(memory_space=pltpu.VMEM)
    d_acts, d_in, d_out = pl.pallas_call(
        functools.partial(layer_kernel, sections, shards),
        out_shape=(
            jax.ShapeDtypeStruct((MB, ROWS, WIDTH), BF16),
            jax.ShapeDtypeStruct((SLICE, 3 * WIDTH), F32),
            jax.ShapeDtypeStruct((SLICE, WIDTH), F32),
        ),
        in_specs=[
            vmem,
            vmem,
            pl.BlockSpec(memory_space=pl.ANY),
            pl.BlockSpec(memory_space=pl.ANY),
            pl.BlockSpec(memory_space=pltpu.SMEM),
        ],
        out_specs=(vmem, vmem, vmem),
        scratch_shapes=[
            pltpu.VMEM((WIDTH, 3 * WIDTH), BF16),
            pltpu.VMEM((WIDTH, WIDTH), BF16),
            pltpu.VMEM((MB, BLOCKS, ROWS, WIDTH), BF16),
            pltpu.VMEM((MB, ROWS, WIDTH), F32),
            pltpu.VMEM((MB, ROWS, 128), F32),
            pltpu.VMEM((MB, GROUPS, GROUP, GROUP), BF16),
            pltpu.VMEM((MB, KEYS, 2 * WIDTH), BF16),
            pltpu.VMEM((MB, GROUPS, KEYS, GROUP), F32),
            pltpu.VMEM((MB, GROUPS, KEYS, GROUP), BF16),
            pltpu.VMEM((GROUP, GROUP), BF16),
            pltpu.VMEM((KEYS, GROUP), F32),
            pltpu.VMEM((MB, ROWS, WIDTH), BF16),
            pltpu.VMEM((MB * ROWS, WIDTH), BF16),
            pltpu.VMEM((MB, KEYS, 2 * WIDTH), BF16),
            pltpu.VMEM((MB * ROWS, WIDTH), BF16),
            pltpu.VMEM((MB, ROWS, WIDTH), F32),
            pltpu.VMEM((MB, ROWS, WIDTH), BF16),
            pltpu.VMEM((MB, CHUNKS, LEVELS, ROWS, CHUNK), BF16),
            pltpu.VMEM((MB, CHUNKS, LEVELS, ROWS, CHUNK), BF16),
            pltpu.SemaphoreType.DMA((2,)),
            pltpu.SemaphoreType.DMA((MB, LEVELS)),
            pltpu.SemaphoreType.DMA((MB, LEVELS)),
            pltpu.SemaphoreType.DMA((MB, CHUNKS, LEVELS)),
            pltpu.SemaphoreType.DMA((MB, CHUNKS, LEVELS)),
            pltpu.SemaphoreType.DMA((MB, 2)),
            pltpu.SemaphoreType.DMA((MB, 2)),
            pltpu.VMEM((2, SIDE, SIDE, SLICE, MB * KEYS), BF16),
            pltpu.VMEM((2, SIDE, SIDE, SLICE, MB * ROWS), BF16),
            pltpu.VMEM((2, SIDE, SIDE, SLICE, MB * ROWS), BF16),
            pltpu.VMEM((PARTS, SIDE, SIDE, SLICE, COLS), BF16),
            pltpu.VMEM((PARTS, SIDE, SIDE, SLICE, COLS), BF16),
            pltpu.VMEM((PARTS, SIDE, SIDE, SLICE, COLS), F32),
            pltpu.VMEM((PARTS, 2, SIDE, SLICE, HALF), BF16),
            pltpu.VMEM((PARTS, 2, SIDE, SLICE, HALF), BF16),
            pltpu.VMEM((PARTS, 2, SIDE, SLICE, COLS), BF16),
            pltpu.VMEM((PARTS, 2, SIDE, SLICE, COLS), BF16),
            pltpu.VMEM((PARTS, SIDE, SLICE, COLS), F32),
            pltpu.VMEM((PARTS, 2, SLICE, HALF), BF16),
            pltpu.VMEM((PARTS, 2, SLICE, HALF), BF16),
            pltpu.VMEM((PARTS, 2, SLICE, COLS), BF16),
            pltpu.VMEM((PARTS, 2, SLICE, COLS), BF16),
            pltpu.SemaphoreType.DMA((PARTS,)),
            pltpu.SemaphoreType.DMA((PARTS,)),
        ]
        + [pltpu.SemaphoreType.DMA((PARTS, 2))] * 8
        + [
            pltpu.VMEM((GROUPS, KEYS, GROUP), BF16),
            pltpu.VMEM((ROWS, WIDTH), F32),
            pltpu.VMEM((ROWS, WIDTH), BF16),
            pltpu.VMEM((MB, CHUNKS, CROSS, ROWS, CHUNK), BF16),
            pltpu.VMEM((CHUNKS, ROWS, CHUNK), F32),
            pltpu.SemaphoreType.DMA((MB, CHUNKS, CROSS)),
            pltpu.SemaphoreType.DMA((MB, CHUNKS, CROSS)),
            pltpu.SemaphoreType.DMA((MB, CROSS)),
            pltpu.VMEM((CHUNKS, ROWS, CHUNK), F32),
            pltpu.VMEM((MB, CHUNKS, ROWS, CHUNK), BF16),
            pltpu.SemaphoreType.DMA((MB, CHUNKS)),
            pltpu.SemaphoreType.DMA((MB, CHUNKS)),
            pltpu.SemaphoreType.DMA((MB,)),
        ],
        compiler_params=pltpu.CompilerParams(
            collective_id=0, has_side_effects=True, vmem_limit_bytes=63 * 1024 * 1024
        ),
        name="layer_kernel",
    )(acts[0], grad_top, w_in[0], w_out[0], offsets)
    results = (d_acts, d_in, d_out)
    anywhere = pl.BlockSpec(memory_space=pl.ANY)
    d_acts, d_in, d_out = pl.pallas_call(
        result_kernel,
        out_shape=tuple(jax.ShapeDtypeStruct(r.shape, r.dtype) for r in results),
        in_specs=[anywhere] * 3,
        out_specs=(anywhere,) * 3,
        scratch_shapes=[pltpu.VMEM(r.shape, r.dtype) for r in results]
        + [pltpu.SemaphoreType.DMA((3,)), pltpu.SemaphoreType.DMA((3,))],
        name="result_kernel",
    )(*results)
    return (d_acts[None], d_in[None], d_out[None])


def solution(mesh):
    placed = (
        P("section", None, "tm", None),
        P(None, "tm", None),
        P("section", None, None),
        P("section", None, None),
        P("tm", None),
    )
    return jax.shard_map(
        per_device,
        mesh=mesh,
        in_specs=placed,
        out_specs=(
            P("section", None, "tm", None),
            P("section", "tm", None),
            P("section", "tm", None),
        ),
        check_vma=False,
    )
```

```python
import functools

import jax
import jax.numpy as jnp
from jax import lax
from jax.experimental import pallas as pl
from jax.experimental.pallas import tpu as pltpu
from jax.sharding import PartitionSpec as P

HEAD_DIM = 64
SCALE = HEAD_DIM ** (-0.5)
EPSILON = 1e-06
FILL = -1e30
MESH = pl.DeviceIdType.MESH

MB = 2
ROWS = 64
WIDTH = 1024
LEVELS = 5
BLOCKS = LEVELS + 1
KEYS = BLOCKS * ROWS
GROUP = 256
GROUPS = WIDTH // GROUP
CHUNK = 256
CHUNKS = WIDTH // CHUNK
PER = GROUP // HEAD_DIM
SIDE = 4
ROW = 8
CROSS = 3
SLICE = 32
PARTS = 8
COLS = 512
HALF = COLS // 2

BF16 = jnp.bfloat16
F32 = jnp.float32


def dot(a, b):
    return lax.dot_general(a, b, (((1,), (0,)), ((), ())), preferred_element_type=F32)


def dot_nt(a, b):
    return lax.dot_general(a, b, (((1,), (1,)), ((), ())), preferred_element_type=F32)


def dot_tn(a, b):
    return lax.dot_general(a, b, (((0,), (0,)), ((), ())), preferred_element_type=F32)


def layer_kernel(
    sections,
    shards,
    acts_ref,
    gtop_ref,
    w_in_hbm,
    w_out_hbm,
    off_ref,
    dacts_ref,
    dwin_ref,
    dwout_ref,
    w_in,
    w_out,
    nall,
    normed,
    inv,
    qm,
    kv,
    p32,
    p16,
    bm,
    bias,
    inc,
    dq,
    part,
    att,
    ng,
    gsend,
    sbuf,
    rbuf,
    w_sem,
    fs,
    fr,
    bs,
    br,
    zs,
    zr,
    n_t,
    own_t,
    att_t,
    psend,
    precv,
    total,
    send1,
    recv1,
    send2,
    recv2,
    column,
    send3,
    recv3,
    send4,
    recv4,
    ps,
    pr,
    s1,
    r1,
    s2,
    r2,
    s3,
    r3,
    s4,
    r4,
    sg,
    up32,
    up16,
    qbuf,
    direct,
    qs,
    qr,
    fq,
    direct1,
    pbuf,
    bp,
    bq,
    fp,
):
    z = lax.axis_index("section")
    t = lax.axis_index("tm")
    steps = [2**level for level in range(LEVELS)]
    place_x = t // 8
    place_y = lax.rem(t // 2, SIDE)
    core = lax.rem(t, 2)
    partner = t + 1 - 2 * core
    column_of = lax.rem(t, ROW)

    def sends_direct_down(k):
        if k == 0:
            return core == 1
        ok = t >= steps[k]
        return ok & (column_of >= steps[k]) if k < CROSS else ok

    def gets_direct_down(k):
        if k == 0:
            return core == 0
        ok = t + steps[k] < shards
        return ok & (column_of + steps[k] < ROW) if k < CROSS else ok

    def sends_direct_up(k):
        return gets_direct_down(k)

    def sends_cross(k):
        return (t >= ROW) & (column_of < steps[k])

    def relays(k):
        return (t >= ROW) & (column_of + steps[k] >= ROW)

    joins = (core == 1) & (t >= 3)
    gives = (core == 0) & (t >= 2)
    relay = (t >= ROW) & (column_of >= ROW // 2)

    def cross_target(k):
        return lax.rem(t + ROW - steps[k], shards)

    def cross_back(k):
        return lax.rem(t + shards - ROW + steps[k], shards)

    def along(axis, step):
        if axis == 0:
            return lax.rem(t + 8 * (step % SIDE), shards)
        return place_x * 8 + lax.rem(place_y + step % SIDE, SIDE) * 2 + core

    def up_shard(k):
        return lax.rem(t + steps[k], shards)

    def down_shard(k):
        return lax.rem(t + shards - steps[k], shards)

    copy_in = pltpu.make_async_copy(w_in_hbm, w_in, w_sem.at[0])
    copy_out = pltpu.make_async_copy(w_out_hbm, w_out, w_sem.at[1])
    copy_in.start()
    copy_out.start()

    barrier = pltpu.get_barrier_semaphore()
    for k in range(LEVELS):
        pl.semaphore_signal(barrier, inc=1, device_id=(z, up_shard(k)), device_id_type=MESH)
        if 2 * steps[k] != shards:
            pl.semaphore_signal(barrier, inc=1, device_id=(z, down_shard(k)), device_id_type=MESH)
    peers = (along(1, 1), along(1, -1), partner)
    peers += (cross_target(1), cross_back(1))
    for peer in peers:
        pl.semaphore_signal(barrier, inc=1, device_id=(z, peer), device_id_type=MESH)
    for step in (1, sections - 1):
        pl.semaphore_signal(
            barrier, inc=1, device_id=(lax.rem(z + step, sections), t), device_id_type=MESH
        )

    def fwd_copy(m, k):
        return pltpu.make_async_remote_copy(
            src_ref=nall.at[m, 0],
            dst_ref=nall.at[m, k + 1],
            send_sem=fs.at[m, k],
            recv_sem=fr.at[m, k],
            device_id=(z, up_shard(k)),
            device_id_type=MESH,
        )

    def bwd_copy(m, c, k):
        return pltpu.make_async_remote_copy(
            src_ref=sbuf.at[m, c, k],
            dst_ref=rbuf.at[m, c, k],
            send_sem=bs.at[m, c, k],
            recv_sem=br.at[m, c, k],
            device_id=(z, down_shard(k)),
            device_id_type=MESH,
        )

    def cross_copy(m, c, k):
        return pltpu.make_async_remote_copy(
            src_ref=sbuf.at[m, c, k],
            dst_ref=qbuf.at[m, c, k],
            send_sem=qs.at[m, c, k],
            recv_sem=qr.at[m, c, k],
            device_id=(z, cross_target(k)),
            device_id_type=MESH,
        )

    def fwd_cross(m, k):
        return pltpu.make_async_remote_copy(
            src_ref=nall.at[m, CROSS + 1],
            dst_ref=nall.at[m, k + 1],
            send_sem=fq.at[m, k],
            recv_sem=fr.at[m, k],
            device_id=(z, cross_back(k)),
            device_id_type=MESH,
        )

    def join_copy(m, c):
        return pltpu.make_async_remote_copy(
            src_ref=sbuf.at[m, c, 0],
            dst_ref=pbuf.at[m, c],
            send_sem=bp.at[m, c],
            recv_sem=bq.at[m, c],
            device_id=(z, partner),
            device_id_type=MESH,
        )

    def fwd_pair(m):
        return pltpu.make_async_remote_copy(
            src_ref=nall.at[m, 2],
            dst_ref=nall.at[m, 1],
            send_sem=fp.at[m],
            recv_sem=fr.at[m, 0],
            device_id=(z, partner),
            device_id_type=MESH,
        )

    def z_copy(m, h):
        cols = pl.ds(h * COLS, COLS)
        return pltpu.make_async_remote_copy(
            src_ref=gsend.at[m, :, cols],
            dst_ref=inc.at[m, :, cols],
            send_sem=zs.at[m, h],
            recv_sem=zr.at[m, h],
            device_id=(lax.rem(z + sections - 1, sections), t),
            device_id_type=MESH,
        )

    def forward_send(m, levels):
        for k in levels:

            @pl.when(sends_direct_up(k))
            def _():
                fwd_copy(m, k).start()

    for m in range(MB):
        x = acts_ref[m].astype(F32)
        inverse = lax.rsqrt(jnp.mean(x * x, axis=-1, keepdims=True) + EPSILON)
        value = x * inverse
        normed[m] = value
        inv[m] = jnp.broadcast_to(inverse, (ROWS, 128))
        nall[m, 0] = value.astype(BF16)
        if m == 0:
            pl.semaphore_wait(barrier, 2 * LEVELS + 6)
        if m == 0:
            forward_send(0, (3, 4, 2, 1, 0))
        else:
            forward_send(1, (3,))

        for k in range(LEVELS):

            @pl.when(t < steps[k])
            def _():
                nall[m, k + 1] = jnp.zeros((ROWS, WIDTH), BF16)

    row_head = lax.broadcasted_iota(jnp.int32, (GROUP, GROUP), 0) // HEAD_DIM
    lane_head = lax.broadcasted_iota(jnp.int32, (GROUP, GROUP), 1) // HEAD_DIM
    bm[...] = jnp.where(row_head == lane_head, 1.0, 0.0).astype(BF16)
    key_pos = lax.broadcasted_iota(jnp.int32, (ROWS, GROUP), 0)
    query_pos = lax.broadcasted_iota(jnp.int32, (ROWS, GROUP), 1) % ROWS
    bias[0:ROWS, :] = jnp.where(key_pos <= query_pos, 0.0, FILL)
    for k in range(LEVELS):
        fill = jnp.where(off_ref[0, k] != 0, 0.0, FILL)
        bias[(k + 1) * ROWS : (k + 2) * ROWS, :] = jnp.full((ROWS, GROUP), fill, F32)

    @pl.when(z == sections - 1)
    def _():
        inc[...] = gtop_ref[...]

    for k in range(LEVELS):

        @pl.when(jnp.logical_not(gets_direct_down(k)))
        def _():
            rbuf[:, :, k] = jnp.zeros((MB, CHUNKS, ROWS, CHUNK), BF16)

    def spread(rows):
        return jnp.concatenate([rows] * PER, 0) * bm[...]

    def gather_heads(stacked):
        lanes = lax.broadcasted_iota(jnp.int32, (ROWS, GROUP), 1) // HEAD_DIM
        total = jnp.where(lanes == 0, stacked[0:ROWS], 0.0)
        for head in range(1, PER):
            total = jnp.where(lanes == head, stacked[head * ROWS : (head + 1) * ROWS], total)
        return total

    def own_query(c, carry):
        cols = pl.ds(pl.multiple_of(c * GROUP, GROUP), GROUP)
        both = jnp.concatenate([nall[0, 0], nall[1, 0]], 0)
        result = dot(both, w_in[:, cols]).astype(BF16)
        for m in range(MB):
            qm[m, c] = spread(result[m * ROWS : (m + 1) * ROWS])
        return carry

    def own_pair(c, carry):
        cols = pl.ds(pl.multiple_of(c * GROUP, GROUP), GROUP)
        source = pl.ds(pl.multiple_of(WIDTH + c * GROUP, GROUP), GROUP)
        both = jnp.concatenate([nall[0, 0], nall[1, 0]], 0)
        result = dot(both, w_in[:, source]).astype(BF16)
        for m in range(MB):
            kv[m, 0:ROWS, cols] = result[m * ROWS : (m + 1) * ROWS]
        return carry

    def own_projections():
        lax.fori_loop(0, GROUPS, own_query, 0, unroll=2)
        lax.fori_loop(0, 2 * GROUPS, own_pair, 0, unroll=2)

    def forward_relay(m):
        @pl.when(t >= steps[CROSS])
        def _():
            fwd_copy(m, CROSS).wait_recv()

        for k in reversed(range(1, CROSS)):

            @pl.when(relays(k))
            def _():
                fwd_cross(m, k).start()

    def forward_join(m):
        @pl.when(t >= steps[1])
        def _():
            fwd_copy(m, 1).wait_recv()

        @pl.when(joins)
        def _():
            fwd_pair(m).start()

    def forward_keys(m):
        for k in (0, 2, 4):

            @pl.when(t >= steps[k])
            def _():
                fwd_copy(m, k).wait_recv()

        def far_pair(c, carry):
            cols = pl.ds(pl.multiple_of(c * GROUP, GROUP), GROUP)
            source = pl.ds(pl.multiple_of(WIDTH + c * GROUP, GROUP), GROUP)
            rows = nall[m, 1:BLOCKS].reshape(LEVELS * ROWS, WIDTH)
            kv[m, ROWS:KEYS, cols] = dot(rows, w_in[:, source]).astype(BF16)
            return carry

        lax.fori_loop(0, 2 * GROUPS, far_pair, 0, unroll=2)

    def forward_weights(m):
        def probability(g, carry):
            cols = pl.ds(pl.multiple_of(g * GROUP, GROUP), GROUP)
            scores = dot_nt(kv[m, :, cols], qm[m, g]) * SCALE + bias[...]
            highest = jnp.max(scores, axis=0, keepdims=True)
            weights = jnp.exp(scores - highest)
            result = weights / jnp.sum(weights, axis=0, keepdims=True)
            p32[m, g] = result
            p16[m, g] = result.astype(BF16)
            return carry

        lax.fori_loop(0, GROUPS, probability, 0, unroll=True)

    def attend(m):
        def group(g, carry):
            cols = pl.ds(pl.multiple_of(g * GROUP, GROUP), GROUP)
            values = pl.ds(pl.multiple_of(WIDTH + g * GROUP, GROUP), GROUP)
            stacked = dot_tn(p16[m, g], kv[m, :, values])
            att[m * ROWS : (m + 1) * ROWS, cols] = gather_heads(stacked).astype(BF16)
            return carry

        lax.fori_loop(0, GROUPS, group, 0)

    def wait_incoming(m, h):
        z_copy(m, h).wait_recv()

    def stage_upstream(m):
        waits = (z < sections - 1) if m == 0 else (z < sections - 1) & (z > 0)

        @pl.when(waits)
        def _():
            wait_incoming(m, 0)

        def first(g, carry):
            cols = pl.ds(pl.multiple_of(g * GROUP, GROUP), GROUP)
            up32[:, cols] = dot_nt(inc[m, :, 0:COLS], w_out[cols, 0:COLS])
            return carry

        lax.fori_loop(0, GROUPS, first, 0, unroll=True)

        @pl.when(waits)
        def _():
            wait_incoming(m, 1)

        def second(g, carry):
            cols = pl.ds(pl.multiple_of(g * GROUP, GROUP), GROUP)
            rest = dot_nt(inc[m, :, COLS : 2 * COLS], w_out[cols, COLS : 2 * COLS])
            up16[:, cols] = (up32[:, cols] + rest).astype(BF16)
            return carry

        lax.fori_loop(0, GROUPS, second, 0, unroll=True)

    def stage_parts(m):
        def group(g, carry):
            cols = pl.ds(pl.multiple_of(g * GROUP, GROUP), GROUP)
            values = pl.ds(pl.multiple_of(WIDTH + g * GROUP, GROUP), GROUP)
            up_heads = spread(up16[:, cols])
            prob_grad = dot_nt(kv[m, :, values], up_heads)
            part[m, :, values] = dot(p16[m, g], up_heads).astype(BF16)
            prob = p32[m, g]
            delta = jnp.sum(prob * prob_grad, axis=0, keepdims=True)
            score_grad = (prob * (prob_grad - delta)).astype(BF16)
            sg[g] = score_grad
            part[m, :, cols] = (dot(score_grad, qm[m, g]) * SCALE).astype(BF16)
            return carry

        lax.fori_loop(0, GROUPS, group, 0, unroll=True)

    def stage_project(m):
        def near(c, carry):
            cols = pl.ds(pl.multiple_of(c * CHUNK, CHUNK), CHUNK)
            rows = part[m, ROWS : (CROSS + 1) * ROWS, :]
            result = dot_nt(rows, w_in[cols, WIDTH : 3 * WIDTH])
            for k in (2, 0, 1):
                term = result[k * ROWS : (k + 1) * ROWS]
                sbuf[m, c, k] = term.astype(BF16)
                send = sends_direct_down(k)
                if k == 0:

                    @pl.when(gives)
                    def _():
                        join_copy(m, c).start()

                if k == 1:
                    direct1[c] = term
                    send = send & jnp.logical_not(joins)

                    @pl.when(sends_cross(k) & jnp.logical_not(joins))
                    def _():
                        cross_copy(m, c, k).start()

                if k == 2:

                    @pl.when(sends_cross(k))
                    def _():
                        cross_copy(m, c, k).start()

                @pl.when(send)
                def _():
                    bwd_copy(m, c, k).start()

            return carry

        def join_send(c):
            join_copy(m, c).wait_recv()
            sbuf[m, c, 1] = (direct1[c] + pbuf[m, c].astype(F32)).astype(BF16)

            @pl.when(sends_direct_down(1))
            def _():
                bwd_copy(m, c, 1).start()

            @pl.when(sends_cross(1))
            def _():
                cross_copy(m, c, 1).start()

        def far(c, carry):
            @pl.when(joins & (c == 0))
            def _():
                join_send(0)
                join_send(1)

            @pl.when(joins & (c == 2))
            def _():
                join_send(2)

            cols = pl.ds(pl.multiple_of(c * CHUNK, CHUNK), CHUNK)
            rows = jnp.concatenate([part[m, 0:ROWS, :], part[m, (CROSS + 1) * ROWS : KEYS, :]], 0)
            result = dot_nt(rows, w_in[cols, WIDTH : 3 * WIDTH])
            ng[m, :, cols] = result[0:ROWS]
            for k in (4, 3):
                term = result[(k - 2) * ROWS : (k - 1) * ROWS]
                sbuf[m, c, k] = term.astype(BF16)
                send = sends_direct_down(k)
                if k == CROSS:
                    direct[c] = term
                    send = send & jnp.logical_not(relay)

                @pl.when(send)
                def _():
                    bwd_copy(m, c, k).start()

            return carry

        lax.fori_loop(0, CHUNKS, near, 0)
        lax.fori_loop(0, CHUNKS, far, 0)

        @pl.when(joins)
        def _():
            join_send(3)

    def stage_relay(m):
        @pl.when(relay)
        def _():
            for c in range(CHUNKS):
                for k in reversed(range(1, CROSS)):

                    @pl.when(relays(k))
                    def _():
                        cross_copy(m, c, k).wait_recv()
                        direct[c] += qbuf[m, c, k].astype(F32)

                sbuf[m, c, CROSS] = direct[c].astype(BF16)
                bwd_copy(m, c, CROSS).start()

    def stage_query(m):
        def group(g, carry):
            cols = pl.ds(pl.multiple_of(g * GROUP, GROUP), GROUP)
            stacked = dot_tn(sg[g], kv[m, :, cols])
            dq[m * ROWS : (m + 1) * ROWS, cols] = (gather_heads(stacked) * SCALE).astype(BF16)
            return carry

        lax.fori_loop(0, GROUPS, group, 0, unroll=True)

    def stage_own(m):
        def own(c, carry):
            cols = pl.ds(pl.multiple_of(c * CHUNK, CHUNK), CHUNK)
            ng[m, :, cols] += dot_nt(dq[m * ROWS : (m + 1) * ROWS, :], w_in[cols, 0:WIDTH])
            return carry

        lax.fori_loop(0, CHUNKS, own, 0)

    def backward_finish(m):
        early = (0, 1, 2, 4)
        for c in range(CHUNKS):
            cols = slice(c * CHUNK, (c + 1) * CHUNK)
            for k in early:

                @pl.when(gets_direct_down(k))
                def _():
                    bwd_copy(m, c, k).wait_recv()

            ng[m, :, cols] += sum(rbuf[m, c, k].astype(F32) for k in early)

        for c in range(CHUNKS):

            @pl.when(gets_direct_down(CROSS))
            def _():
                bwd_copy(m, c, CROSS).wait_recv()

        pieces = []
        for c in range(CHUNKS):
            cols = slice(c * CHUNK, (c + 1) * CHUNK)
            pieces.append(ng[m, :, cols] + rbuf[m, c, CROSS].astype(F32))
        grad = jnp.concatenate(pieces, 1)
        value = normed[m]
        inner = jnp.mean(grad * value, axis=-1, keepdims=True)
        for h in range(2):
            cols = slice(h * COLS, (h + 1) * COLS)
            change = inv[m, :, 0:1] * (grad[:, cols] - value[:, cols] * inner)
            result = (inc[m, :, cols].astype(F32) + change).astype(BF16)
            gsend[m, :, cols] = result

            @pl.when(z > 0)
            def _():
                z_copy(m, h).start()

            dacts_ref[m, :, cols] = result

    def remote(src, dst, send_sem, recv_sem, peer):
        return pltpu.make_async_remote_copy(
            src_ref=src,
            dst_ref=dst,
            send_sem=send_sem,
            recv_sem=recv_sem,
            device_id=(z, peer),
            device_id_type=MESH,
        )

    def pair_copy(i):
        return remote(psend.at[i], precv.at[i], ps.at[i], pr.at[i], partner)

    def ring_copy(stage, i, side):
        send, recv, ss, rs = ring_refs[stage]
        axis = (i + stage // 2) % 2
        return remote(
            send.at[i, side],
            recv.at[i, side],
            ss.at[i, side],
            rs.at[i, side],
            along(axis, 1 if side == 0 else -1),
        )

    ring_refs = (
        (send1, recv1, s1, r1),
        (send2, recv2, s2, r2),
        (send3, recv3, s3, r3),
        (send4, recv4, s4, r4),
    )

    def transpose_rows():
        def block(r, carry):
            rows = pl.ds(pl.multiple_of(r * CHUNK, CHUNK), CHUNK)
            owns = []
            for m in range(MB):
                tokens = nall[m, :, :, rows].reshape(KEYS, CHUNK)
                turned = tokens.T.reshape(SIDE, 2, SLICE, KEYS)
                for parity in range(2):
                    n_t[parity, r, :, :, m * KEYS : (m + 1) * KEYS] = turned[:, parity]
                owns.append(nall[m, 0, :, rows])
            turned = jnp.concatenate(owns, 0).T.reshape(SIDE, 2, SLICE, MB * ROWS)
            turned_att = att[:, rows].T.reshape(SIDE, 2, SLICE, MB * ROWS)
            for parity in range(2):
                own_t[parity, r] = turned[:, parity]
                att_t[parity, r] = turned_att[:, parity]
            return carry

        lax.fori_loop(0, SIDE, block, 0)

    def operands(i):
        if i < 2:
            low = i * COLS
            right = inc[:, :, low : low + COLS].reshape(MB * ROWS, COLS)
            return att_t, right, 3 * WIDTH + low
        if i < 4:
            low = (i - 2) * COLS
            return own_t, dq[:, low : low + COLS], low
        low = (i - 4) * COLS
        right = part[:, :, low : low + COLS].reshape(MB * KEYS, COLS)
        return n_t, right, WIDTH + low

    def weight_part(i):
        left, right, _ = operands(i)
        depth = right.shape[0]
        shape = (SIDE, SIDE, SLICE, COLS)
        away = left[1 - core].reshape(WIDTH // 2, depth)
        psend[i] = dot(away, right).astype(BF16).reshape(shape)
        pair_copy(i).start()
        here = left[core].reshape(WIDTH // 2, depth)
        total[i] = dot(here, right).reshape(shape)

    def pick(i, step):
        axis = i % 2
        where = lax.rem((place_x if axis == 0 else place_y) + step % SIDE, SIDE)
        return total[i, where] if axis == 0 else total[i, :, where]

    def pick_row(i, step):
        axis = (i + 1) % 2
        return column[i, lax.rem((place_x if axis == 0 else place_y) + step % SIDE, SIDE)]

    def ring_one(i):
        pair_copy(i).wait_recv()
        total[i] += precv[i].astype(F32)
        far = pick(i, 2).astype(BF16)
        send1[i, 0] = far[:, :, :HALF]
        send1[i, 1] = far[:, :, HALF:]
        for side in range(2):
            ring_copy(0, i, side).start()

    def ring_two(i):
        for side in range(2):
            ring_copy(0, i, side).wait_recv()
        right, left = pick(i, 1), pick(i, -1)
        send2[i, 0, :, :, :HALF] = (right[:, :, :HALF] + recv1[i, 0].astype(F32)).astype(BF16)
        send2[i, 0, :, :, HALF:] = right[:, :, HALF:].astype(BF16)
        ring_copy(1, i, 0).start()
        send2[i, 1, :, :, :HALF] = left[:, :, :HALF].astype(BF16)
        send2[i, 1, :, :, HALF:] = (left[:, :, HALF:] + recv1[i, 1].astype(F32)).astype(BF16)
        ring_copy(1, i, 1).start()

    def ring_three(i):
        for side in range(2):
            ring_copy(1, i, side).wait_recv()
        column[i] = pick(i, 0) + recv2[i, 0].astype(F32) + recv2[i, 1].astype(F32)
        far = pick_row(i, 2).astype(BF16)
        send3[i, 0] = far[:, :HALF]
        send3[i, 1] = far[:, HALF:]
        for side in range(2):
            ring_copy(2, i, side).start()

    def ring_four(i):
        for side in range(2):
            ring_copy(2, i, side).wait_recv()
        right, left = pick_row(i, 1), pick_row(i, -1)
        send4[i, 0, :, :HALF] = (right[:, :HALF] + recv3[i, 0].astype(F32)).astype(BF16)
        send4[i, 0, :, HALF:] = right[:, HALF:].astype(BF16)
        ring_copy(3, i, 0).start()
        send4[i, 1, :, :HALF] = left[:, :HALF].astype(BF16)
        send4[i, 1, :, HALF:] = (left[:, HALF:] + recv3[i, 1].astype(F32)).astype(BF16)
        ring_copy(3, i, 1).start()

    def ring_last(i):
        for side in range(2):
            ring_copy(3, i, side).wait_recv()
        result = pick_row(i, 0) + recv4[i, 0].astype(F32) + recv4[i, 1].astype(F32)
        low = (3 * WIDTH if i < 2 else -2 * COLS if i < 4 else WIDTH - 4 * COLS) + i * COLS
        if low < 3 * WIDTH:
            dwin_ref[:, low : low + COLS] = result
        else:
            dwout_ref[:, low - 3 * WIDTH : low - 3 * WIDTH + COLS] = result

    def rest_forward():
        attend(0)
        attend(1)
        transpose_rows()

    last = z == sections - 1
    forward_relay(0)
    forward_send(1, (4, 2, 1, 0))
    copy_in.wait()
    own_projections()
    forward_join(0)
    forward_relay(1)
    forward_keys(0)
    forward_weights(0)
    forward_join(1)
    copy_out.wait()

    @pl.when(z < sections - 1)
    def _():
        forward_keys(1)
        forward_weights(1)
        rest_forward()

    stage_upstream(0)
    stage_parts(0)
    stage_project(0)

    @pl.when(last)
    def _():
        forward_keys(1)

    stage_query(0)
    stage_relay(0)

    @pl.when(last)
    def _():
        forward_weights(1)

    stage_own(0)
    backward_finish(0)

    @pl.when(z == 0)
    def _():
        wait_incoming(1, 0)
        wait_incoming(1, 1)
        weight_part(0)
        weight_part(1)

    stage_upstream(1)

    stage_parts(1)

    @pl.when(z == 0)
    def _():
        ring_one(0)
        ring_one(1)

    @pl.when(z > 0)
    def _():
        stage_project(1)

    stage_query(1)

    @pl.when(z > 0)
    def _():
        stage_relay(1)
        stage_own(1)
        backward_finish(1)

        @pl.when(last)
        def _():
            rest_forward()

        weight_part(0)
        weight_part(1)
        ring_one(0)
        ring_one(1)

    for i in range(2, PARTS):
        weight_part(i)
        if i > 2:
            ring_one(i - 1)
            ring_two(i - 3)
    ring_one(PARTS - 1)
    ring_two(PARTS - 3)

    @pl.when(z == 0)
    def _():
        stage_project(1)
        stage_own(1)

    ring_three(0)
    ring_two(PARTS - 2)
    ring_three(1)
    ring_two(PARTS - 1)

    @pl.when(z == 0)
    def _():
        stage_relay(1)

    for i in range(2, PARTS + 3):
        if i < PARTS:
            ring_three(i)
        if i < PARTS + 2:
            ring_four(i - 2)
        if 4 <= i:
            ring_last(i - 4)
        if i == PARTS - 1:

            @pl.when(z == 0)
            def _():
                backward_finish(1)

    ring_last(PARTS - 1)

    for i in range(PARTS):
        pair_copy(i).wait_send()
        for stage in range(4):
            for side in range(2):
                ring_copy(stage, i, side).wait_send()

    for m in range(MB):
        for k in range(LEVELS):

            @pl.when(sends_direct_up(k))
            def _():
                fwd_copy(m, k).wait_send()

            @pl.when(sends_direct_down(k))
            def _():
                for c in range(CHUNKS):
                    bwd_copy(m, c, k).wait_send()

            if 0 < k < CROSS:

                @pl.when(relays(k))
                def _():
                    fwd_cross(m, k).wait_send()

                @pl.when(sends_cross(k))
                def _():
                    for c in range(CHUNKS):
                        cross_copy(m, c, k).wait_send()

        @pl.when(joins)
        def _():
            fwd_pair(m).wait_send()

        @pl.when(gives)
        def _():
            for c in range(CHUNKS):
                join_copy(m, c).wait_send()

        @pl.when(z > 0)
        def _():
            for h in range(2):
                z_copy(m, h).wait_send()


def result_kernel(a, b, c, a_out, b_out, c_out, a_buf, b_buf, c_buf, sem_in, sem_out):
    sources, buffers, targets = (a, b, c), (a_buf, b_buf, c_buf), (a_out, b_out, c_out)
    fetch = [pltpu.make_async_copy(sources[i], buffers[i], sem_in.at[i]) for i in range(3)]
    store = [pltpu.make_async_copy(buffers[i], targets[i], sem_out.at[i]) for i in range(3)]
    for copy in fetch:
        copy.start()
    for i in range(3):
        fetch[i].wait()
        store[i].start()
    for copy in store:
        copy.wait()


def per_device(acts, grad_top, w_in, w_out, offsets):
    sections = lax.axis_size("section")
    shards = lax.axis_size("tm")
    vmem = pl.BlockSpec(memory_space=pltpu.VMEM)
    d_acts, d_in, d_out = pl.pallas_call(
        functools.partial(layer_kernel, sections, shards),
        out_shape=(
            jax.ShapeDtypeStruct((MB, ROWS, WIDTH), BF16),
            jax.ShapeDtypeStruct((SLICE, 3 * WIDTH), F32),
            jax.ShapeDtypeStruct((SLICE, WIDTH), F32),
        ),
        in_specs=[
            vmem,
            vmem,
            pl.BlockSpec(memory_space=pl.ANY),
            pl.BlockSpec(memory_space=pl.ANY),
            pl.BlockSpec(memory_space=pltpu.SMEM),
        ],
        out_specs=(vmem, vmem, vmem),
        scratch_shapes=[
            pltpu.VMEM((WIDTH, 3 * WIDTH), BF16),
            pltpu.VMEM((WIDTH, WIDTH), BF16),
            pltpu.VMEM((MB, BLOCKS, ROWS, WIDTH), BF16),
            pltpu.VMEM((MB, ROWS, WIDTH), F32),
            pltpu.VMEM((MB, ROWS, 128), F32),
            pltpu.VMEM((MB, GROUPS, GROUP, GROUP), BF16),
            pltpu.VMEM((MB, KEYS, 2 * WIDTH), BF16),
            pltpu.VMEM((MB, GROUPS, KEYS, GROUP), F32),
            pltpu.VMEM((MB, GROUPS, KEYS, GROUP), BF16),
            pltpu.VMEM((GROUP, GROUP), BF16),
            pltpu.VMEM((KEYS, GROUP), F32),
            pltpu.VMEM((MB, ROWS, WIDTH), BF16),
            pltpu.VMEM((MB * ROWS, WIDTH), BF16),
            pltpu.VMEM((MB, KEYS, 2 * WIDTH), BF16),
            pltpu.VMEM((MB * ROWS, WIDTH), BF16),
            pltpu.VMEM((MB, ROWS, WIDTH), F32),
            pltpu.VMEM((MB, ROWS, WIDTH), BF16),
            pltpu.VMEM((MB, CHUNKS, LEVELS, ROWS, CHUNK), BF16),
            pltpu.VMEM((MB, CHUNKS, LEVELS, ROWS, CHUNK), BF16),
            pltpu.SemaphoreType.DMA((2,)),
            pltpu.SemaphoreType.DMA((MB, LEVELS)),
            pltpu.SemaphoreType.DMA((MB, LEVELS)),
            pltpu.SemaphoreType.DMA((MB, CHUNKS, LEVELS)),
            pltpu.SemaphoreType.DMA((MB, CHUNKS, LEVELS)),
            pltpu.SemaphoreType.DMA((MB, 2)),
            pltpu.SemaphoreType.DMA((MB, 2)),
            pltpu.VMEM((2, SIDE, SIDE, SLICE, MB * KEYS), BF16),
            pltpu.VMEM((2, SIDE, SIDE, SLICE, MB * ROWS), BF16),
            pltpu.VMEM((2, SIDE, SIDE, SLICE, MB * ROWS), BF16),
            pltpu.VMEM((PARTS, SIDE, SIDE, SLICE, COLS), BF16),
            pltpu.VMEM((PARTS, SIDE, SIDE, SLICE, COLS), BF16),
            pltpu.VMEM((PARTS, SIDE, SIDE, SLICE, COLS), F32),
            pltpu.VMEM((PARTS, 2, SIDE, SLICE, HALF), BF16),
            pltpu.VMEM((PARTS, 2, SIDE, SLICE, HALF), BF16),
            pltpu.VMEM((PARTS, 2, SIDE, SLICE, COLS), BF16),
            pltpu.VMEM((PARTS, 2, SIDE, SLICE, COLS), BF16),
            pltpu.VMEM((PARTS, SIDE, SLICE, COLS), F32),
            pltpu.VMEM((PARTS, 2, SLICE, HALF), BF16),
            pltpu.VMEM((PARTS, 2, SLICE, HALF), BF16),
            pltpu.VMEM((PARTS, 2, SLICE, COLS), BF16),
            pltpu.VMEM((PARTS, 2, SLICE, COLS), BF16),
            pltpu.SemaphoreType.DMA((PARTS,)),
            pltpu.SemaphoreType.DMA((PARTS,)),
        ]
        + [pltpu.SemaphoreType.DMA((PARTS, 2))] * 8
        + [
            pltpu.VMEM((GROUPS, KEYS, GROUP), BF16),
            pltpu.VMEM((ROWS, WIDTH), F32),
            pltpu.VMEM((ROWS, WIDTH), BF16),
            pltpu.VMEM((MB, CHUNKS, CROSS, ROWS, CHUNK), BF16),
            pltpu.VMEM((CHUNKS, ROWS, CHUNK), F32),
            pltpu.SemaphoreType.DMA((MB, CHUNKS, CROSS)),
            pltpu.SemaphoreType.DMA((MB, CHUNKS, CROSS)),
            pltpu.SemaphoreType.DMA((MB, CROSS)),
            pltpu.VMEM((CHUNKS, ROWS, CHUNK), F32),
            pltpu.VMEM((MB, CHUNKS, ROWS, CHUNK), BF16),
            pltpu.SemaphoreType.DMA((MB, CHUNKS)),
            pltpu.SemaphoreType.DMA((MB, CHUNKS)),
            pltpu.SemaphoreType.DMA((MB,)),
        ],
        compiler_params=pltpu.CompilerParams(
            collective_id=0, has_side_effects=True, vmem_limit_bytes=63 * 1024 * 1024
        ),
        name="layer_kernel",
    )(acts[0], grad_top, w_in[0], w_out[0], offsets)
    results = (d_acts, d_in, d_out)
    anywhere = pl.BlockSpec(memory_space=pl.ANY)
    d_acts, d_in, d_out = pl.pallas_call(
        result_kernel,
        out_shape=tuple(jax.ShapeDtypeStruct(r.shape, r.dtype) for r in results),
        in_specs=[anywhere] * 3,
        out_specs=(anywhere,) * 3,
        scratch_shapes=[pltpu.VMEM(r.shape, r.dtype) for r in results]
        + [pltpu.SemaphoreType.DMA((3,)), pltpu.SemaphoreType.DMA((3,))],
        name="result_kernel",
    )(*results)
    return (d_acts[None], d_in[None], d_out[None])


def solution(mesh):
    placed = (
        P("section", None, "tm", None),
        P(None, "tm", None),
        P("section", None, None),
        P("section", None, None),
        P("tm", None),
    )
    return jax.shard_map(
        per_device,
        mesh=mesh,
        in_specs=placed,
        out_specs=(
            P("section", None, "tm", None),
            P("section", "tm", None),
            P("section", "tm", None),
        ),
        check_vma=False,
    )
```
